512 devices in a mesh: sec: 8 (over x, core), xy: 64 (over y, z).
Axes of the slice: x: 4, y: 4, z: 16, core: 2. Of those that a mesh axis runs over, the one named last changes fastest.
Arguments:
- source: bfloat16 [8, 32768, 1024], P('sec', 'xy'), may hold values from -6 to 6
- coarse: int32 [8, 2, 128], P('sec', None, 'xy'), may hold values from -1 to 1, as said below
- fraction: float32 [8, 2, 128], P('sec', None, 'xy'), may hold values from 0.25 to 0.75
- kernel_one: float32 [3, 3, 3], replicated, may hold values from -1.25 to 1.25
- kernel_two: float32 [3, 3, 3], replicated, may hold values from -1.25 to 1.25
Outputs:
- denoised: bfloat16 [8, 1024, 32768], P(None, 'xy', 'sec')
The draws below stay inside these ranges and needn't reach their ends.
Inputs may be any that keep to these rules, and one draw needn't show every extreme that they name: Destination block (r, c) reads source block (r + coarse[z, 0, b], c + coarse[z, 1, b]); c + coarse[z, 1, b] always lies in 0 to 1. Among the 2 blocks of one block row of a section, at most one has a row offset of -1 and at most one has +1.
All inputs are finite; a program needn't handle non-finite values.
Results may differ from the reference program's by a relative error of at most 0.003.
The reference program's roundings to bfloat16 on the way (of `picked`, `rows_warped`, `aligned` and `first_pass`) count: a program that leaves them out, or rounds other values in their place, can miss the bound.
Values may be sent and summed in bfloat16 or wider, within the bound.
No kernel may reach another device: no remote copies, remote signals or barrier semaphores. Data moves between devices by JAX's collectives and lax.ppermute only.
A program may use at most 128 MiB of HBM per device.

```python
import jax
import jax.numpy as jnp
from jax import lax

BS = 512
NBX = 2
SECTIONS = 8
W = 1024
H = 32768
BLOCKS = 128
N_XY = 64


def draw_coarse(key, part):
    row_key, col_key = jax.random.split(jax.random.fold_in(key, 7))
    row_draw = jax.random.randint(row_key, (SECTIONS, BLOCKS // NBX, NBX), -1, 2)
    columns_kept = [row_draw[:, :, 0]]
    for column in range(1, NBX):
        current = row_draw[:, :, column]
        collides = jnp.zeros(current.shape, jnp.bool_)
        for earlier in columns_kept:
            collides = collides | (earlier == current)
        columns_kept.append(jnp.where(collides & (current != 0), 0, current))
    row_shift = jnp.stack(columns_kept, axis=2).reshape(SECTIONS, BLOCKS)
    anchor = jax.random.randint(col_key, (SECTIONS, BLOCKS), 0, NBX)
    col_shift = anchor - jnp.arange(BLOCKS, dtype=jnp.int32) % NBX
    return jnp.stack([row_shift, col_shift], axis=1).astype(jnp.int32)


def block_levels(key, dims, cuts, least, largest):
    def one(position, parts):
        draws = jax.random.uniform(jax.random.fold_in(jax.random.fold_in(key, 6), position), (parts,), jnp.float32, least / len(cuts), largest / len(cuts))
        return jnp.repeat(jnp.exp(draws), dims[position] // parts).reshape((-1,) + (1,) * (len(dims) - position - 1))

    level = one(*cuts[0])
    for cut in cuts[1:]:
        level = level * one(*cut)
    return level


def noise(own_key, shape, scale, limit, shards=(), kind=jnp.bfloat16):
    factor_of = block_levels(own_key, shape, shards, -0.22, 0.18) if shards else 1.0
    array = jax.random.normal(own_key, shape, jnp.float32) * scale * factor_of
    return jnp.minimum(jnp.maximum(array, -limit), limit).astype(kind)


def setup_inputs(seed: int = 0) -> dict:
    arg_keys = jax.random.split(jax.random.key(seed), 6)
    source = noise(arg_keys[0], (SECTIONS, H, W), 1.0, 6.0, ((0, 8), (1, 64)))
    coarse = draw_coarse(jax.random.fold_in(arg_keys[5], 71), 0)
    fraction = jnp.clip(0.25 + 0.5 * jax.random.uniform(arg_keys[2], (SECTIONS, 2, BLOCKS), jnp.float32) ** block_levels(arg_keys[2], (SECTIONS, 2, BLOCKS), ((0, 8), (2, 64)), -0.2, 0.2), 0.25, 0.75)
    kernel_one = noise(arg_keys[3], (3, 3, 3), 27 ** -0.5, 1.25, (), jnp.float32)
    kernel_two = noise(arg_keys[4], (3, 3, 3), 27 ** -0.5, 1.25, (), jnp.float32)
    return {"source": source, "coarse": coarse, "fraction": fraction, "kernel_one": kernel_one, "kernel_two": kernel_two}


def interpolation(shift, edge):
    row_index = lax.broadcasted_iota(jnp.int32, (edge, edge), 0)
    col_index = lax.broadcasted_iota(jnp.int32, (edge, edge), 1)
    offset = col_index - row_index
    amount = shift[..., None, None]
    w_before = ((-0.5 * amount + 1.0) * amount - 0.5) * amount
    w_center = (1.5 * amount - 2.5) * amount * amount + 1.0
    w_after = ((-1.5 * amount + 2.0) * amount + 0.5) * amount
    w_beyond = (0.5 * amount - 0.5) * amount * amount
    matrix = jnp.where(offset == -1, w_before, 0.0) + jnp.where(offset == 0, w_center, 0.0)
    matrix = matrix + jnp.where(offset == 1, w_after, 0.0) + jnp.where(offset == 2, w_beyond, 0.0)
    return matrix.astype(jnp.bfloat16)


def stencil_volume(volume, kernel):
    result = lax.conv_general_dilated(volume[None, None], kernel[None, None], (1, 1, 1), "SAME",
                                      dimension_numbers=("NCDHW", "OIDHW", "NCDHW"),
                                      precision=lax.Precision.HIGHEST)
    return result[0, 0]


def align_section(inputs):
    section_image, offsets, fractions = inputs
    blocks = section_image.reshape(N_XY, BS, NBX, BS).transpose(0, 2, 1, 3)
    empty_row = jnp.zeros((1, NBX, BS, BS), section_image.dtype)
    padded = jnp.concatenate([empty_row, blocks, empty_row], axis=0)
    block_rows = jnp.arange(BLOCKS, dtype=jnp.int32) // NBX
    block_cols = jnp.arange(BLOCKS, dtype=jnp.int32) % NBX
    picked = padded[(block_rows + offsets[0] + 1).astype(jnp.int32), (block_cols + offsets[1]).astype(jnp.int32)]
    row_matrix = interpolation(fractions[0], BS)
    col_matrix = interpolation(fractions[1], BS)
    rows_warped = jnp.einsum("bij,bjk->bik", row_matrix.astype(jnp.float32), picked.astype(jnp.float32)).astype(jnp.bfloat16)
    warped = jnp.einsum("bcj,brj->bcr", col_matrix.astype(jnp.float32), rows_warped.astype(jnp.float32)).astype(jnp.bfloat16)
    return warped.reshape(N_XY, NBX, BS, BS).transpose(1, 2, 0, 3).reshape(W, H)


def reference(source, coarse, fraction, kernel_one, kernel_two):
    aligned = lax.map(align_section, (source, coarse, fraction))
    first_pass = jnp.maximum(stencil_volume(aligned.astype(jnp.float32), kernel_one), 0.0).astype(jnp.bfloat16)
    second = stencil_volume(first_pass.astype(jnp.float32), kernel_two)
    return (second + aligned.astype(jnp.float32)).astype(jnp.bfloat16)
```

```python
import jax
import jax.numpy as jnp
from jax import lax
from jax.experimental import pallas as pl
from jax.experimental.pallas import tpu as pltpu
from jax.sharding import PartitionSpec as P

LANES = 128
HALO = 2
VMEM = pl.BlockSpec(memory_space=pltpu.VMEM)
SMEM = pl.BlockSpec(memory_space=pltpu.SMEM)


def shift_pairs(count, steps):
    first, last = (max(0, -steps), min(count, count - steps))
    return [(source, source + steps) for source in range(first, last)]


def from_behind(value, axis, steps):
    return lax.ppermute(value, axis, shift_pairs(lax.axis_size(axis), steps))


def interpolation(amount, edge):
    row_index = lax.broadcasted_iota(jnp.int32, (edge, edge), 0)
    col_index = lax.broadcasted_iota(jnp.int32, (edge, edge), 1)
    offset = col_index - row_index
    w_before = ((-0.5 * amount + 1.0) * amount - 0.5) * amount
    w_center = (1.5 * amount - 2.5) * amount * amount + 1.0
    w_after = ((-1.5 * amount + 2.0) * amount + 0.5) * amount
    w_beyond = (0.5 * amount - 0.5) * amount * amount
    matrix = jnp.where(offset == -1, w_before, 0.0)
    matrix = jnp.where(offset == 0, w_center, matrix)
    matrix = jnp.where(offset == 1, w_after, matrix)
    return jnp.where(offset == 2, w_beyond, matrix)


def matrices_body(fraction_ref, out_ref):
    _, kinds, columns = fraction_ref.shape
    edge = out_ref.shape[-1]
    for kind in range(kinds):
        for block in range(columns):
            out_ref[kind, block] = interpolation(fraction_ref[0, kind, block], edge).astype(jnp.bfloat16)


def warp_body(coarse_ref, source_ref, above_ref, below_ref, matrix_ref, out_ref):
    _, edge, width = source_ref.shape
    columns = width // edge
    groups = out_ref.shape[0] // columns
    chunks, cols = out_ref.shape[1], out_ref.shape[2]
    for block in range(columns):
        down = coarse_ref[0, 0, block]
        anchor = block + coarse_ref[0, 1, block]
        picked = source_ref[0, :, 0:edge]
        for column in range(1, columns):
            picked = jnp.where(anchor == column, source_ref[0, :, column * edge : (column + 1) * edge], picked)
        picked = jnp.where(down < 0, above_ref[0], picked)
        picked = jnp.where(down > 0, below_ref[0], picked)
        rows_warped = jnp.dot(
            matrix_ref[0, block], picked, preferred_element_type=jnp.float32
        ).astype(jnp.bfloat16)
        warped = lax.dot_general(
            matrix_ref[1, block], rows_warped, (((1,), (1,)), ((), ())), preferred_element_type=jnp.float32
        ).astype(jnp.bfloat16)
        warped = warped.reshape(groups, cols, edge)
        for chunk in range(chunks):
            out_ref[block * groups : (block + 1) * groups, chunk] = warped[
                :, :, chunk * LANES : (chunk + 1) * LANES
            ]


def section_column(index, sections, cols, halo):
    main = sections * cols
    side = sections * halo
    in_main = index < main
    in_left = index < main + side
    left = index - main
    right = index - main - side
    section = jnp.where(in_main, index // cols, jnp.where(in_left, left // halo, right // halo))
    column = jnp.where(in_main, index % cols, jnp.where(in_left, left % halo - halo, right % halo + cols))
    return section, column


def stencil_matrix(kernel_ref, out_ref, sections, cols, halo_out, halo_in):
    _, _, rows_out, rows_in = out_ref.shape
    shape = (rows_out, rows_in)
    out_index = lax.broadcasted_iota(jnp.int32, shape, 0)
    in_index = lax.broadcasted_iota(jnp.int32, shape, 1)
    out_sec, out_col = section_column(out_index, sections, cols, halo_out) if halo_out else (out_index // cols, out_index % cols)
    in_sec, in_col = section_column(in_index, sections, cols, halo_in)
    delta_sec = in_sec - out_sec + 1
    delta_col = in_col - out_col + 1
    delta = jnp.where((delta_col >= 0) & (delta_col < 3), delta_sec * 3 + delta_col, -1)
    for tap_y in range(3):
        value = jnp.zeros(shape, jnp.float32)
        for tap_z in range(3):
            for tap_x in range(3):
                value = jnp.where(delta == tap_z * 3 + tap_x, kernel_ref[tap_z, tap_x, tap_y], value)
        high = value.astype(jnp.bfloat16)
        out_ref[tap_y, 0] = high
        out_ref[tap_y, 1] = (value - high.astype(jnp.float32)).astype(jnp.bfloat16)


def stencils_body(sections, cols, one_ref, two_ref, first_ref, second_ref):
    stencil_matrix(one_ref, first_ref, sections, cols, 1, HALO)
    stencil_matrix(two_ref, second_ref, sections, cols, 0, 1)


def edges_body(data_ref, first_ref, last_ref):
    sections, chunks, cols, lanes = data_ref.shape
    side = sections * HALO
    shape = (side, sections * cols)
    index = lax.broadcasted_iota(jnp.int32, shape, 0)
    source = lax.broadcasted_iota(jnp.int32, shape, 1)
    head = index // HALO * cols + index % HALO
    take_first = jnp.where(source == head, 1.0, 0.0).astype(jnp.bfloat16)
    take_last = jnp.where(source == head + cols - HALO, 1.0, 0.0).astype(jnp.bfloat16)
    for chunk in range(chunks):
        block = data_ref[:, chunk].reshape(sections * cols, lanes)
        where = slice(chunk * lanes, (chunk + 1) * lanes)
        first_ref[:, where] = jnp.dot(take_first, block, preferred_element_type=jnp.float32).astype(jnp.bfloat16)
        last_ref[:, where] = jnp.dot(take_last, block, preferred_element_type=jnp.float32).astype(jnp.bfloat16)


def shifted_sum(matrix_ref, volume):
    def tap(index):
        high = jnp.dot(matrix_ref[index, 0], volume, preferred_element_type=jnp.float32)
        return high + jnp.dot(matrix_ref[index, 1], volume, preferred_element_type=jnp.float32)

    size = volume.shape[1]
    return pltpu.roll(tap(0), 1, 1) + tap(1) + pltpu.roll(tap(2), size - 1, 1)


def denoise_body(place_ref, first_ref, second_ref, data_ref, left_ref, right_ref, out_ref, volume_ref, pass_ref):
    sections, chunks, cols, lanes = data_ref.shape
    main = sections * cols
    side = sections * HALO
    for chunk in range(chunks):
        volume_ref[0:main, chunk * lanes : (chunk + 1) * lanes] = data_ref[:, chunk].reshape(main, lanes)
    volume_ref[main : main + side, :] = left_ref[...]
    volume_ref[main + side : main + 2 * side, :] = right_ref[...]
    length = chunks * lanes
    passed = jnp.maximum(shifted_sum(first_ref, volume_ref[...]), 0.0)
    row = lax.broadcasted_iota(jnp.int32, passed.shape, 0)
    lane = lax.broadcasted_iota(jnp.int32, passed.shape, 1)
    gone = (row >= main) & (row < main + sections) & (place_ref[0] > 0)
    gone = gone | ((row >= main + sections) & (place_ref[1] > 0))
    gone = gone | ((lane < lanes) & (place_ref[2] > 0))
    gone = gone | ((lane >= length - lanes) & (place_ref[3] > 0))
    pass_ref[...] = jnp.where(gone, 0.0, passed).astype(jnp.bfloat16)
    second = shifted_sum(second_ref, pass_ref[...])
    total = second + volume_ref[0:main, :].astype(jnp.float32)
    out_ref[...] = total[:, lanes : length - lanes].astype(jnp.bfloat16).reshape(sections, cols, length - 2 * lanes)


def body(source, coarse, fraction, kernel_one, kernel_two):
    _, edge, width = source.shape
    columns = width // edge
    n_xy, n_sec = lax.axis_size("xy"), lax.axis_size("sec")
    cols = width // n_xy
    chunks = edge // LANES
    bf16 = jnp.bfloat16

    down, anchor = coarse[0, 0], coarse[0, 1] + jnp.arange(columns, dtype=jnp.int32)
    want_above = jnp.sum(jnp.where(down < 0, anchor, 0)).reshape(1, 1)
    want_below = jnp.sum(jnp.where(down > 0, anchor, 0)).reshape(1, 1)
    for_below = from_behind(want_above, "xy", -1)
    for_above = from_behind(want_below, "xy", 1)

    def choose(column):
        block = source[:, :, 0:edge]
        for index in range(1, columns):
            block = jnp.where(column == index, source[:, :, index * edge : (index + 1) * edge], block)
        return block

    above = from_behind(choose(for_below[0, 0]), "xy", 1)
    below = from_behind(choose(for_above[0, 0]), "xy", -1)

    matrix = pl.pallas_call(
        matrices_body,
        out_shape=jax.ShapeDtypeStruct((2, columns, edge, edge), bf16),
        in_specs=[SMEM],
        out_specs=VMEM,
        name="matrices",
    )(fraction)
    main, side = n_sec * cols, n_sec * HALO
    rows_in, rows_mid = main + 2 * side, main + 2 * n_sec
    first, second = pl.pallas_call(
        lambda *refs: stencils_body(n_sec, cols, *refs),
        out_shape=(
            jax.ShapeDtypeStruct((3, 2, rows_mid, rows_in), bf16),
            jax.ShapeDtypeStruct((3, 2, main, rows_mid), bf16),
        ),
        in_specs=[SMEM, SMEM],
        out_specs=(VMEM, VMEM),
        name="stencils",
    )(kernel_one, kernel_two)

    strip = pl.pallas_call(
        warp_body,
        out_shape=jax.ShapeDtypeStruct((n_xy, chunks, cols, LANES), bf16),
        in_specs=[SMEM, VMEM, VMEM, VMEM, VMEM],
        out_specs=VMEM,
        name="warp",
    )(coarse, source, above, below, matrix)

    mine = lax.all_to_all(strip, "xy", split_axis=0, concat_axis=0, tiled=True)
    per_sec = n_xy * chunks // n_sec
    mine = jnp.pad(mine.reshape(n_xy * chunks, cols, LANES), ((1, 1), (0, 0), (0, 0)))
    spread = jnp.stack([mine[index * per_sec : (index + 1) * per_sec + 2] for index in range(n_sec)])
    data = lax.all_to_all(spread, "sec", split_axis=0, concat_axis=0, tiled=True)

    length = (per_sec + 2) * LANES
    firsts, lasts = pl.pallas_call(
        edges_body,
        out_shape=(jax.ShapeDtypeStruct((side, length), bf16),) * 2,
        in_specs=[VMEM],
        out_specs=(VMEM, VMEM),
        name="edges",
    )(data)
    left = from_behind(lasts, "xy", 1)
    right = from_behind(firsts, "xy", -1)

    at_xy, at_sec = lax.axis_index("xy"), lax.axis_index("sec")
    place = jnp.stack([at_xy == 0, at_xy == n_xy - 1, at_sec == 0, at_sec == n_sec - 1]).astype(jnp.int32)
    return pl.pallas_call(
        denoise_body,
        out_shape=jax.ShapeDtypeStruct((n_sec, cols, per_sec * LANES), bf16),
        in_specs=[SMEM, VMEM, VMEM, VMEM, VMEM, VMEM],
        out_specs=VMEM,
        scratch_shapes=[pltpu.VMEM((rows_in, length), bf16), pltpu.VMEM((rows_mid, length), bf16)],
        name="denoise",
    )(place, first, second, data, left, right)


def solution(mesh):
    placed = (P("sec", "xy", None), P("sec", None, "xy"), P("sec", None, "xy"), P(), P())
    return jax.shard_map(
        body, mesh=mesh, in_specs=placed, out_specs=P(None, "xy", "sec"), check_vma=False
    )
```

```python
import numpy as np
import jax
import jax.numpy as jnp
from jax import lax
from jax.experimental import pallas as pl
from jax.experimental.pallas import tpu as pltpu
from jax.sharding import PartitionSpec as P

LANES = 128
HALO = 2
BF16 = jnp.bfloat16
F32 = jnp.float32
VMEM = pl.BlockSpec(memory_space=pltpu.VMEM)
SMEM = pl.BlockSpec(memory_space=pltpu.SMEM)


def call(body, outs, ins, name, mib, scratch=()):
    return pl.pallas_call(
        body,
        out_shape=outs,
        in_specs=ins,
        out_specs=jax.tree.map(lambda _: VMEM, outs),
        scratch_shapes=scratch,
        compiler_params=pltpu.CompilerParams(vmem_limit_bytes=mib << 20),
        name=name,
    )


def shaped(*shape):
    return jax.ShapeDtypeStruct(shape, BF16)


def dot(left, right):
    return jnp.dot(left, right, preferred_element_type=F32)


def shift_pairs(count, steps):
    first, last = (max(0, -steps), min(count, count - steps))
    return [(source, source + steps) for source in range(first, last)]


def from_behind(value, axis, steps):
    return lax.ppermute(value, axis, shift_pairs(lax.axis_size(axis), steps))


def interpolation(amount, edge):
    row_index = lax.broadcasted_iota(jnp.int32, (edge, edge), 0)
    col_index = lax.broadcasted_iota(jnp.int32, (edge, edge), 1)
    offset = col_index - row_index
    w_before = ((-0.5 * amount + 1.0) * amount - 0.5) * amount
    w_center = (1.5 * amount - 2.5) * amount * amount + 1.0
    w_after = ((-1.5 * amount + 2.0) * amount + 0.5) * amount
    w_beyond = (0.5 * amount - 0.5) * amount * amount
    matrix = jnp.where(offset == -1, w_before, 0.0)
    matrix = jnp.where(offset == 0, w_center, matrix)
    matrix = jnp.where(offset == 1, w_after, matrix)
    return jnp.where(offset == 2, w_beyond, matrix)


def matrices_body(fraction_ref, out_ref):
    _, kinds, columns = fraction_ref.shape
    edge = out_ref.shape[-1]
    for kind in range(kinds):
        for block in range(columns):
            out_ref[kind, block] = interpolation(fraction_ref[0, kind, block], edge).astype(BF16)


def warp_body(coarse_ref, source_ref, above_ref, below_ref, matrix_ref, out_ref):
    _, edge, width = source_ref.shape
    columns = width // edge
    groups = out_ref.shape[0] // columns
    chunks, cols = out_ref.shape[1], out_ref.shape[2]
    for block in range(columns):
        down = coarse_ref[0, 0, block]
        anchor = block + coarse_ref[0, 1, block]
        picked = source_ref[0, :, 0:edge]
        for column in range(1, columns):
            picked = jnp.where(anchor == column, source_ref[0, :, column * edge : (column + 1) * edge], picked)
        picked = jnp.where(down < 0, above_ref[0], picked)
        picked = jnp.where(down > 0, below_ref[0], picked)
        rows_warped = dot(matrix_ref[0, block], picked).astype(BF16)
        warped = lax.dot_general(
            matrix_ref[1, block], rows_warped, (((1,), (1,)), ((), ())), preferred_element_type=F32
        ).astype(BF16)
        warped = warped.reshape(groups, cols, edge)
        for chunk in range(chunks):
            out_ref[block * groups : (block + 1) * groups, chunk] = warped[
                :, :, chunk * LANES : (chunk + 1) * LANES
            ]


def tap_index(out_pixels, in_pixels):
    out_sec, out_col = np.array(out_pixels).T[:, :, None]
    in_sec, in_col = np.array(in_pixels).T[:, None, :]
    tap_z, tap_x = in_sec - out_sec + 1, in_col - out_col + 1
    linked = (tap_z >= 0) & (tap_z < 3) & (tap_x >= 0) & (tap_x < 3)
    return np.where(linked, tap_z * 3 + tap_x, -1).astype(np.int32)


def stencil_matrix(index, kernel_ref, out_ref):
    rows, width = index.shape
    for tap_y in range(3):
        value = jnp.zeros((rows, width), F32)
        for tap in range(9):
            value = jnp.where(index == tap, kernel_ref[tap // 3, tap % 3, tap_y], value)
        high = value.astype(BF16)
        low = (value - high.astype(F32)).astype(BF16)
        out_ref[tap_y * rows : (tap_y + 1) * rows, :] = jnp.concatenate([high, low], axis=1)


def stencils_body(one_ref, two_ref, *refs):
    indices, outs = refs[:4], refs[4:]
    for place, (index_ref, out_ref) in enumerate(zip(indices, outs)):
        stencil_matrix(index_ref[...], one_ref if place % 2 == 0 else two_ref, out_ref)


def edges_body(pad, data_ref, first_ref, last_ref):
    parts, chunks, cols, lanes = data_ref.shape
    shape = (pad, chunks * cols)
    index = lax.broadcasted_iota(jnp.int32, shape, 0)
    source = lax.broadcasted_iota(jnp.int32, shape, 1)
    head = index // HALO * cols + index % HALO
    used = index < chunks * HALO
    take_first = jnp.where(used & (source == head), 1.0, 0.0).astype(BF16)
    take_last = jnp.where(used & (source == head + cols - HALO), 1.0, 0.0).astype(BF16)
    take = jnp.concatenate([take_first, take_last], axis=0)
    for part in range(parts):
        rim = dot(take, data_ref[part].reshape(chunks * cols, lanes)).astype(BF16)
        first_ref[part] = rim[:pad]
        last_ref[part] = rim[pad:]


def shifted_sum(matrix_ref, volume, rows):
    size = volume.shape[1]
    before = dot(matrix_ref[0:rows], volume)
    here = dot(matrix_ref[rows : 2 * rows], volume)
    after = dot(matrix_ref[2 * rows : 3 * rows], volume)
    return pltpu.roll(before, 1, 1) + here + pltpu.roll(after, size - 1, 1)


def outside(place_ref, shape, lanes):
    lane = lax.broadcasted_iota(jnp.int32, shape, 1)
    gone = (lane < lanes) & (place_ref[2] > 0)
    return gone | ((lane >= shape[1] - lanes) & (place_ref[3] > 0))


def interior_body(place_ref, first_ref, second_ref, rim_ref, data_ref, out_ref, passed_ref, aligned_ref, volume_ref, pass_ref):
    sections, chunks, cols, lanes = data_ref.shape
    main = sections * cols
    length = chunks * lanes
    for chunk in range(chunks):
        block = data_ref[:, chunk].reshape(main, lanes)
        volume_ref[0:main, chunk * lanes : (chunk + 1) * lanes] = block
        volume_ref[main : 2 * main, chunk * lanes : (chunk + 1) * lanes] = block
    volume = volume_ref[...]
    aligned_ref[...] = dot(rim_ref[...], volume[0:main]).astype(BF16)
    rows = first_ref.shape[0] // 3
    passed = jnp.maximum(shifted_sum(first_ref, volume, rows), 0.0)
    passed = jnp.where(outside(place_ref, passed.shape, lanes), 0.0, passed).astype(BF16)
    passed_ref[...] = passed[0 : passed_ref.shape[0]]
    pass_ref[0:rows] = passed
    pass_ref[rows : 2 * rows] = passed
    second = shifted_sum(second_ref, pass_ref[...], main)
    total = (second + volume_ref[0:main, :].astype(F32))[:, lanes : length - lanes]
    column = lax.broadcasted_iota(jnp.int32, total.shape, 0) % cols
    inside = (column >= HALO) & (column < cols - HALO)
    out_ref[...] = jnp.where(inside, total, 0.0).astype(BF16).reshape(out_ref.shape)


def rim_body(place_ref, first_ref, second_ref, put_ref, halo_ref, passed_ref, aligned_ref, inner_ref, out_ref, volume_ref, pass_ref):
    sections, sides, pad, lanes = halo_ref.shape
    rim, length = aligned_ref.shape
    chunks = length // lanes
    side = sections * HALO
    shape = (chunks * side, sections * pad)
    index = lax.broadcasted_iota(jnp.int32, shape, 0)
    source = lax.broadcasted_iota(jnp.int32, shape, 1)
    wanted = (index % side) // HALO * pad + index // side * HALO + index % HALO
    gather = jnp.where(source == wanted, 1.0, 0.0).astype(BF16)
    high = rim + sides * side
    volume_ref[0:rim] = aligned_ref[...]
    volume_ref[high : high + rim] = aligned_ref[...]
    for which in range(sides):
        halo = dot(gather, halo_ref[:, which].reshape(sections * pad, lanes)).astype(BF16)
        for chunk in range(chunks):
            where = slice(chunk * lanes, (chunk + 1) * lanes)
            block = halo[chunk * side : (chunk + 1) * side]
            start = rim + which * side
            volume_ref[start : start + side, where] = block
            volume_ref[high + start : high + start + side, where] = block
    rows = first_ref.shape[0] // 3
    passed = jnp.maximum(shifted_sum(first_ref, volume_ref[...], rows), 0.0)
    row = lax.broadcasted_iota(jnp.int32, passed.shape, 0)
    gone = outside(place_ref, passed.shape, lanes)
    gone = gone | ((row < sections) & (place_ref[0] > 0))
    gone = gone | ((row >= rows - sections) & (place_ref[1] > 0))
    passed = jnp.where(gone, 0.0, passed).astype(BF16)
    inner = passed_ref.shape[0]
    for start in (0, inner + rows):
        pass_ref[start : start + inner] = passed_ref[...]
        pass_ref[start + inner : start + inner + rows] = passed
    second = shifted_sum(second_ref, pass_ref[...], rim)
    total = (second + aligned_ref[...].astype(F32))[:, lanes : length - lanes].astype(BF16)
    placed = dot(put_ref[...], total)
    inner_out = inner_ref[...].reshape(placed.shape).astype(F32)
    out_ref[...] = (placed + inner_out).astype(BF16).reshape(out_ref.shape)


def one_hot(out_pixels, in_pixels):
    match = [[pixel == other for other in in_pixels] for pixel in out_pixels]
    return jnp.asarray(np.array(match, np.float32), BF16)


def body(source, coarse, fraction, kernel_one, kernel_two):
    _, edge, width = source.shape
    columns = width // edge
    n_xy, n_sec = lax.axis_size("xy"), lax.axis_size("sec")
    cols = width // n_xy
    chunks = edge // LANES

    down, anchor = coarse[0, 0], coarse[0, 1] + jnp.arange(columns, dtype=jnp.int32)
    want_above = jnp.sum(jnp.where(down < 0, anchor, 0)).reshape(1, 1)
    want_below = jnp.sum(jnp.where(down > 0, anchor, 0)).reshape(1, 1)
    for_below = from_behind(want_above, "xy", -1)
    for_above = from_behind(want_below, "xy", 1)

    def choose(column):
        block = source[:, :, 0:edge]
        for index in range(1, columns):
            block = jnp.where(column == index, source[:, :, index * edge : (index + 1) * edge], block)
        return block

    above = from_behind(choose(for_below[0, 0]), "xy", 1)
    below = from_behind(choose(for_above[0, 0]), "xy", -1)

    matrix = call(matrices_body, shaped(2, columns, edge, edge), [SMEM], "matrices", 16)(fraction)

    def pixels(*columns_taken):
        return [(section, column) for section in range(n_sec) for column in columns_taken]

    def by_column(*columns_taken):
        return [(section, column) for column in columns_taken for section in range(n_sec)]

    last = cols - 1
    natural = pixels(*range(cols))
    near = pixels(1, 2, last - 2, last - 1)
    rim = pixels(0, 1, last - 1, last)
    inner_pass = near + pixels(*range(3, last - 2))
    rim_in = rim + pixels(-2, -1) + pixels(last + 1, last + 2)
    rim_pass = by_column(-1, 0, last, last + 1)
    inner_out = [(s, c) if HALO <= c < cols - HALO else (-9, -9) for s, c in natural]
    indices = [
        tap_index(inner_pass, natural),
        tap_index(inner_out, inner_pass),
        tap_index(rim_pass, rim_in),
        tap_index(rim, near + rim_pass),
    ]
    stencils = call(
        stencils_body,
        tuple(shaped(3 * index.shape[0], 2 * index.shape[1]) for index in indices),
        [SMEM, SMEM] + [VMEM] * 4,
        "stencils",
        8,
    )(kernel_one, kernel_two, *map(jnp.asarray, indices))

    at_xy, at_sec = lax.axis_index("xy"), lax.axis_index("sec")
    place = jnp.stack([at_xy == 0, at_xy == n_xy - 1, at_sec == 0, at_sec == n_sec - 1]).astype(jnp.int32)
    above, below, matrix, stencils, place = lax.optimization_barrier((above, below, matrix, stencils, place))

    strip = call(warp_body, shaped(n_xy, chunks, cols, LANES), [SMEM] + [VMEM] * 4, "warp", 16)(
        coarse, source, above, below, matrix
    )
    mine = lax.all_to_all(strip, "xy", split_axis=0, concat_axis=0, tiled=True)
    per_sec = n_xy * chunks // n_sec
    mine = jnp.pad(mine.reshape(n_xy * chunks, cols, LANES), ((1, 1), (0, 0), (0, 0)))
    spread = jnp.stack([mine[index * per_sec : (index + 1) * per_sec + 2] for index in range(n_sec)])
    data = lax.all_to_all(spread, "sec", split_axis=0, concat_axis=0, tiled=True)

    pad = -(-(per_sec + 2) * HALO // 16) * 16
    firsts, lasts = call(
        lambda *refs: edges_body(pad, *refs), (shaped(n_sec, pad, LANES),) * 2, [VMEM], "edges", 8
    )(spread)
    sides = jnp.stack([from_behind(lasts, "xy", 1), from_behind(firsts, "xy", -1)], axis=1)
    halo = lax.all_to_all(sides, "sec", split_axis=0, concat_axis=0, tiled=True)

    length = (per_sec + 2) * LANES
    out = shaped(n_sec, cols, per_sec * LANES)
    inner, passed, aligned = call(
        interior_body,
        (out, shaped(len(near), length), shaped(len(rim), length)),
        [SMEM] + [VMEM] * 4,
        "interior",
        32,
        [pltpu.VMEM((2 * len(natural), length), BF16), pltpu.VMEM((2 * len(inner_pass), length), BF16)],
    )(place, stencils[0], stencils[1], one_hot(rim, natural), data)
    return call(
        rim_body,
        out,
        [SMEM] + [VMEM] * 7,
        "rim",
        32,
        [pltpu.VMEM((2 * len(rim_in), length), BF16), pltpu.VMEM((2 * (len(near) + len(rim_pass)), length), BF16)],
    )(place, stencils[2], stencils[3], one_hot(natural, rim), halo, passed, aligned, inner)


def solution(mesh):
    placed = (P("sec", "xy", None), P("sec", None, "xy"), P("sec", None, "xy"), P(), P())
    return jax.shard_map(
        body, mesh=mesh, in_specs=placed, out_specs=P(None, "xy", "sec"), check_vma=False
    )
```

```python
import numpy as np
import jax
import jax.numpy as jnp
from jax import lax
from jax.experimental import pallas as pl
from jax.experimental.pallas import tpu as pltpu
from jax.sharding import PartitionSpec as P

LANES = 128
HALO = 2
BF16 = jnp.bfloat16
F32 = jnp.float32
VMEM = pl.BlockSpec(memory_space=pltpu.VMEM)
SMEM = pl.BlockSpec(memory_space=pltpu.SMEM)


def call(body, outs, ins, name, mib, scratch=()):
    return pl.pallas_call(
        body,
        out_shape=outs,
        in_specs=ins,
        out_specs=jax.tree.map(lambda _: VMEM, outs),
        scratch_shapes=scratch,
        compiler_params=pltpu.CompilerParams(vmem_limit_bytes=mib << 20),
        name=name,
    )


def shaped(*shape):
    return jax.ShapeDtypeStruct(shape, BF16)


def dot(left, right):
    return jnp.dot(left, right, preferred_element_type=F32)


def shift_pairs(count, steps):
    first, last = (max(0, -steps), min(count, count - steps))
    return [(source, source + steps) for source in range(first, last)]


def from_behind(value, axis, steps):
    return lax.ppermute(value, axis, shift_pairs(lax.axis_size(axis), steps))


def interpolation(amount, edge):
    row_index = lax.broadcasted_iota(jnp.int32, (edge, edge), 0)
    col_index = lax.broadcasted_iota(jnp.int32, (edge, edge), 1)
    offset = col_index - row_index
    w_before = ((-0.5 * amount + 1.0) * amount - 0.5) * amount
    w_center = (1.5 * amount - 2.5) * amount * amount + 1.0
    w_after = ((-1.5 * amount + 2.0) * amount + 0.5) * amount
    w_beyond = (0.5 * amount - 0.5) * amount * amount
    matrix = jnp.where(offset == -1, w_before, 0.0)
    matrix = jnp.where(offset == 0, w_center, matrix)
    matrix = jnp.where(offset == 1, w_after, matrix)
    return jnp.where(offset == 2, w_beyond, matrix)


def matrices_body(fraction_ref, out_ref):
    _, kinds, columns = fraction_ref.shape
    edge = out_ref.shape[-1]
    for kind in range(kinds):
        for block in range(columns):
            out_ref[kind, block] = interpolation(fraction_ref[0, kind, block], edge).astype(BF16)


def choose_body(below_ref, above_ref, source_ref, for_below_ref, for_above_ref):
    edge = for_below_ref.shape[-1]
    columns = source_ref.shape[-1] // edge
    for coarse_ref, sign, out_ref in ((below_ref, -1, for_below_ref), (above_ref, 1, for_above_ref)):
        wanted = 0
        for block in range(columns):
            wanted += jnp.where(coarse_ref[0, 0, block] == sign, block + coarse_ref[0, 1, block], 0)
        for column in range(columns):

            @pl.when(wanted == column)
            def _():
                out_ref[0] = source_ref[0, :, column * edge : (column + 1) * edge]


def warp_body(coarse_ref, source_ref, above_ref, below_ref, matrix_ref, out_ref):
    _, edge, width = source_ref.shape
    columns = width // edge
    groups = out_ref.shape[0] // columns
    chunks, cols = out_ref.shape[1], out_ref.shape[2]
    for block in range(columns):
        down = coarse_ref[0, 0, block]
        anchor = block + coarse_ref[0, 1, block]
        picked = source_ref[0, :, 0:edge]
        for column in range(1, columns):
            picked = jnp.where(anchor == column, source_ref[0, :, column * edge : (column + 1) * edge], picked)
        picked = jnp.where(down < 0, above_ref[0], picked)
        picked = jnp.where(down > 0, below_ref[0], picked)
        rows_warped = dot(matrix_ref[0, block], picked).astype(BF16)
        warped = lax.dot_general(
            matrix_ref[1, block], rows_warped, (((1,), (1,)), ((), ())), preferred_element_type=F32
        ).astype(BF16)
        warped = warped.reshape(groups, cols, edge)
        for chunk in range(chunks):
            out_ref[block * groups : (block + 1) * groups, chunk] = warped[
                :, :, chunk * LANES : (chunk + 1) * LANES
            ]


def tap_index(out_pixels, in_pixels):
    out_sec, out_col = np.array(out_pixels).T[:, :, None]
    in_sec, in_col = np.array(in_pixels).T[:, None, :]
    tap_z, tap_x = in_sec - out_sec + 1, in_col - out_col + 1
    linked = (tap_z >= 0) & (tap_z < 3) & (tap_x >= 0) & (tap_x < 3)
    return np.where(linked, tap_z * 3 + tap_x, -1).astype(np.int32)


def stencil_matrix(index, kernel_ref, out_ref):
    rows, width = index.shape
    for tap_y in range(3):
        value = jnp.zeros((rows, width), F32)
        for tap in range(9):
            value = jnp.where(index == tap, kernel_ref[tap // 3, tap % 3, tap_y], value)
        high = value.astype(BF16)
        low = (value - high.astype(F32)).astype(BF16)
        out_ref[tap_y * rows : (tap_y + 1) * rows, :] = jnp.concatenate([high, low], axis=1)


def stencils_body(one_ref, two_ref, *refs):
    indices, outs = refs[:4], refs[4:]
    for place, (index_ref, out_ref) in enumerate(zip(indices, outs)):
        stencil_matrix(index_ref[...], one_ref if place % 2 == 0 else two_ref, out_ref)


def edges_body(data_ref, take_ref, first_ref, last_ref):
    sections, chunks, cols, lanes = data_ref.shape
    side = first_ref.shape[0]
    for chunk in range(chunks):
        rim = dot(take_ref[...], data_ref[:, chunk].reshape(sections * cols, lanes)).astype(BF16)
        where = slice(chunk * lanes, (chunk + 1) * lanes)
        first_ref[:, where] = rim[:side]
        last_ref[:, where] = rim[side:]


def shifted_sum(matrix_ref, volume, rows):
    size = volume.shape[1]
    before = dot(matrix_ref[0:rows], volume)
    here = dot(matrix_ref[rows : 2 * rows], volume)
    after = dot(matrix_ref[2 * rows : 3 * rows], volume)
    return pltpu.roll(before, 1, 1) + here + pltpu.roll(after, size - 1, 1)


def outside(place_ref, shape, lanes):
    lane = lax.broadcasted_iota(jnp.int32, shape, 1)
    gone = (lane < lanes) & (place_ref[2] > 0)
    return gone | ((lane >= shape[1] - lanes) & (place_ref[3] > 0))


def interior_body(place_ref, first_ref, second_ref, rim_ref, data_ref, out_ref, passed_ref, aligned_ref, volume_ref, pass_ref):
    sections, chunks, cols, lanes = data_ref.shape
    main = sections * cols
    length = chunks * lanes
    for chunk in range(chunks):
        block = data_ref[:, chunk].reshape(main, lanes)
        volume_ref[0:main, chunk * lanes : (chunk + 1) * lanes] = block
        volume_ref[main : 2 * main, chunk * lanes : (chunk + 1) * lanes] = block
    volume = volume_ref[...]
    aligned_ref[...] = dot(rim_ref[...], volume[0:main]).astype(BF16)
    rows = first_ref.shape[0] // 3
    passed = jnp.maximum(shifted_sum(first_ref, volume, rows), 0.0)
    passed = jnp.where(outside(place_ref, passed.shape, lanes), 0.0, passed).astype(BF16)
    passed_ref[...] = passed[0 : passed_ref.shape[0]]
    pass_ref[0:rows] = passed
    pass_ref[rows : 2 * rows] = passed
    second = shifted_sum(second_ref, pass_ref[...], main)
    total = (second + volume_ref[0:main, :].astype(F32))[:, lanes : length - lanes]
    column = lax.broadcasted_iota(jnp.int32, total.shape, 0) % cols
    inside = (column >= HALO) & (column < cols - HALO)
    out_ref[...] = jnp.where(inside, total, 0.0).astype(BF16).reshape(out_ref.shape)


def rim_body(place_ref, first_ref, second_ref, put_ref, left_ref, right_ref, passed_ref, aligned_ref, inner_ref, out_ref, volume_ref, pass_ref):
    lanes = LANES
    sections = inner_ref.shape[0]
    rim, length = aligned_ref.shape
    side = left_ref.shape[0]
    for start in (0, rim + 2 * side):
        volume_ref[start : start + rim] = aligned_ref[...]
        volume_ref[start + rim : start + rim + side] = left_ref[...]
        volume_ref[start + rim + side : start + rim + 2 * side] = right_ref[...]
    rows = first_ref.shape[0] // 3
    passed = jnp.maximum(shifted_sum(first_ref, volume_ref[...], rows), 0.0)
    row = lax.broadcasted_iota(jnp.int32, passed.shape, 0)
    gone = outside(place_ref, passed.shape, lanes)
    gone = gone | ((row < sections) & (place_ref[0] > 0))
    gone = gone | ((row >= rows - sections) & (place_ref[1] > 0))
    passed = jnp.where(gone, 0.0, passed).astype(BF16)
    inner = passed_ref.shape[0]
    for start in (0, inner + rows):
        pass_ref[start : start + inner] = passed_ref[...]
        pass_ref[start + inner : start + inner + rows] = passed
    second = shifted_sum(second_ref, pass_ref[...], rim)
    total = (second + aligned_ref[...].astype(F32))[:, lanes : length - lanes].astype(BF16)
    placed = dot(put_ref[...], total)
    inner_out = inner_ref[...].reshape(placed.shape).astype(F32)
    out_ref[...] = (placed + inner_out).astype(BF16).reshape(out_ref.shape)


def one_hot(out_pixels, in_pixels):
    match = [[pixel == other for other in in_pixels] for pixel in out_pixels]
    return jnp.asarray(np.array(match, np.float32), BF16)


def body(source, coarse, fraction, kernel_one, kernel_two):
    _, edge, width = source.shape
    columns = width // edge
    n_xy, n_sec = lax.axis_size("xy"), lax.axis_size("sec")
    cols = width // n_xy
    chunks = edge // LANES

    of_below, of_above = from_behind(coarse, "xy", -1), from_behind(coarse, "xy", 1)
    for_below, for_above = call(
        choose_body, (shaped(1, edge, edge),) * 2, [SMEM, SMEM, VMEM], "choose", 8
    )(of_below, of_above, source)
    above, below = from_behind(for_below, "xy", 1), from_behind(for_above, "xy", -1)

    matrix = call(matrices_body, shaped(2, columns, edge, edge), [SMEM], "matrices", 16)(fraction)

    def pixels(*columns_taken):
        return [(section, column) for section in range(n_sec) for column in columns_taken]

    def by_column(*columns_taken):
        return [(section, column) for column in columns_taken for section in range(n_sec)]

    last = cols - 1
    natural = pixels(*range(cols))
    near = pixels(1, 2, last - 2, last - 1)
    rim = pixels(0, 1, last - 1, last)
    inner_pass = near + pixels(*range(3, last - 2))
    rim_in = rim + pixels(-2, -1) + pixels(last + 1, last + 2)
    rim_pass = by_column(-1, 0, last, last + 1)
    inner_out = [(s, c) if HALO <= c < cols - HALO else (-9, -9) for s, c in natural]
    indices = [
        tap_index(inner_pass, natural),
        tap_index(inner_out, inner_pass),
        tap_index(rim_pass, rim_in),
        tap_index(rim, near + rim_pass),
    ]
    stencils = call(
        stencils_body,
        tuple(shaped(3 * index.shape[0], 2 * index.shape[1]) for index in indices),
        [SMEM, SMEM] + [VMEM] * 4,
        "stencils",
        8,
    )(kernel_one, kernel_two, *map(jnp.asarray, indices))

    at_xy, at_sec = lax.axis_index("xy"), lax.axis_index("sec")
    place = jnp.stack([at_xy == 0, at_xy == n_xy - 1, at_sec == 0, at_sec == n_sec - 1]).astype(jnp.int32)
    above, below, matrix, stencils, place = lax.optimization_barrier((above, below, matrix, stencils, place))

    strip = call(warp_body, shaped(n_xy, chunks, cols, LANES), [SMEM] + [VMEM] * 4, "warp", 16)(
        coarse, source, above, below, matrix
    )
    mine = lax.all_to_all(strip, "xy", split_axis=0, concat_axis=0, tiled=True)
    per_sec = n_xy * chunks // n_sec
    mine = jnp.pad(mine.reshape(n_xy * chunks, cols, LANES), ((1, 1), (0, 0), (0, 0)))
    spread = jnp.stack([mine[index * per_sec : (index + 1) * per_sec + 2] for index in range(n_sec)])
    data = lax.all_to_all(spread, "sec", split_axis=0, concat_axis=0, tiled=True)

    length = (per_sec + 2) * LANES
    out = shaped(n_sec, cols, per_sec * LANES)
    firsts, lasts = call(
        edges_body, (shaped(n_sec * HALO, length),) * 2, [VMEM, VMEM], "edges", 8
    )(data, one_hot(pixels(0, 1) + pixels(last - 1, last), natural))
    left, right = from_behind(lasts, "xy", 1), from_behind(firsts, "xy", -1)
    inner, passed, aligned = call(
        interior_body,
        (out, shaped(len(near), length), shaped(len(rim), length)),
        [SMEM] + [VMEM] * 4,
        "interior",
        32,
        [pltpu.VMEM((2 * len(natural), length), BF16), pltpu.VMEM((2 * len(inner_pass), length), BF16)],
    )(place, stencils[0], stencils[1], one_hot(rim, natural), data)
    return call(
        rim_body,
        out,
        [SMEM] + [VMEM] * 8,
        "rim",
        32,
        [pltpu.VMEM((2 * len(rim_in), length), BF16), pltpu.VMEM((2 * (len(near) + len(rim_pass)), length), BF16)],
    )(place, stencils[2], stencils[3], one_hot(natural, rim), left, right, passed, aligned, inner)


def solution(mesh):
    placed = (P("sec", "xy", None), P("sec", None, "xy"), P("sec", None, "xy"), P(), P())
    return jax.shard_map(
        body, mesh=mesh, in_specs=placed, out_specs=P(None, "xy", "sec"), check_vma=False
    )
```

```python
import numpy as np
import jax
import jax.numpy as jnp
from jax import lax
from jax.experimental import pallas as pl
from jax.experimental.pallas import tpu as pltpu
from jax.sharding import PartitionSpec as P

LANES = 128
HALO = 2
PARTS = 2
BF16 = jnp.bfloat16
F32 = jnp.float32
VMEM = pl.BlockSpec(memory_space=pltpu.VMEM)
SMEM = pl.BlockSpec(memory_space=pltpu.SMEM)


def call(body, outs, ins, name, mib, scratch=()):
    return pl.pallas_call(
        body,
        out_shape=outs,
        in_specs=ins,
        out_specs=jax.tree.map(lambda _: VMEM, outs),
        scratch_shapes=scratch,
        compiler_params=pltpu.CompilerParams(vmem_limit_bytes=mib << 20),
        name=name,
    )


def shaped(*shape):
    return jax.ShapeDtypeStruct(shape, BF16)


def dot(left, right):
    return jnp.dot(left, right, preferred_element_type=F32)


def shift_pairs(count, steps):
    first, last = (max(0, -steps), min(count, count - steps))
    return [(source, source + steps) for source in range(first, last)]


def far_pairs(step, count):
    half = count // 2
    return [(i, (i // 2 + step // 2) % half * 2 + (i + step) % 2) for i in range(count)]


def from_behind(value, axis, steps):
    return lax.ppermute(value, axis, shift_pairs(lax.axis_size(axis), steps))


def interpolation(amount, edge, cols, parts):
    order = lax.broadcasted_iota(jnp.int32, (edge, edge), 0)
    size = cols // parts
    inside = order % (edge // parts)
    row_index = inside // size * cols + order // (edge // parts) * size + inside % size
    col_index = lax.broadcasted_iota(jnp.int32, (edge, edge), 1)
    offset = col_index - row_index
    w_before = ((-0.5 * amount + 1.0) * amount - 0.5) * amount
    w_center = (1.5 * amount - 2.5) * amount * amount + 1.0
    w_after = ((-1.5 * amount + 2.0) * amount + 0.5) * amount
    w_beyond = (0.5 * amount - 0.5) * amount * amount
    matrix = jnp.where(offset == -1, w_before, 0.0)
    matrix = jnp.where(offset == 0, w_center, matrix)
    matrix = jnp.where(offset == 1, w_after, matrix)
    return jnp.where(offset == 2, w_beyond, matrix)


def matrices_body(cols, parts, fraction_ref, out_ref):
    _, kinds, columns = fraction_ref.shape
    edge = out_ref.shape[-1]
    for kind in range(kinds):
        for block in range(columns):
            out_ref[kind, block] = interpolation(
                fraction_ref[0, kind, block], edge, cols, parts if kind else 1
            ).astype(BF16)


def choose_body(below_ref, above_ref, source_ref, for_below_ref, for_above_ref):
    edge = for_below_ref.shape[-1]
    columns = source_ref.shape[-1] // edge
    for coarse_ref, sign, out_ref in ((below_ref, -1, for_below_ref), (above_ref, 1, for_above_ref)):
        wanted = 0
        for block in range(columns):
            wanted += jnp.where(coarse_ref[0, 0, block] == sign, block + coarse_ref[0, 1, block], 0)
        for column in range(columns):

            @pl.when(wanted == column)
            def _():
                out_ref[0] = source_ref[0, :, column * edge : (column + 1) * edge]


def warp_body(coarse_ref, source_ref, above_ref, below_ref, matrix_ref, *out_refs):
    _, edge, width = source_ref.shape
    columns = width // edge
    parts = len(out_refs)
    groups = out_refs[0].shape[0] // columns
    chunks, cols = out_refs[0].shape[1], out_refs[0].shape[2]
    for block in range(columns):
        down = coarse_ref[0, 0, block]
        anchor = block + coarse_ref[0, 1, block]
        picked = source_ref[0, :, 0:edge]
        for column in range(1, columns):
            picked = jnp.where(anchor == column, source_ref[0, :, column * edge : (column + 1) * edge], picked)
        picked = jnp.where(down < 0, above_ref[0], picked)
        picked = jnp.where(down > 0, below_ref[0], picked)
        rows_warped = dot(matrix_ref[0, block], picked).astype(BF16)
        warped = lax.dot_general(
            matrix_ref[1, block], rows_warped, (((1,), (1,)), ((), ())), preferred_element_type=F32
        ).astype(BF16)
        size = edge // parts
        for part, out_ref in enumerate(out_refs):
            half = warped[part * size : (part + 1) * size].reshape(groups, cols, edge)
            for chunk in range(chunks):
                out_ref[block * groups : (block + 1) * groups, chunk] = half[:, :, chunk * LANES : (chunk + 1) * LANES]


def tap_index(out_pixels, in_pixels):
    out_sec, out_col = np.array(out_pixels).T[:, :, None]
    in_sec, in_col = np.array(in_pixels).T[:, None, :]
    tap_z, tap_x = in_sec - out_sec + 1, in_col - out_col + 1
    linked = (tap_z >= 0) & (tap_z < 3) & (tap_x >= 0) & (tap_x < 3)
    return np.where(linked, tap_z * 3 + tap_x, -1).astype(np.int32)


def stencil_matrix(index, kernel_ref, out_ref):
    rows, width = index.shape
    for tap_y in range(3):
        value = jnp.zeros((rows, width), F32)
        for tap in range(9):
            value = jnp.where(index == tap, kernel_ref[tap // 3, tap % 3, tap_y], value)
        high = value.astype(BF16)
        low = (value - high.astype(F32)).astype(BF16)
        out_ref[tap_y * rows : (tap_y + 1) * rows, :] = jnp.concatenate([high, low], axis=1)


def stencils_body(one_ref, two_ref, *refs):
    indices, outs = refs[:4], refs[4:]
    for place, (index_ref, out_ref) in enumerate(zip(indices, outs)):
        stencil_matrix(index_ref[...], one_ref if place % 2 == 0 else two_ref, out_ref)


def owner(device, step, count, sign):
    around = lax.rem(lax.div(device, 2) + (sign * (step // 2)) % (count // 2), count // 2)
    return around * 2 + lax.rem(lax.rem(device, 2) + step % 2, 2)


def spread_body(steps, place_ref, data_ref, *out_refs):
    total = data_ref.shape[0]
    for out_ref, step in zip(out_refs, steps):
        count = out_ref.shape[0] - 2
        first = owner(place_ref[4], step, len(steps), 1) * count
        before = data_ref[jnp.maximum(first - 1, 0)]
        after = data_ref[jnp.minimum(first + count, total - 1)]
        out_ref[0] = jnp.where(first > 0, before, jnp.zeros_like(before))
        out_ref[1 : count + 1] = data_ref[pl.ds(first, count)]
        out_ref[count + 1] = jnp.where(first + count < total, after, jnp.zeros_like(after))


def assemble_body(steps, place_ref, *refs):
    ins, out_ref = refs[:-1], refs[-1]
    for in_ref, step in zip(ins, steps):
        out_ref[owner(place_ref[4], step, len(steps), -1)] = in_ref[...]


def edges_body(data_ref, take_ref, out_ref):
    sections, chunks, cols, lanes = data_ref.shape
    for chunk in range(chunks):
        block = data_ref[:, chunk].reshape(sections * cols, lanes)
        out_ref[:, chunk * lanes : (chunk + 1) * lanes] = dot(take_ref[...], block).astype(BF16)


def shifted_sum(matrix_ref, volume, rows):
    size = volume.shape[1]
    before = dot(matrix_ref[0:rows], volume)
    here = dot(matrix_ref[rows : 2 * rows], volume)
    after = dot(matrix_ref[2 * rows : 3 * rows], volume)
    return pltpu.roll(before, 1, 1) + here + pltpu.roll(after, size - 1, 1)


def outside(place_ref, shape, lanes):
    lane = lax.broadcasted_iota(jnp.int32, shape, 1)
    gone = (lane < lanes) & (place_ref[2] > 0)
    return gone | ((lane >= shape[1] - lanes) & (place_ref[3] > 0))


def interior_body(place_ref, first_ref, second_ref, rim_ref, low_ref, high_ref, out_ref, passed_ref, aligned_ref, volume_ref, pass_ref):
    sections, chunks, cols, lanes = low_ref.shape
    half = sections * cols
    main = 2 * half
    length = chunks * lanes
    for chunk in range(chunks):
        for start, data_ref in ((0, low_ref), (half, high_ref)):
            block = data_ref[:, chunk].reshape(half, lanes)
            volume_ref[start : start + half, chunk * lanes : (chunk + 1) * lanes] = block
            volume_ref[main + start : main + start + half, chunk * lanes : (chunk + 1) * lanes] = block
    volume = volume_ref[...]
    aligned_ref[...] = dot(rim_ref[...], volume[0:main]).astype(BF16)
    rows = first_ref.shape[0] // 3
    passed = jnp.maximum(shifted_sum(first_ref, volume, rows), 0.0)
    passed = jnp.where(outside(place_ref, passed.shape, lanes), 0.0, passed).astype(BF16)
    passed_ref[...] = passed[0 : passed_ref.shape[0]]
    pass_ref[0:rows] = passed
    pass_ref[rows : 2 * rows] = passed
    second = shifted_sum(second_ref, pass_ref[...], main)
    total = (second + volume_ref[0:main, :].astype(F32))[:, lanes : length - lanes]
    row = lax.broadcasted_iota(jnp.int32, total.shape, 0)
    column = jnp.where(row < half, row % cols, cols - 1 - row % cols)
    total = jnp.where(column >= HALO, total, 0.0).astype(BF16)
    for part in range(2):
        out_ref[:, part * cols : (part + 1) * cols, :] = total[part * half : (part + 1) * half].reshape(
            sections, cols, length - 2 * lanes
        )


def rim_body(place_ref, first_ref, second_ref, put_ref, left_ref, right_ref, passed_ref, aligned_ref, inner_ref, out_ref, volume_ref, pass_ref):
    lanes = LANES
    sections = inner_ref.shape[0]
    rim, length = aligned_ref.shape
    side = left_ref.shape[0]
    for start in (0, rim + 2 * side):
        volume_ref[start : start + rim] = aligned_ref[...]
        volume_ref[start + rim : start + rim + side] = left_ref[...]
        volume_ref[start + rim + side : start + rim + 2 * side] = right_ref[...]
    rows = first_ref.shape[0] // 3
    passed = jnp.maximum(shifted_sum(first_ref, volume_ref[...], rows), 0.0)
    row = lax.broadcasted_iota(jnp.int32, passed.shape, 0)
    gone = outside(place_ref, passed.shape, lanes)
    gone = gone | ((row < sections) & (place_ref[0] > 0))
    gone = gone | ((row >= rows - sections) & (place_ref[1] > 0))
    passed = jnp.where(gone, 0.0, passed).astype(BF16)
    inner = passed_ref.shape[0]
    for start in (0, inner + rows):
        pass_ref[start : start + inner] = passed_ref[...]
        pass_ref[start + inner : start + inner + rows] = passed
    second = shifted_sum(second_ref, pass_ref[...], rim)
    total = (second + aligned_ref[...].astype(F32))[:, lanes : length - lanes].astype(BF16)
    placed = dot(put_ref[...], total)
    inner_out = inner_ref[...].reshape(placed.shape).astype(F32)
    out_ref[...] = (placed + inner_out).astype(BF16).reshape(out_ref.shape)


def one_hot(out_pixels, in_pixels):
    match = [[pixel == other for other in in_pixels] for pixel in out_pixels]
    return jnp.asarray(np.array(match, np.float32), BF16)


def body(source, coarse, fraction, kernel_one, kernel_two):
    _, edge, width = source.shape
    columns = width // edge
    n_xy, n_sec = lax.axis_size("xy"), lax.axis_size("sec")
    cols = width // n_xy
    chunks = edge // LANES

    of_below, of_above = from_behind(coarse, "xy", -1), from_behind(coarse, "xy", 1)
    for_below, for_above = call(
        choose_body, (shaped(1, edge, edge),) * 2, [SMEM, SMEM, VMEM], "choose", 8
    )(of_below, of_above, source)
    above, below = from_behind(for_below, "xy", 1), from_behind(for_above, "xy", -1)

    matrix = call(
        lambda *refs: matrices_body(cols, PARTS, *refs), shaped(2, columns, edge, edge), [SMEM], "matrices", 16
    )(fraction)

    def pixels(*columns_taken):
        return [(section, column) for section in range(n_sec) for column in columns_taken]

    def by_column(*columns_taken):
        return [(section, column) for column in columns_taken for section in range(n_sec)]

    last = cols - 1
    half = cols // PARTS
    low, high = pixels(*range(half)), pixels(*range(half, cols))
    natural, stored = pixels(*range(cols)), low + high
    near = pixels(1, 2, last - 2, last - 1)
    rim = pixels(0, 1, last - 1, last)
    inner_pass = near + pixels(*range(3, last - 2))
    rim_in = rim + pixels(-2, -1) + pixels(last + 1, last + 2)
    rim_pass = by_column(-1, 0, last, last + 1)
    inner_out = [(s, c) if HALO <= c < cols - HALO else (-9, -9) for s, c in stored]
    indices = [
        tap_index(inner_pass, stored),
        tap_index(inner_out, inner_pass),
        tap_index(rim_pass, rim_in),
        tap_index(rim, near + rim_pass),
    ]
    stencils = call(
        stencils_body,
        tuple(shaped(3 * index.shape[0], 2 * index.shape[1]) for index in indices),
        [SMEM, SMEM] + [VMEM] * 4,
        "stencils",
        8,
    )(kernel_one, kernel_two, *map(jnp.asarray, indices))

    at_xy, at_sec = lax.axis_index("xy"), lax.axis_index("sec")
    rims = [at_xy == 0, at_xy == n_xy - 1, at_sec == 0, at_sec == n_sec - 1]
    place = jnp.stack([*(rim.astype(jnp.int32) for rim in rims), at_sec.astype(jnp.int32)])
    above, below, matrix, stencils, place = lax.optimization_barrier((above, below, matrix, stencils, place))

    strips = call(warp_body, (shaped(n_xy, chunks, half, LANES),) * PARTS, [SMEM] + [VMEM] * 4, "warp", 16)(
        coarse, source, above, below, matrix
    )
    per_sec = n_xy * chunks // n_sec
    length = (per_sec + 2) * LANES

    def over_xy(strip):
        part = lax.all_to_all(strip, "xy", split_axis=0, concat_axis=0, tiled=True)
        return part.reshape(n_xy * chunks, half, LANES)

    def rim_of(data, taken, held, name):
        return call(edges_body, shaped(n_sec * HALO, length), [VMEM, VMEM], name, 8)(data, one_hot(taken, held))

    first_part = over_xy(strips[0])
    second_part = over_xy(strips[1])
    far = [step for step in range(n_sec) if step != 0]
    far = [0] + sorted(far, key=lambda step: -min(step // 2, n_sec // 2 - step // 2))

    pieces = call(
        lambda *refs: spread_body(far, *refs), (shaped(per_sec + 2, half, LANES),) * n_sec, [SMEM, VMEM], "spread", 8
    )(place, first_part)
    pieces = [pieces[0]] + [
        lax.ppermute(piece, "sec", far_pairs(step, n_sec))
        for step, piece in zip(far[1:], pieces[1:])
    ]
    data_low = call(
        lambda *refs: assemble_body(far, *refs), shaped(n_sec, per_sec + 2, half, LANES), [SMEM] + [VMEM] * n_sec, "assemble", 8
    )(place, *pieces)
    right = from_behind(rim_of(data_low, pixels(0, 1), low, "firsts"), "xy", -1)
    second_part, data_low, right = lax.optimization_barrier((second_part, data_low, right))

    second_part = jnp.pad(second_part, ((1, 1), (0, 0), (0, 0)))
    spread = jnp.stack([second_part[index * per_sec : (index + 1) * per_sec + 2] for index in range(n_sec)])
    data_high = lax.all_to_all(spread, "sec", split_axis=0, concat_axis=0, tiled=True)
    left = from_behind(rim_of(data_high, pixels(last - 1, last), high, "lasts"), "xy", 1)

    out = shaped(n_sec, cols, per_sec * LANES)
    inner, passed, aligned = call(
        interior_body,
        (out, shaped(len(near), length), shaped(len(rim), length)),
        [SMEM] + [VMEM] * 5,
        "interior",
        32,
        [pltpu.VMEM((2 * len(natural), length), BF16), pltpu.VMEM((2 * len(inner_pass), length), BF16)],
    )(place, stencils[0], stencils[1], one_hot(rim, stored), data_low, data_high)
    return call(
        rim_body,
        out,
        [SMEM] + [VMEM] * 8,
        "rim",
        32,
        [pltpu.VMEM((2 * len(rim_in), length), BF16), pltpu.VMEM((2 * (len(near) + len(rim_pass)), length), BF16)],
    )(place, stencils[2], stencils[3], one_hot(natural, rim), left, right, passed, aligned, inner)


def solution(mesh):
    placed = (P("sec", "xy", None), P("sec", None, "xy"), P("sec", None, "xy"), P(), P())
    return jax.shard_map(
        body, mesh=mesh, in_specs=placed, out_specs=P(None, "xy", "sec"), check_vma=False
    )
```

```python
import numpy as np
import jax
import jax.numpy as jnp
from jax import lax
from jax.experimental import pallas as pl
from jax.experimental.pallas import tpu as pltpu
from jax.sharding import PartitionSpec as P

LANES = 128
HALO = 2
BF16 = jnp.bfloat16
F32 = jnp.float32
VMEM = pl.BlockSpec(memory_space=pltpu.VMEM)
SMEM = pl.BlockSpec(memory_space=pltpu.SMEM)
ANY = pl.BlockSpec(memory_space=pl.ANY)


def call(body, outs, ins, name, mib, scratch=(), space=VMEM):
    return pl.pallas_call(
        body,
        out_shape=outs,
        in_specs=ins,
        out_specs=jax.tree.map(lambda _: space, outs),
        scratch_shapes=scratch,
        compiler_params=pltpu.CompilerParams(vmem_limit_bytes=mib << 20),
        name=name,
    )


def shaped(*shape):
    return jax.ShapeDtypeStruct(shape, BF16)


def dot(left, right):
    return jnp.dot(left, right, preferred_element_type=F32)


def shift_pairs(count, steps):
    first, last = (max(0, -steps), min(count, count - steps))
    return [(source, source + steps) for source in range(first, last)]


def from_behind(value, axis, steps):
    return lax.ppermute(value, axis, shift_pairs(lax.axis_size(axis), steps))


def interpolation(amount, edge):
    row_index = lax.broadcasted_iota(jnp.int32, (edge, edge), 0)
    col_index = lax.broadcasted_iota(jnp.int32, (edge, edge), 1)
    offset = col_index - row_index
    w_before = ((-0.5 * amount + 1.0) * amount - 0.5) * amount
    w_center = (1.5 * amount - 2.5) * amount * amount + 1.0
    w_after = ((-1.5 * amount + 2.0) * amount + 0.5) * amount
    w_beyond = (0.5 * amount - 0.5) * amount * amount
    matrix = jnp.where(offset == -1, w_before, 0.0)
    matrix = jnp.where(offset == 0, w_center, matrix)
    matrix = jnp.where(offset == 1, w_after, matrix)
    return jnp.where(offset == 2, w_beyond, matrix)


def matrices_body(fraction_ref, out_ref):
    _, kinds, columns = fraction_ref.shape
    edge = out_ref.shape[-1]
    for kind in range(kinds):
        for block in range(columns):
            out_ref[kind, block] = interpolation(fraction_ref[0, kind, block], edge).astype(BF16)


def stage_body(source_ref, out_ref, sem):
    copy = pltpu.make_async_copy(source_ref, out_ref, sem)
    copy.start()
    copy.wait()


def choose_body(below_ref, above_ref, source_ref, for_below_ref, for_above_ref):
    edge = for_below_ref.shape[-1]
    columns = source_ref.shape[-1] // edge
    for coarse_ref, sign, out_ref in ((below_ref, -1, for_below_ref), (above_ref, 1, for_above_ref)):
        wanted = 0
        for block in range(columns):
            wanted += jnp.where(coarse_ref[0, 0, block] == sign, block + coarse_ref[0, 1, block], 0)
        for column in range(columns):

            @pl.when(wanted == column)
            def _():
                out_ref[0] = source_ref[0, :, column * edge : (column + 1) * edge]


def warp_body(coarse_ref, source_ref, above_ref, below_ref, matrix_ref, out_ref):
    _, edge, width = source_ref.shape
    columns = width // edge
    groups = out_ref.shape[0] // columns
    chunks, cols = out_ref.shape[1], out_ref.shape[2]
    for block in range(columns):
        down = coarse_ref[0, 0, block]
        anchor = block + coarse_ref[0, 1, block]
        picked = source_ref[0, :, 0:edge]
        for column in range(1, columns):
            picked = jnp.where(anchor == column, source_ref[0, :, column * edge : (column + 1) * edge], picked)
        picked = jnp.where(down < 0, above_ref[0], picked)
        picked = jnp.where(down > 0, below_ref[0], picked)
        rows_warped = dot(matrix_ref[0, block], picked).astype(BF16)
        warped = lax.dot_general(
            matrix_ref[1, block], rows_warped, (((1,), (1,)), ((), ())), preferred_element_type=F32
        ).astype(BF16)
        warped = warped.reshape(groups, cols, edge)
        for chunk in range(chunks):
            out_ref[block * groups : (block + 1) * groups, chunk] = warped[
                :, :, chunk * LANES : (chunk + 1) * LANES
            ]


def tap_index(out_pixels, in_pixels):
    out_sec, out_col = np.array(out_pixels).T[:, :, None]
    in_sec, in_col = np.array(in_pixels).T[:, None, :]
    tap_z, tap_x = in_sec - out_sec + 1, in_col - out_col + 1
    linked = (tap_z >= 0) & (tap_z < 3) & (tap_x >= 0) & (tap_x < 3)
    return np.where(linked, tap_z * 3 + tap_x, -1).astype(np.int32)


def stencil_matrix(index, kernel_ref, out_ref):
    rows, width = index.shape
    for tap_y in range(3):
        value = jnp.zeros((rows, width), F32)
        for tap in range(9):
            value = jnp.where(index == tap, kernel_ref[tap // 3, tap % 3, tap_y], value)
        high = value.astype(BF16)
        low = (value - high.astype(F32)).astype(BF16)
        out_ref[tap_y * rows : (tap_y + 1) * rows, :] = jnp.concatenate([high, low], axis=1)


def stencils_body(one_ref, two_ref, *refs):
    indices, outs = refs[:4], refs[4:]
    for place, (index_ref, out_ref) in enumerate(zip(indices, outs)):
        stencil_matrix(index_ref[...], one_ref if place % 2 == 0 else two_ref, out_ref)


def edges_body(data_ref, take_ref, first_ref, last_ref):
    sections, chunks, cols, lanes = data_ref.shape
    side = first_ref.shape[0]
    for chunk in range(chunks):
        rim = dot(take_ref[...], data_ref[:, chunk].reshape(sections * cols, lanes)).astype(BF16)
        where = slice(chunk * lanes, (chunk + 1) * lanes)
        first_ref[:, where] = rim[:side]
        last_ref[:, where] = rim[side:]


def shifted_sum(matrix_ref, volume, rows):
    size = volume.shape[1]
    before = dot(matrix_ref[0:rows], volume)
    here = dot(matrix_ref[rows : 2 * rows], volume)
    after = dot(matrix_ref[2 * rows : 3 * rows], volume)
    return pltpu.roll(before, 1, 1) + here + pltpu.roll(after, size - 1, 1)


def outside(place_ref, shape, lanes):
    lane = lax.broadcasted_iota(jnp.int32, shape, 1)
    gone = (lane < lanes) & (place_ref[2] > 0)
    return gone | ((lane >= shape[1] - lanes) & (place_ref[3] > 0))


def interior_body(place_ref, first_ref, second_ref, rim_ref, data_ref, out_ref, passed_ref, aligned_ref, volume_ref, pass_ref):
    sections, chunks, cols, lanes = data_ref.shape
    main = sections * cols
    length = chunks * lanes
    for chunk in range(chunks):
        block = data_ref[:, chunk].reshape(main, lanes)
        volume_ref[0:main, chunk * lanes : (chunk + 1) * lanes] = block
        volume_ref[main : 2 * main, chunk * lanes : (chunk + 1) * lanes] = block
    volume = volume_ref[...]
    aligned_ref[...] = dot(rim_ref[...], volume[0:main]).astype(BF16)
    rows = first_ref.shape[0] // 3
    passed = jnp.maximum(shifted_sum(first_ref, volume, rows), 0.0)
    passed = jnp.where(outside(place_ref, passed.shape, lanes), 0.0, passed).astype(BF16)
    passed_ref[...] = passed[0 : passed_ref.shape[0]]
    pass_ref[0:rows] = passed
    pass_ref[rows : 2 * rows] = passed
    second = shifted_sum(second_ref, pass_ref[...], main)
    total = (second + volume_ref[0:main, :].astype(F32))[:, lanes : length - lanes]
    column = lax.broadcasted_iota(jnp.int32, total.shape, 0) % cols
    inside = (column >= HALO) & (column < cols - HALO)
    out_ref[...] = jnp.where(inside, total, 0.0).astype(BF16).reshape(out_ref.shape)


def rim_body(place_ref, first_ref, second_ref, put_ref, left_ref, right_ref, passed_ref, aligned_ref, inner_ref, out_ref, volume_ref, pass_ref, done_ref, sems):
    lanes = LANES
    sections = inner_ref.shape[0]
    rim, length = aligned_ref.shape
    side = left_ref.shape[0]
    for start in (0, rim + 2 * side):
        volume_ref[start : start + rim] = aligned_ref[...]
        volume_ref[start + rim : start + rim + side] = left_ref[...]
        volume_ref[start + rim + side : start + rim + 2 * side] = right_ref[...]
    rows = first_ref.shape[0] // 3
    passed = jnp.maximum(shifted_sum(first_ref, volume_ref[...], rows), 0.0)
    row = lax.broadcasted_iota(jnp.int32, passed.shape, 0)
    gone = outside(place_ref, passed.shape, lanes)
    gone = gone | ((row < sections) & (place_ref[0] > 0))
    gone = gone | ((row >= rows - sections) & (place_ref[1] > 0))
    passed = jnp.where(gone, 0.0, passed).astype(BF16)
    inner = passed_ref.shape[0]
    for start in (0, inner + rows):
        pass_ref[start : start + inner] = passed_ref[...]
        pass_ref[start + inner : start + inner + rows] = passed
    second = shifted_sum(second_ref, pass_ref[...], rim)
    total = (second + aligned_ref[...].astype(F32))[:, lanes : length - lanes].astype(BF16)
    pieces = sems.shape[0]
    width = total.shape[1] // pieces
    copies = []
    for piece in range(pieces):
        where = slice(piece * width, (piece + 1) * width)
        placed = dot(put_ref[...], total[:, where]).astype(BF16).reshape(sections, -1, width)
        done_ref[:, :, where] = placed + inner_ref[:, :, where]
        copies.append(pltpu.make_async_copy(done_ref.at[:, :, where], out_ref.at[:, :, where], sems.at[piece]))
        copies[-1].start()
    for copy in copies:
        copy.wait()


def one_hot(out_pixels, in_pixels):
    match = [[pixel == other for other in in_pixels] for pixel in out_pixels]
    return jnp.asarray(np.array(match, np.float32), BF16)


def body(source, coarse, fraction, kernel_one, kernel_two):
    _, edge, width = source.shape
    columns = width // edge
    n_xy, n_sec = lax.axis_size("xy"), lax.axis_size("sec")
    cols = width // n_xy
    chunks = edge // LANES

    of_below, of_above = from_behind(coarse, "xy", -1), from_behind(coarse, "xy", 1)
    staged = call(stage_body, shaped(*source.shape), [ANY], "stage", 8, [pltpu.SemaphoreType.DMA])(source)
    of_below, of_above, staged = lax.optimization_barrier((of_below, of_above, staged))
    for_below, for_above = call(
        choose_body, (shaped(1, edge, edge),) * 2, [SMEM, SMEM, VMEM], "choose", 8
    )(of_below, of_above, staged)
    above, below = from_behind(for_below, "xy", 1), from_behind(for_above, "xy", -1)

    matrix = call(matrices_body, shaped(2, columns, edge, edge), [SMEM], "matrices", 16)(fraction)

    def pixels(*columns_taken):
        return [(section, column) for section in range(n_sec) for column in columns_taken]

    def by_column(*columns_taken):
        return [(section, column) for column in columns_taken for section in range(n_sec)]

    last = cols - 1
    natural = pixels(*range(cols))
    near = pixels(1, 2, last - 2, last - 1)
    rim = pixels(0, 1, last - 1, last)
    inner_pass = near + pixels(*range(3, last - 2))
    rim_in = rim + pixels(-2, -1) + pixels(last + 1, last + 2)
    rim_pass = by_column(-1, 0, last, last + 1)
    inner_out = [(s, c) if HALO <= c < cols - HALO else (-9, -9) for s, c in natural]
    indices = [
        tap_index(inner_pass, natural),
        tap_index(inner_out, inner_pass),
        tap_index(rim_pass, rim_in),
        tap_index(rim, near + rim_pass),
    ]
    stencils = call(
        stencils_body,
        tuple(shaped(3 * index.shape[0], 2 * index.shape[1]) for index in indices),
        [SMEM, SMEM] + [VMEM] * 4,
        "stencils",
        8,
    )(kernel_one, kernel_two, *map(jnp.asarray, indices))

    at_xy, at_sec = lax.axis_index("xy"), lax.axis_index("sec")
    place = jnp.stack([at_xy == 0, at_xy == n_xy - 1, at_sec == 0, at_sec == n_sec - 1]).astype(jnp.int32)
    above, below, matrix, stencils, place = lax.optimization_barrier((above, below, matrix, stencils, place))

    strip = call(warp_body, shaped(n_xy, chunks, cols, LANES), [SMEM] + [VMEM] * 4, "warp", 16)(
        coarse, staged, above, below, matrix
    )
    mine = lax.all_to_all(strip, "xy", split_axis=0, concat_axis=0, tiled=True)
    per_sec = n_xy * chunks // n_sec
    mine = jnp.pad(mine.reshape(n_xy * chunks, cols, LANES), ((1, 1), (0, 0), (0, 0)))
    spread = jnp.stack([mine[index * per_sec : (index + 1) * per_sec + 2] for index in range(n_sec)])
    data = lax.all_to_all(spread, "sec", split_axis=0, concat_axis=0, tiled=True)

    length = (per_sec + 2) * LANES
    out = shaped(n_sec, cols, per_sec * LANES)
    firsts, lasts = call(
        edges_body, (shaped(n_sec * HALO, length),) * 2, [VMEM, VMEM], "edges", 8
    )(data, one_hot(pixels(0, 1) + pixels(last - 1, last), natural))
    left, right = from_behind(lasts, "xy", 1), from_behind(firsts, "xy", -1)
    inner, passed, aligned = call(
        interior_body,
        (out, shaped(len(near), length), shaped(len(rim), length)),
        [SMEM] + [VMEM] * 4,
        "interior",
        32,
        [pltpu.VMEM((2 * len(natural), length), BF16), pltpu.VMEM((2 * len(inner_pass), length), BF16)],
    )(place, stencils[0], stencils[1], one_hot(rim, natural), data)
    return call(
        rim_body,
        out,
        [SMEM] + [VMEM] * 8,
        "rim",
        32,
        [
            pltpu.VMEM((2 * len(rim_in), length), BF16),
            pltpu.VMEM((2 * (len(near) + len(rim_pass)), length), BF16),
            pltpu.VMEM(out.shape, BF16),
            pltpu.SemaphoreType.DMA((4,)),
        ],
        ANY,
    )(place, stencils[2], stencils[3], one_hot(natural, rim), left, right, passed, aligned, inner)


def solution(mesh):
    placed = (P("sec", "xy", None), P("sec", None, "xy"), P("sec", None, "xy"), P(), P())
    return jax.shard_map(
        body, mesh=mesh, in_specs=placed, out_specs=P(None, "xy", "sec"), check_vma=False
    )
```

```python
import numpy as np
import jax
import jax.numpy as jnp
from jax import lax
from jax.experimental import pallas as pl
from jax.experimental.pallas import tpu as pltpu
from jax.sharding import PartitionSpec as P

LANES = 128
HALO = 2
BF16 = jnp.bfloat16
F32 = jnp.float32
VMEM = pl.BlockSpec(memory_space=pltpu.VMEM)
SMEM = pl.BlockSpec(memory_space=pltpu.SMEM)
ANY = pl.BlockSpec(memory_space=pl.ANY)


def call(body, outs, ins, name, mib, scratch=(), space=VMEM):
    return pl.pallas_call(
        body,
        out_shape=outs,
        in_specs=ins,
        out_specs=jax.tree.map(lambda _: space, outs),
        scratch_shapes=scratch,
        compiler_params=pltpu.CompilerParams(vmem_limit_bytes=mib << 20),
        name=name,
    )


def shaped(*shape):
    return jax.ShapeDtypeStruct(shape, BF16)


def dot(left, right):
    return jnp.dot(left, right, preferred_element_type=F32)


def shift_pairs(count, steps):
    first, last = (max(0, -steps), min(count, count - steps))
    return [(source, source + steps) for source in range(first, last)]


def from_behind(value, axis, steps):
    return lax.ppermute(value, axis, shift_pairs(lax.axis_size(axis), steps))


def interpolation(amount, edge):
    row_index = lax.broadcasted_iota(jnp.int32, (edge, edge), 0)
    col_index = lax.broadcasted_iota(jnp.int32, (edge, edge), 1)
    offset = col_index - row_index
    w_before = ((-0.5 * amount + 1.0) * amount - 0.5) * amount
    w_center = (1.5 * amount - 2.5) * amount * amount + 1.0
    w_after = ((-1.5 * amount + 2.0) * amount + 0.5) * amount
    w_beyond = (0.5 * amount - 0.5) * amount * amount
    matrix = jnp.where(offset == -1, w_before, 0.0)
    matrix = jnp.where(offset == 0, w_center, matrix)
    matrix = jnp.where(offset == 1, w_after, matrix)
    return jnp.where(offset == 2, w_beyond, matrix)


def matrices_body(fraction_ref, out_ref):
    _, kinds, columns = fraction_ref.shape
    edge = out_ref.shape[-1]
    for kind in range(kinds):
        for block in range(columns):
            out_ref[kind, block] = interpolation(fraction_ref[0, kind, block], edge).astype(BF16)


def stage_body(source_ref, out_ref, sem):
    copy = pltpu.make_async_copy(source_ref, out_ref, sem)
    copy.start()
    copy.wait()


def choose_body(below_ref, above_ref, source_ref, for_below_ref, for_above_ref):
    edge = for_below_ref.shape[-1]
    columns = source_ref.shape[-1] // edge
    for coarse_ref, sign, out_ref in ((below_ref, -1, for_below_ref), (above_ref, 1, for_above_ref)):
        wanted = 0
        for block in range(columns):
            wanted += jnp.where(coarse_ref[0, 0, block] == sign, block + coarse_ref[0, 1, block], 0)
        for column in range(columns):

            @pl.when(wanted == column)
            def _():
                out_ref[0] = source_ref[0, :, column * edge : (column + 1) * edge]


def warp_body(coarse_ref, source_ref, above_ref, below_ref, matrix_ref, out_ref):
    _, edge, width = source_ref.shape
    columns = width // edge
    groups = out_ref.shape[0] // columns
    chunks, cols = out_ref.shape[1], out_ref.shape[2]
    for block in range(columns):
        down = coarse_ref[0, 0, block]
        anchor = block + coarse_ref[0, 1, block]
        picked = source_ref[0, :, 0:edge]
        for column in range(1, columns):
            picked = jnp.where(anchor == column, source_ref[0, :, column * edge : (column + 1) * edge], picked)
        picked = jnp.where(down < 0, above_ref[0], picked)
        picked = jnp.where(down > 0, below_ref[0], picked)
        rows_warped = dot(matrix_ref[0, block], picked).astype(BF16)
        warped = lax.dot_general(
            matrix_ref[1, block], rows_warped, (((1,), (1,)), ((), ())), preferred_element_type=F32
        ).astype(BF16)
        warped = warped.reshape(groups, cols, edge)
        for chunk in range(chunks):
            out_ref[block * groups : (block + 1) * groups, chunk] = warped[
                :, :, chunk * LANES : (chunk + 1) * LANES
            ]


def tap_index(out_pixels, in_pixels):
    out_sec, out_col = np.array(out_pixels).T[:, :, None]
    in_sec, in_col = np.array(in_pixels).T[:, None, :]
    tap_z, tap_x = in_sec - out_sec + 1, in_col - out_col + 1
    linked = (tap_z >= 0) & (tap_z < 3) & (tap_x >= 0) & (tap_x < 3)
    return np.where(linked, tap_z * 3 + tap_x, -1).astype(np.int32)


def stencil_matrix(index, kernel_ref, out_ref):
    rows, width = index.shape
    for tap_y in range(3):
        value = jnp.zeros((rows, width), F32)
        for tap in range(9):
            value = jnp.where(index == tap, kernel_ref[tap // 3, tap % 3, tap_y], value)
        high = value.astype(BF16)
        low = (value - high.astype(F32)).astype(BF16)
        out_ref[tap_y * rows : (tap_y + 1) * rows, :] = jnp.concatenate([high, low], axis=1)


def stencils_body(one_ref, two_ref, *refs):
    indices, outs = refs[:4], refs[4:]
    for place, (index_ref, out_ref) in enumerate(zip(indices, outs)):
        stencil_matrix(index_ref[...], one_ref if place % 2 == 0 else two_ref, out_ref)


def edges_body(data_ref, take_ref, first_ref, last_ref):
    sections, chunks, cols, lanes = data_ref.shape
    side = first_ref.shape[0]
    for chunk in range(chunks):
        rim = dot(take_ref[...], data_ref[:, chunk].reshape(sections * cols, lanes)).astype(BF16)
        where = slice(chunk * lanes, (chunk + 1) * lanes)
        first_ref[:, where] = rim[:side]
        last_ref[:, where] = rim[side:]


def shifted_sum(matrix_ref, volume, rows):
    size = volume.shape[1]
    every = dot(matrix_ref[...], volume)
    before, here, after = every[0:rows], every[rows : 2 * rows], every[2 * rows : 3 * rows]
    return pltpu.roll(before, 1, 1) + here + pltpu.roll(after, size - 1, 1)


def outside(place_ref, shape, lanes):
    lane = lax.broadcasted_iota(jnp.int32, shape, 1)
    gone = (lane < lanes) & (place_ref[2] > 0)
    return gone | ((lane >= shape[1] - lanes) & (place_ref[3] > 0))


def interior_body(place_ref, first_ref, second_ref, order_ref, data_ref, out_ref, passed_ref, aligned_ref, volume_ref, pass_ref):
    sections, chunks, cols, lanes = data_ref.shape
    main = sections * cols
    length = chunks * lanes
    for chunk in range(chunks):
        block = data_ref[:, chunk].reshape(main, lanes)
        volume_ref[0:main, chunk * lanes : (chunk + 1) * lanes] = block
        volume_ref[main : 2 * main, chunk * lanes : (chunk + 1) * lanes] = block
    volume = volume_ref[...]
    ordered = dot(order_ref[...], volume[0:main])
    rim = aligned_ref.shape[0]
    aligned_ref[...] = ordered[0:rim].astype(BF16)
    rows = first_ref.shape[0] // 3
    passed = jnp.maximum(shifted_sum(first_ref, volume, rows), 0.0)
    passed = jnp.where(outside(place_ref, passed.shape, lanes), 0.0, passed).astype(BF16)
    passed_ref[...] = passed[0 : passed_ref.shape[0]]
    pass_ref[0:rows] = passed
    pass_ref[rows : 2 * rows] = passed
    total = shifted_sum(second_ref, pass_ref[...], main - rim) + ordered[rim:]
    out_ref[...] = total[:, lanes : length - lanes].astype(BF16)


def rim_body(place_ref, first_ref, second_ref, put_ref, left_ref, right_ref, passed_ref, aligned_ref, inner_ref, out_ref, volume_ref, pass_ref, done_ref, sems):
    lanes = LANES
    sections = out_ref.shape[0]
    rim, length = aligned_ref.shape
    side = left_ref.shape[0]
    for start in (0, rim + 2 * side):
        volume_ref[start : start + rim] = aligned_ref[...]
        volume_ref[start + rim : start + rim + side] = left_ref[...]
        volume_ref[start + rim + side : start + rim + 2 * side] = right_ref[...]
    rows = first_ref.shape[0] // 3
    passed = jnp.maximum(shifted_sum(first_ref, volume_ref[...], rows), 0.0)
    row = lax.broadcasted_iota(jnp.int32, passed.shape, 0)
    gone = outside(place_ref, passed.shape, lanes)
    gone = gone | ((row < sections) & (place_ref[0] > 0))
    gone = gone | ((row >= rows - sections) & (place_ref[1] > 0))
    passed = jnp.where(gone, 0.0, passed).astype(BF16)
    inner = passed_ref.shape[0]
    for start in (0, inner + rows):
        pass_ref[start : start + inner] = passed_ref[...]
        pass_ref[start + inner : start + inner + rows] = passed
    second = shifted_sum(second_ref, pass_ref[...], rim)
    total = (second + aligned_ref[...].astype(F32))[:, lanes : length - lanes].astype(BF16)
    pieces = sems.shape[0]
    width = total.shape[1] // pieces
    copies = []
    for piece in range(pieces):
        where = slice(piece * width, (piece + 1) * width)
        rows_out = jnp.concatenate([total[:, where], inner_ref[:, where]], axis=0)
        done_ref[:, :, where] = dot(put_ref[...], rows_out).astype(BF16).reshape(sections, -1, width)
        copies.append(pltpu.make_async_copy(done_ref.at[:, :, where], out_ref.at[:, :, where], sems.at[piece]))
        copies[-1].start()
    for copy in copies:
        copy.wait()


def one_hot(out_pixels, in_pixels):
    match = [[pixel == other for other in in_pixels] for pixel in out_pixels]
    return jnp.asarray(np.array(match, np.float32), BF16)


def body(source, coarse, fraction, kernel_one, kernel_two):
    _, edge, width = source.shape
    columns = width // edge
    n_xy, n_sec = lax.axis_size("xy"), lax.axis_size("sec")
    cols = width // n_xy
    chunks = edge // LANES

    of_below, of_above = from_behind(coarse, "xy", -1), from_behind(coarse, "xy", 1)
    staged = call(stage_body, shaped(*source.shape), [ANY], "stage", 8, [pltpu.SemaphoreType.DMA])(source)
    of_below, of_above, staged = lax.optimization_barrier((of_below, of_above, staged))
    for_below, for_above = call(
        choose_body, (shaped(1, edge, edge),) * 2, [SMEM, SMEM, VMEM], "choose", 8
    )(of_below, of_above, staged)
    above, below = from_behind(for_below, "xy", 1), from_behind(for_above, "xy", -1)

    matrix = call(matrices_body, shaped(2, columns, edge, edge), [SMEM], "matrices", 16)(fraction)

    def pixels(*columns_taken):
        return [(section, column) for section in range(n_sec) for column in columns_taken]

    def by_column(*columns_taken):
        return [(section, column) for column in columns_taken for section in range(n_sec)]

    last = cols - 1
    natural = pixels(*range(cols))
    near = pixels(1, 2, last - 2, last - 1)
    rim = pixels(0, 1, last - 1, last)
    inner_pass = near + pixels(*range(3, last - 2))
    rim_in = rim + pixels(-2, -1) + pixels(last + 1, last + 2)
    rim_pass = by_column(-1, 0, last, last + 1)
    inner_out = pixels(*range(HALO, cols - HALO))
    indices = [
        tap_index(inner_pass, natural),
        tap_index(inner_out, inner_pass),
        tap_index(rim_pass, rim_in),
        tap_index(rim, near + rim_pass),
    ]
    stencils = call(
        stencils_body,
        tuple(shaped(3 * index.shape[0], 2 * index.shape[1]) for index in indices),
        [SMEM, SMEM] + [VMEM] * 4,
        "stencils",
        8,
    )(kernel_one, kernel_two, *map(jnp.asarray, indices))

    at_xy, at_sec = lax.axis_index("xy"), lax.axis_index("sec")
    place = jnp.stack([at_xy == 0, at_xy == n_xy - 1, at_sec == 0, at_sec == n_sec - 1]).astype(jnp.int32)
    above, below, matrix, stencils, place = lax.optimization_barrier((above, below, matrix, stencils, place))

    strip = call(warp_body, shaped(n_xy, chunks, cols, LANES), [SMEM] + [VMEM] * 4, "warp", 16)(
        coarse, staged, above, below, matrix
    )
    mine = lax.all_to_all(strip, "xy", split_axis=0, concat_axis=0, tiled=True)
    per_sec = n_xy * chunks // n_sec
    mine = jnp.pad(mine.reshape(n_xy * chunks, cols, LANES), ((1, 1), (0, 0), (0, 0)))
    spread = jnp.stack([mine[index * per_sec : (index + 1) * per_sec + 2] for index in range(n_sec)])
    data = lax.all_to_all(spread, "sec", split_axis=0, concat_axis=0, tiled=True)

    length = (per_sec + 2) * LANES
    out = shaped(n_sec, cols, per_sec * LANES)
    firsts, lasts = call(
        edges_body, (shaped(n_sec * HALO, length),) * 2, [VMEM, VMEM], "edges", 8
    )(data, one_hot(pixels(0, 1) + pixels(last - 1, last), natural))
    left, right = from_behind(lasts, "xy", 1), from_behind(firsts, "xy", -1)
    inner, passed, aligned = call(
        interior_body,
        (shaped(len(inner_out), per_sec * LANES), shaped(len(near), length), shaped(len(rim), length)),
        [SMEM] + [VMEM] * 4,
        "interior",
        32,
        [pltpu.VMEM((2 * len(natural), length), BF16), pltpu.VMEM((2 * len(inner_pass), length), BF16)],
    )(place, stencils[0], stencils[1], one_hot(rim + inner_out, natural), data)
    return call(
        rim_body,
        out,
        [SMEM] + [VMEM] * 8,
        "rim",
        32,
        [
            pltpu.VMEM((2 * len(rim_in), length), BF16),
            pltpu.VMEM((2 * (len(near) + len(rim_pass)), length), BF16),
            pltpu.VMEM(out.shape, BF16),
            pltpu.SemaphoreType.DMA((4,)),
        ],
        ANY,
    )(place, stencils[2], stencils[3], one_hot(natural, rim + inner_out), left, right, passed, aligned, inner)


def solution(mesh):
    placed = (P("sec", "xy", None), P("sec", None, "xy"), P("sec", None, "xy"), P(), P())
    return jax.shard_map(
        body, mesh=mesh, in_specs=placed, out_specs=P(None, "xy", "sec"), check_vma=False
    )
```

```python
import numpy as np
import jax
import jax.numpy as jnp
from jax import lax
from jax.experimental import pallas as pl
from jax.experimental.pallas import tpu as pltpu
from jax.sharding import PartitionSpec as P

LANES = 128
HALO = 2
BF16 = jnp.bfloat16
F32 = jnp.float32
VMEM = pl.BlockSpec(memory_space=pltpu.VMEM)
SMEM = pl.BlockSpec(memory_space=pltpu.SMEM)
ANY = pl.BlockSpec(memory_space=pl.ANY)


def call(body, outs, ins, name, mib, scratch=(), space=VMEM):
    return pl.pallas_call(
        body,
        out_shape=outs,
        in_specs=ins,
        out_specs=jax.tree.map(lambda _: space, outs),
        scratch_shapes=scratch,
        compiler_params=pltpu.CompilerParams(vmem_limit_bytes=mib << 20),
        name=name,
    )


def shaped(*shape):
    return jax.ShapeDtypeStruct(shape, BF16)


def dot(left, right):
    return jnp.dot(left, right, preferred_element_type=F32)


def shift_pairs(count, steps):
    first, last = (max(0, -steps), min(count, count - steps))
    return [(source, source + steps) for source in range(first, last)]


def from_behind(value, axis, steps):
    return lax.ppermute(value, axis, shift_pairs(lax.axis_size(axis), steps))


def interpolation(amount, edge):
    row_index = lax.broadcasted_iota(jnp.int32, (edge, edge), 0)
    col_index = lax.broadcasted_iota(jnp.int32, (edge, edge), 1)
    offset = col_index - row_index
    w_before = ((-0.5 * amount + 1.0) * amount - 0.5) * amount
    w_center = (1.5 * amount - 2.5) * amount * amount + 1.0
    w_after = ((-1.5 * amount + 2.0) * amount + 0.5) * amount
    w_beyond = (0.5 * amount - 0.5) * amount * amount
    matrix = jnp.where(offset == -1, w_before, 0.0)
    matrix = jnp.where(offset == 0, w_center, matrix)
    matrix = jnp.where(offset == 1, w_after, matrix)
    return jnp.where(offset == 2, w_beyond, matrix)


def matrices_body(fraction_ref, out_ref):
    _, kinds, columns = fraction_ref.shape
    edge = out_ref.shape[-1]
    for kind in range(kinds):
        for block in range(columns):
            out_ref[kind, block] = interpolation(fraction_ref[0, kind, block], edge).astype(BF16)


def stage_body(source_ref, out_ref, sem):
    copy = pltpu.make_async_copy(source_ref, out_ref, sem)
    copy.start()
    copy.wait()


def offsets(coarse_ref):
    tile = coarse_ref[0].astype(F32)
    return tile[0:1], tile[1:2] + lax.broadcasted_iota(jnp.int32, (1, tile.shape[1]), 1).astype(F32)


def choose_body(below_ref, above_ref, source_ref, for_below_ref, for_above_ref):
    edge = for_below_ref.shape[-1]
    columns = source_ref.shape[-1] // edge
    for coarse_ref, sign, out_ref in ((below_ref, -1, for_below_ref), (above_ref, 1, for_above_ref)):
        down, anchor = offsets(coarse_ref)
        wanted = jnp.sum(jnp.where(down == sign, anchor, 0.0)).astype(jnp.int32)
        for column in range(columns):

            @pl.when(wanted == column)
            def _():
                out_ref[0] = source_ref[0, :, column * edge : (column + 1) * edge]


def warp_body(coarse_ref, source_ref, above_ref, below_ref, matrix_ref, out_ref):
    _, edge, width = source_ref.shape
    columns = width // edge
    groups = out_ref.shape[0] // columns
    chunks, cols = out_ref.shape[1], out_ref.shape[2]
    downs, anchors = offsets(coarse_ref)
    lane = lax.broadcasted_iota(jnp.int32, downs.shape, 1)
    for block in range(columns):
        down = jnp.sum(jnp.where(lane == block, downs, 0.0)).astype(jnp.int32)
        anchor = jnp.sum(jnp.where(lane == block, anchors, 0.0)).astype(jnp.int32)
        picked = source_ref[0, :, 0:edge]
        for column in range(1, columns):
            picked = jnp.where(anchor == column, source_ref[0, :, column * edge : (column + 1) * edge], picked)
        picked = jnp.where(down < 0, above_ref[0], picked)
        picked = jnp.where(down > 0, below_ref[0], picked)
        rows_warped = dot(matrix_ref[0, block], picked).astype(BF16)
        warped = lax.dot_general(
            matrix_ref[1, block], rows_warped, (((1,), (1,)), ((), ())), preferred_element_type=F32
        ).astype(BF16)
        warped = warped.reshape(groups, cols, edge)
        for chunk in range(chunks):
            out_ref[block * groups : (block + 1) * groups, chunk] = warped[
                :, :, chunk * LANES : (chunk + 1) * LANES
            ]


def tap_index(out_pixels, in_pixels):
    out_sec, out_col = np.array(out_pixels).T[:, :, None]
    in_sec, in_col = np.array(in_pixels).T[:, None, :]
    tap_z, tap_x = in_sec - out_sec + 1, in_col - out_col + 1
    linked = (tap_z >= 0) & (tap_z < 3) & (tap_x >= 0) & (tap_x < 3)
    return np.where(linked, tap_z * 3 + tap_x, -1).astype(np.int32)


def stencil_matrix(index, kernel_ref, out_ref):
    rows, width = index.shape
    for tap_y in range(3):
        value = jnp.zeros((rows, width), F32)
        for tap in range(9):
            value = jnp.where(index == tap, kernel_ref[tap // 3, tap % 3, tap_y], value)
        high = value.astype(BF16)
        low = (value - high.astype(F32)).astype(BF16)
        out_ref[tap_y * rows : (tap_y + 1) * rows, :] = jnp.concatenate([high, low], axis=1)


def stencils_body(one_ref, two_ref, *refs):
    indices, outs = refs[:4], refs[4:]
    for place, (index_ref, out_ref) in enumerate(zip(indices, outs)):
        stencil_matrix(index_ref[...], one_ref if place % 2 == 0 else two_ref, out_ref)


def edges_body(data_ref, take_ref, first_ref, last_ref):
    sections, chunks, cols, lanes = data_ref.shape
    side = first_ref.shape[0]
    for chunk in range(chunks):
        rim = dot(take_ref[...], data_ref[:, chunk].reshape(sections * cols, lanes)).astype(BF16)
        where = slice(chunk * lanes, (chunk + 1) * lanes)
        first_ref[:, where] = rim[:side]
        last_ref[:, where] = rim[side:]


def shifted_sum(matrix_ref, volume, rows):
    size = volume.shape[1]
    every = dot(matrix_ref[...], volume)
    before, here, after = every[0:rows], every[rows : 2 * rows], every[2 * rows : 3 * rows]
    return pltpu.roll(before, 1, 1) + here + pltpu.roll(after, size - 1, 1)


def inside(keep_ref, which, values):
    keep = jnp.broadcast_to(keep_ref[which : which + 1], values.shape)
    return jnp.where(keep > 0.0, values, 0.0)


def interior_body(keep_ref, first_ref, second_ref, order_ref, data_ref, out_ref, passed_ref, aligned_ref, volume_ref, pass_ref):
    sections, chunks, cols, lanes = data_ref.shape
    main = sections * cols
    length = chunks * lanes
    for chunk in range(chunks):
        block = data_ref[:, chunk].reshape(main, lanes)
        volume_ref[0:main, chunk * lanes : (chunk + 1) * lanes] = block
        volume_ref[main : 2 * main, chunk * lanes : (chunk + 1) * lanes] = block
    volume = volume_ref[...]
    ordered = dot(order_ref[...], volume[0:main])
    rim = aligned_ref.shape[0]
    aligned_ref[...] = ordered[0:rim].astype(BF16)
    rows = first_ref.shape[0] // 3
    passed = jnp.maximum(shifted_sum(first_ref, volume, rows), 0.0)
    passed = inside(keep_ref, 0, passed).astype(BF16)
    passed_ref[...] = passed[0 : passed_ref.shape[0]]
    pass_ref[0:rows] = passed
    pass_ref[rows : 2 * rows] = passed
    total = shifted_sum(second_ref, pass_ref[...], main - rim) + ordered[rim:]
    out_ref[...] = total[:, lanes : length - lanes].astype(BF16)


def rim_body(keep_ref, first_ref, second_ref, put_ref, left_ref, right_ref, passed_ref, aligned_ref, inner_ref, out_ref, volume_ref, pass_ref, done_ref, sems):
    lanes = LANES
    sections = out_ref.shape[0]
    rim, length = aligned_ref.shape
    side = left_ref.shape[0]
    for start in (0, rim + 2 * side):
        volume_ref[start : start + rim] = aligned_ref[...]
        volume_ref[start + rim : start + rim + side] = left_ref[...]
        volume_ref[start + rim + side : start + rim + 2 * side] = right_ref[...]
    rows = first_ref.shape[0] // 3
    passed = jnp.maximum(shifted_sum(first_ref, volume_ref[...], rows), 0.0)
    passed = [
        inside(keep_ref, 1, passed[0:sections]),
        inside(keep_ref, 0, passed[sections : rows - sections]),
        inside(keep_ref, 2, passed[rows - sections :]),
    ]
    passed = jnp.concatenate(passed, axis=0).astype(BF16)
    inner = passed_ref.shape[0]
    for start in (0, inner + rows):
        pass_ref[start : start + inner] = passed_ref[...]
        pass_ref[start + inner : start + inner + rows] = passed
    second = shifted_sum(second_ref, pass_ref[...], rim)
    total = (second + aligned_ref[...].astype(F32))[:, lanes : length - lanes].astype(BF16)
    pieces = sems.shape[0]
    width = total.shape[1] // pieces
    copies = []
    for piece in range(pieces):
        where = slice(piece * width, (piece + 1) * width)
        rows_out = jnp.concatenate([total[:, where], inner_ref[:, where]], axis=0)
        done_ref[:, :, where] = dot(put_ref[...], rows_out).astype(BF16).reshape(sections, -1, width)
        copies.append(pltpu.make_async_copy(done_ref.at[:, :, where], out_ref.at[:, :, where], sems.at[piece]))
        copies[-1].start()
    for copy in copies:
        copy.wait()


def one_hot(out_pixels, in_pixels):
    match = [[pixel == other for other in in_pixels] for pixel in out_pixels]
    return jnp.asarray(np.array(match, np.float32), BF16)


def body(source, coarse, fraction, kernel_one, kernel_two):
    _, edge, width = source.shape
    columns = width // edge
    n_xy, n_sec = lax.axis_size("xy"), lax.axis_size("sec")
    cols = width // n_xy
    chunks = edge // LANES

    of_below, of_above = from_behind(coarse, "xy", -1), from_behind(coarse, "xy", 1)
    staged = call(stage_body, shaped(*source.shape), [ANY], "stage", 8, [pltpu.SemaphoreType.DMA])(source)
    of_below, of_above, staged = lax.optimization_barrier((of_below, of_above, staged))
    for_below, for_above = call(
        choose_body, (shaped(1, edge, edge),) * 2, [VMEM] * 3, "choose", 8
    )(of_below, of_above, staged)
    for_below, for_above, fraction, kernel_one, kernel_two = lax.optimization_barrier(
        (for_below, for_above, fraction, kernel_one, kernel_two)
    )
    above, below = from_behind(for_below, "xy", 1), from_behind(for_above, "xy", -1)

    matrix = call(matrices_body, shaped(2, columns, edge, edge), [SMEM], "matrices", 16)(fraction)

    def pixels(*columns_taken):
        return [(section, column) for section in range(n_sec) for column in columns_taken]

    def by_column(*columns_taken):
        return [(section, column) for column in columns_taken for section in range(n_sec)]

    last = cols - 1
    natural = pixels(*range(cols))
    near = pixels(1, 2, last - 2, last - 1)
    rim = pixels(0, 1, last - 1, last)
    inner_pass = near + pixels(*range(3, last - 2))
    rim_in = rim + pixels(-2, -1) + pixels(last + 1, last + 2)
    rim_pass = by_column(-1, 0, last, last + 1)
    inner_out = pixels(*range(HALO, cols - HALO))
    indices = [
        tap_index(inner_pass, natural),
        tap_index(inner_out, inner_pass),
        tap_index(rim_pass, rim_in),
        tap_index(rim, near + rim_pass),
    ]
    stencils = call(
        stencils_body,
        tuple(shaped(3 * index.shape[0], 2 * index.shape[1]) for index in indices),
        [SMEM, SMEM] + [VMEM] * 4,
        "stencils",
        8,
    )(kernel_one, kernel_two, *map(jnp.asarray, indices))

    at_xy, at_sec = lax.axis_index("xy"), lax.axis_index("sec")
    per_sec = n_xy * chunks // n_sec
    length = (per_sec + 2) * LANES
    lane = jnp.arange(length, dtype=jnp.int32)
    real = (lane >= jnp.where(at_sec == 0, LANES, 0)) & (lane < length - jnp.where(at_sec == n_sec - 1, LANES, 0))
    keep = jnp.stack([real, real & (at_xy > 0), real & (at_xy < n_xy - 1)]).astype(F32)
    above, below, matrix, stencils, keep = lax.optimization_barrier((above, below, matrix, stencils, keep))

    strip = call(warp_body, shaped(n_xy, chunks, cols, LANES), [VMEM] * 5, "warp", 16)(
        coarse, staged, above, below, matrix
    )
    mine = lax.all_to_all(strip, "xy", split_axis=0, concat_axis=0, tiled=True)
    mine = jnp.pad(mine.reshape(n_xy * chunks, cols, LANES), ((1, 1), (0, 0), (0, 0)))
    spread = jnp.stack([mine[index * per_sec : (index + 1) * per_sec + 2] for index in range(n_sec)])
    data = lax.all_to_all(spread, "sec", split_axis=0, concat_axis=0, tiled=True)

    out = shaped(n_sec, cols, per_sec * LANES)
    firsts, lasts = call(
        edges_body, (shaped(n_sec * HALO, length),) * 2, [VMEM, VMEM], "edges", 8
    )(data, one_hot(pixels(0, 1) + pixels(last - 1, last), natural))
    left, right = from_behind(lasts, "xy", 1), from_behind(firsts, "xy", -1)
    inner, passed, aligned = call(
        interior_body,
        (shaped(len(inner_out), per_sec * LANES), shaped(len(near), length), shaped(len(rim), length)),
        [VMEM] * 5,
        "interior",
        32,
        [pltpu.VMEM((2 * len(natural), length), BF16), pltpu.VMEM((2 * len(inner_pass), length), BF16)],
    )(keep, stencils[0], stencils[1], one_hot(rim + inner_out, natural), data)
    return call(
        rim_body,
        out,
        [VMEM] * 9,
        "rim",
        32,
        [
            pltpu.VMEM((2 * len(rim_in), length), BF16),
            pltpu.VMEM((2 * (len(near) + len(rim_pass)), length), BF16),
            pltpu.VMEM(out.shape, BF16),
            pltpu.SemaphoreType.DMA((4,)),
        ],
        ANY,
    )(keep, stencils[2], stencils[3], one_hot(natural, rim + inner_out), left, right, passed, aligned, inner)


def solution(mesh):
    placed = (P("sec", "xy", None), P("sec", None, "xy"), P("sec", None, "xy"), P(), P())
    return jax.shard_map(
        body, mesh=mesh, in_specs=placed, out_specs=P(None, "xy", "sec"), check_vma=False
    )
```

```python
import numpy as np
import jax
import jax.numpy as jnp
from jax import lax
from jax.experimental import pallas as pl
from jax.experimental.pallas import tpu as pltpu
from jax.sharding import PartitionSpec as P

LANES = 128
HALO = 2
BF16 = jnp.bfloat16
F32 = jnp.float32
VMEM = pl.BlockSpec(memory_space=pltpu.VMEM)
SMEM = pl.BlockSpec(memory_space=pltpu.SMEM)
ANY = pl.BlockSpec(memory_space=pl.ANY)


def call(body, outs, ins, name, mib, scratch=(), space=VMEM):
    return pl.pallas_call(
        body,
        out_shape=outs,
        in_specs=ins,
        out_specs=jax.tree.map(lambda _: space, outs),
        scratch_shapes=scratch,
        compiler_params=pltpu.CompilerParams(vmem_limit_bytes=mib << 20),
        name=name,
    )


def shaped(*shape):
    return jax.ShapeDtypeStruct(shape, BF16)


def dot(left, right):
    return jnp.dot(left, right, preferred_element_type=F32)


def shift_pairs(count, steps):
    first, last = (max(0, -steps), min(count, count - steps))
    return [(source, source + steps) for source in range(first, last)]


def from_behind(value, axis, steps):
    return lax.ppermute(value, axis, shift_pairs(lax.axis_size(axis), steps))


def interpolation(amount, edge):
    row_index = lax.broadcasted_iota(jnp.int32, (edge, edge), 0)
    col_index = lax.broadcasted_iota(jnp.int32, (edge, edge), 1)
    offset = col_index - row_index
    w_before = ((-0.5 * amount + 1.0) * amount - 0.5) * amount
    w_center = (1.5 * amount - 2.5) * amount * amount + 1.0
    w_after = ((-1.5 * amount + 2.0) * amount + 0.5) * amount
    w_beyond = (0.5 * amount - 0.5) * amount * amount
    matrix = jnp.where(offset == -1, w_before, 0.0)
    matrix = jnp.where(offset == 0, w_center, matrix)
    matrix = jnp.where(offset == 1, w_after, matrix)
    return jnp.where(offset == 2, w_beyond, matrix)


def matrices_body(fraction_ref, out_ref):
    _, kinds, columns = fraction_ref.shape
    edge = out_ref.shape[-1]
    for kind in range(kinds):
        for block in range(columns):
            out_ref[kind, block] = interpolation(fraction_ref[0, kind, block], edge).astype(BF16)


def stage_body(source_ref, out_ref, sem):
    copy = pltpu.make_async_copy(source_ref, out_ref, sem)
    copy.start()
    copy.wait()


def offsets(coarse_ref):
    tile = coarse_ref[0].astype(F32)
    return tile[0:1], tile[1:2] + lax.broadcasted_iota(jnp.int32, (1, tile.shape[1]), 1).astype(F32)


def choose_body(below_ref, above_ref, source_ref, for_below_ref, for_above_ref):
    edge = for_below_ref.shape[-1]
    columns = source_ref.shape[-1] // edge
    for coarse_ref, sign, out_ref in ((below_ref, -1, for_below_ref), (above_ref, 1, for_above_ref)):
        down, anchor = offsets(coarse_ref)
        wanted = jnp.sum(jnp.where(down == sign, anchor, 0.0)).astype(jnp.int32)
        for column in range(columns):

            @pl.when(wanted == column)
            def _():
                out_ref[0] = source_ref[0, :, column * edge : (column + 1) * edge]


def warp_body(coarse_ref, source_ref, above_ref, below_ref, matrix_ref, out_ref):
    _, edge, width = source_ref.shape
    columns = width // edge
    groups = out_ref.shape[0] // columns
    chunks, cols = out_ref.shape[1], out_ref.shape[2]
    downs, anchors = offsets(coarse_ref)
    lane = lax.broadcasted_iota(jnp.int32, downs.shape, 1)
    for block in range(columns):
        down = jnp.sum(jnp.where(lane == block, downs, 0.0)).astype(jnp.int32)
        anchor = jnp.sum(jnp.where(lane == block, anchors, 0.0)).astype(jnp.int32)
        picked = source_ref[0, :, 0:edge]
        for column in range(1, columns):
            picked = jnp.where(anchor == column, source_ref[0, :, column * edge : (column + 1) * edge], picked)
        picked = jnp.where(down < 0, above_ref[0], picked)
        picked = jnp.where(down > 0, below_ref[0], picked)
        rows_warped = dot(matrix_ref[0, block], picked).astype(BF16)
        warped = lax.dot_general(
            matrix_ref[1, block], rows_warped, (((1,), (1,)), ((), ())), preferred_element_type=F32
        ).astype(BF16)
        warped = warped.reshape(groups, cols, edge)
        for chunk in range(chunks):
            out_ref[block * groups : (block + 1) * groups, chunk] = warped[
                :, :, chunk * LANES : (chunk + 1) * LANES
            ]


def tap_index(out_pixels, in_pixels):
    out_sec, out_col = np.array(out_pixels).T[:, :, None]
    in_sec, in_col = np.array(in_pixels).T[:, None, :]
    tap_z, tap_x = in_sec - out_sec + 1, in_col - out_col + 1
    linked = (tap_z >= 0) & (tap_z < 3) & (tap_x >= 0) & (tap_x < 3)
    return np.where(linked, tap_z * 3 + tap_x, -1).astype(np.int32)


def stencil_matrix(index, kernel_ref, out_ref):
    rows, width = index.shape
    for tap_y in range(3):
        value = jnp.zeros((rows, width), F32)
        for tap in range(9):
            value = jnp.where(index == tap, kernel_ref[tap // 3, tap % 3, tap_y], value)
        high = value.astype(BF16)
        low = (value - high.astype(F32)).astype(BF16)
        out_ref[tap_y * rows : (tap_y + 1) * rows, :] = jnp.concatenate([high, low], axis=1)


def stencils_body(one_ref, two_ref, *refs):
    indices, outs = refs[:4], refs[4:]
    for place, (index_ref, out_ref) in enumerate(zip(indices, outs)):
        stencil_matrix(index_ref[...], one_ref if place % 2 == 0 else two_ref, out_ref)


def spread_body(data_ref, out_ref):
    parts, chunks, cols, lanes = out_ref.shape
    count = chunks - 1
    low = lax.broadcasted_iota(jnp.int32, (cols, lanes), 1) < lanes // 2
    nothing = jnp.zeros((cols, lanes), F32)
    for part in range(parts):
        first, end = part * count, (part + 1) * count
        before = data_ref[first - 1].astype(F32) if part > 0 else nothing
        after = data_ref[end].astype(F32) if part < parts - 1 else nothing
        out_ref[part, 0] = jnp.where(low, after, before).astype(BF16)
        out_ref[part, 1:chunks] = data_ref[first:end]


def edges_body(data_ref, take_ref, first_ref, last_ref):
    sections, chunks, cols, lanes = data_ref.shape
    side = first_ref.shape[0]
    for chunk in range(chunks):
        rim = dot(take_ref[...], data_ref[:, chunk].reshape(sections * cols, lanes)).astype(BF16)
        where = slice(chunk * lanes, (chunk + 1) * lanes)
        first_ref[:, where] = rim[:side]
        last_ref[:, where] = rim[side:]


def shifted_sum(matrix_ref, volume, rows):
    size = volume.shape[1]
    every = dot(matrix_ref[...], volume)
    before, here, after = every[0:rows], every[rows : 2 * rows], every[2 * rows : 3 * rows]
    return pltpu.roll(before, 1, 1) + here + pltpu.roll(after, size - 1, 1)


def inside(keep_ref, which, values):
    keep = jnp.broadcast_to(keep_ref[which : which + 1], values.shape)
    return jnp.where(keep > 0.0, values, 0.0)


def interior_body(keep_ref, first_ref, second_ref, order_ref, data_ref, out_ref, passed_ref, aligned_ref, volume_ref, pass_ref):
    sections, chunks, cols, lanes = data_ref.shape
    main = sections * cols
    length = chunks * lanes
    for chunk in range(chunks):
        block = data_ref[:, chunk].reshape(main, lanes)
        volume_ref[0:main, chunk * lanes : (chunk + 1) * lanes] = block
        volume_ref[main : 2 * main, chunk * lanes : (chunk + 1) * lanes] = block
    volume = volume_ref[...]
    ordered = dot(order_ref[...], volume[0:main])
    rim = aligned_ref.shape[0]
    aligned_ref[...] = ordered[0:rim].astype(BF16)
    rows = first_ref.shape[0] // 3
    passed = jnp.maximum(shifted_sum(first_ref, volume, rows), 0.0)
    passed = inside(keep_ref, 0, passed).astype(BF16)
    passed_ref[...] = passed[0 : passed_ref.shape[0]]
    pass_ref[0:rows] = passed
    pass_ref[rows : 2 * rows] = passed
    total = shifted_sum(second_ref, pass_ref[...], main - rim) + ordered[rim:]
    out_ref[...] = total[:, lanes:].astype(BF16)


def rim_body(keep_ref, first_ref, second_ref, put_ref, left_ref, right_ref, passed_ref, aligned_ref, inner_ref, out_ref, volume_ref, pass_ref, done_ref, sems):
    lanes = LANES
    sections = out_ref.shape[0]
    rim, length = aligned_ref.shape
    side = left_ref.shape[0]
    for start in (0, rim + 2 * side):
        volume_ref[start : start + rim] = aligned_ref[...]
        volume_ref[start + rim : start + rim + side] = left_ref[...]
        volume_ref[start + rim + side : start + rim + 2 * side] = right_ref[...]
    rows = first_ref.shape[0] // 3
    passed = jnp.maximum(shifted_sum(first_ref, volume_ref[...], rows), 0.0)
    passed = [
        inside(keep_ref, 1, passed[0:sections]),
        inside(keep_ref, 0, passed[sections : rows - sections]),
        inside(keep_ref, 2, passed[rows - sections :]),
    ]
    passed = jnp.concatenate(passed, axis=0).astype(BF16)
    inner = passed_ref.shape[0]
    for start in (0, inner + rows):
        pass_ref[start : start + inner] = passed_ref[...]
        pass_ref[start + inner : start + inner + rows] = passed
    second = shifted_sum(second_ref, pass_ref[...], rim)
    total = (second + aligned_ref[...].astype(F32))[:, lanes:].astype(BF16)
    pieces = sems.shape[0]
    width = total.shape[1] // pieces
    copies = []
    for piece in range(pieces):
        where = slice(piece * width, (piece + 1) * width)
        rows_out = jnp.concatenate([total[:, where], inner_ref[:, where]], axis=0)
        done_ref[:, :, where] = dot(put_ref[...], rows_out).astype(BF16).reshape(sections, -1, width)
        copies.append(pltpu.make_async_copy(done_ref.at[:, :, where], out_ref.at[:, :, where], sems.at[piece]))
        copies[-1].start()
    for copy in copies:
        copy.wait()


def one_hot(out_pixels, in_pixels):
    match = [[pixel == other for other in in_pixels] for pixel in out_pixels]
    return jnp.asarray(np.array(match, np.float32), BF16)


def body(source, coarse, fraction, kernel_one, kernel_two):
    _, edge, width = source.shape
    columns = width // edge
    n_xy, n_sec = lax.axis_size("xy"), lax.axis_size("sec")
    cols = width // n_xy
    chunks = edge // LANES

    of_below, of_above = from_behind(coarse, "xy", -1), from_behind(coarse, "xy", 1)
    staged = call(stage_body, shaped(*source.shape), [ANY], "stage", 8, [pltpu.SemaphoreType.DMA])(source)
    of_below, of_above, staged = lax.optimization_barrier((of_below, of_above, staged))
    for_below, for_above = call(
        choose_body, (shaped(1, edge, edge),) * 2, [VMEM] * 3, "choose", 8
    )(of_below, of_above, staged)
    for_below, for_above, fraction, kernel_one, kernel_two = lax.optimization_barrier(
        (for_below, for_above, fraction, kernel_one, kernel_two)
    )
    above, below = from_behind(for_below, "xy", 1), from_behind(for_above, "xy", -1)

    matrix = call(matrices_body, shaped(2, columns, edge, edge), [SMEM], "matrices", 16)(fraction)

    def pixels(*columns_taken):
        return [(section, column) for section in range(n_sec) for column in columns_taken]

    def by_column(*columns_taken):
        return [(section, column) for column in columns_taken for section in range(n_sec)]

    last = cols - 1
    natural = pixels(*range(cols))
    near = pixels(1, 2, last - 2, last - 1)
    rim = pixels(0, 1, last - 1, last)
    inner_pass = near + pixels(*range(3, last - 2))
    rim_in = rim + pixels(-2, -1) + pixels(last + 1, last + 2)
    rim_pass = by_column(-1, 0, last, last + 1)
    inner_out = pixels(*range(HALO, cols - HALO))
    indices = [
        tap_index(inner_pass, natural),
        tap_index(inner_out, inner_pass),
        tap_index(rim_pass, rim_in),
        tap_index(rim, near + rim_pass),
    ]
    stencils = call(
        stencils_body,
        tuple(shaped(3 * index.shape[0], 2 * index.shape[1]) for index in indices),
        [SMEM, SMEM] + [VMEM] * 4,
        "stencils",
        8,
    )(kernel_one, kernel_two, *map(jnp.asarray, indices))

    at_xy, at_sec = lax.axis_index("xy"), lax.axis_index("sec")
    per_sec = n_xy * chunks // n_sec
    length = (per_sec + 1) * LANES
    lane = jnp.arange(length, dtype=jnp.int32)
    after, before = lane < LANES // 2, (lane >= LANES // 2) & (lane < LANES)
    real = ~(after & (at_sec == n_sec - 1)) & ~(before & (at_sec == 0))
    keep = jnp.stack([real, real & (at_xy > 0), real & (at_xy < n_xy - 1)]).astype(F32)
    above, below, matrix, stencils, keep = lax.optimization_barrier((above, below, matrix, stencils, keep))

    strip = call(warp_body, shaped(n_xy, chunks, cols, LANES), [VMEM] * 5, "warp", 16)(
        coarse, staged, above, below, matrix
    )
    mine = lax.all_to_all(strip, "xy", split_axis=0, concat_axis=0, tiled=True)
    spread = call(spread_body, shaped(n_sec, per_sec + 1, cols, LANES), [VMEM], "spread", 8)(
        mine.reshape(n_xy * chunks, cols, LANES)
    )
    data = lax.all_to_all(spread, "sec", split_axis=0, concat_axis=0, tiled=True)

    out = shaped(n_sec, cols, per_sec * LANES)
    firsts, lasts = call(
        edges_body, (shaped(n_sec * HALO, length),) * 2, [VMEM, VMEM], "edges", 8
    )(data, one_hot(pixels(0, 1) + pixels(last - 1, last), natural))
    left, right = from_behind(lasts, "xy", 1), from_behind(firsts, "xy", -1)
    inner, passed, aligned = call(
        interior_body,
        (shaped(len(inner_out), per_sec * LANES), shaped(len(near), length), shaped(len(rim), length)),
        [VMEM] * 5,
        "interior",
        32,
        [pltpu.VMEM((2 * len(natural), length), BF16), pltpu.VMEM((2 * len(inner_pass), length), BF16)],
    )(keep, stencils[0], stencils[1], one_hot(rim + inner_out, natural), data)
    return call(
        rim_body,
        out,
        [VMEM] * 9,
        "rim",
        32,
        [
            pltpu.VMEM((2 * len(rim_in), length), BF16),
            pltpu.VMEM((2 * (len(near) + len(rim_pass)), length), BF16),
            pltpu.VMEM(out.shape, BF16),
            pltpu.SemaphoreType.DMA((4,)),
        ],
        ANY,
    )(keep, stencils[2], stencils[3], one_hot(natural, rim + inner_out), left, right, passed, aligned, inner)


def solution(mesh):
    placed = (P("sec", "xy", None), P("sec", None, "xy"), P("sec", None, "xy"), P(), P())
    return jax.shard_map(
        body, mesh=mesh, in_specs=placed, out_specs=P(None, "xy", "sec"), check_vma=False
    )
```

```python
import numpy as np
import jax
import jax.numpy as jnp
from jax import lax
from jax.experimental import pallas as pl
from jax.experimental.pallas import tpu as pltpu
from jax.sharding import PartitionSpec as P

LANES = 128
HALO = 2
BF16 = jnp.bfloat16
F32 = jnp.float32
VMEM = pl.BlockSpec(memory_space=pltpu.VMEM)
SMEM = pl.BlockSpec(memory_space=pltpu.SMEM)
ANY = pl.BlockSpec(memory_space=pl.ANY)


def call(body, outs, ins, name, mib, scratch=(), space=VMEM):
    return pl.pallas_call(
        body,
        out_shape=outs,
        in_specs=ins,
        out_specs=jax.tree.map(lambda _: space, outs),
        scratch_shapes=scratch,
        compiler_params=pltpu.CompilerParams(vmem_limit_bytes=mib << 20),
        name=name,
    )


def shaped(*shape):
    return jax.ShapeDtypeStruct(shape, BF16)


def dot(left, right):
    return jnp.dot(left, right, preferred_element_type=F32)


def shift_pairs(count, steps):
    first, last = (max(0, -steps), min(count, count - steps))
    return [(source, source + steps) for source in range(first, last)]


def from_behind(value, axis, steps):
    return lax.ppermute(value, axis, shift_pairs(lax.axis_size(axis), steps))


def interpolation(amount, edge):
    row_index = lax.broadcasted_iota(jnp.int32, (edge, edge), 0)
    col_index = lax.broadcasted_iota(jnp.int32, (edge, edge), 1)
    offset = col_index - row_index
    w_before = ((-0.5 * amount + 1.0) * amount - 0.5) * amount
    w_center = (1.5 * amount - 2.5) * amount * amount + 1.0
    w_after = ((-1.5 * amount + 2.0) * amount + 0.5) * amount
    w_beyond = (0.5 * amount - 0.5) * amount * amount
    matrix = jnp.where(offset == -1, w_before, 0.0)
    matrix = jnp.where(offset == 0, w_center, matrix)
    matrix = jnp.where(offset == 1, w_after, matrix)
    return jnp.where(offset == 2, w_beyond, matrix)


def matrices_body(fraction_ref, out_ref):
    _, kinds, columns = fraction_ref.shape
    edge = out_ref.shape[-1]
    for kind in range(kinds):
        for block in range(columns):
            out_ref[kind, block] = interpolation(fraction_ref[0, kind, block], edge).astype(BF16)


def stage_body(source_ref, out_ref, sem):
    copy = pltpu.make_async_copy(source_ref, out_ref, sem)
    copy.start()
    copy.wait()


def offsets(coarse_ref):
    tile = coarse_ref[0].astype(F32)
    return tile[0:1], tile[1:2] + lax.broadcasted_iota(jnp.int32, (1, tile.shape[1]), 1).astype(F32)


def choose_body(below_ref, above_ref, source_ref, for_below_ref, for_above_ref):
    edge = for_below_ref.shape[-1]
    columns = source_ref.shape[-1] // edge
    for coarse_ref, sign, out_ref in ((below_ref, -1, for_below_ref), (above_ref, 1, for_above_ref)):
        down, anchor = offsets(coarse_ref)
        wanted = jnp.sum(jnp.where(down == sign, anchor, 0.0)).astype(jnp.int32)
        for column in range(columns):

            @pl.when(wanted == column)
            def _():
                out_ref[0] = source_ref[0, :, column * edge : (column + 1) * edge]


def warp_block(matrix_ref, block, picked, out_ref):
    edge = picked.shape[0]
    total, chunks, cols, _ = out_ref.shape
    groups = edge // cols
    rows_warped = dot(matrix_ref[0, block], picked).astype(BF16)
    warped = lax.dot_general(
        matrix_ref[1, block], rows_warped, (((1,), (1,)), ((), ())), preferred_element_type=F32
    ).astype(BF16)
    warped = warped.reshape(groups, cols, edge)
    for chunk in range(chunks):
        out_ref[block * groups : (block + 1) * groups, chunk] = warped[:, :, chunk * LANES : (chunk + 1) * LANES]


def block_offsets(coarse_ref, columns):
    downs, anchors = offsets(coarse_ref)
    lane = lax.broadcasted_iota(jnp.int32, downs.shape, 1)

    def at(values, block):
        return jnp.sum(jnp.where(lane == block, values, 0.0)).astype(jnp.int32)

    return [(at(downs, block), at(anchors, block)) for block in range(columns)]


def warp_body(coarse_ref, source_ref, matrix_ref, out_ref):
    _, edge, width = source_ref.shape
    columns = width // edge
    for block, (_, anchor) in enumerate(block_offsets(coarse_ref, columns)):
        picked = source_ref[0, :, 0:edge]
        for column in range(1, columns):
            picked = jnp.where(anchor == column, source_ref[0, :, column * edge : (column + 1) * edge], picked)
        warp_block(matrix_ref, block, picked, out_ref)


def moved_body(sign, coarse_ref, moved_ref, matrix_ref, strip_ref, out_ref):
    out_ref[...] = strip_ref[...]
    for block, (down, _) in enumerate(block_offsets(coarse_ref, matrix_ref.shape[1])):

        @pl.when(down == sign)
        def _():
            warp_block(matrix_ref, block, moved_ref[0], out_ref)


def tap_index(out_pixels, in_pixels):
    out_sec, out_col = np.array(out_pixels).T[:, :, None]
    in_sec, in_col = np.array(in_pixels).T[:, None, :]
    tap_z, tap_x = in_sec - out_sec + 1, in_col - out_col + 1
    linked = (tap_z >= 0) & (tap_z < 3) & (tap_x >= 0) & (tap_x < 3)
    return np.where(linked, tap_z * 3 + tap_x, -1).astype(np.int32)


def stencil_matrix(index, kernel_ref, out_ref):
    rows, width = index.shape
    for tap_y in range(3):
        value = jnp.zeros((rows, width), F32)
        for tap in range(9):
            value = jnp.where(index == tap, kernel_ref[tap // 3, tap % 3, tap_y], value)
        high = value.astype(BF16)
        low = (value - high.astype(F32)).astype(BF16)
        out_ref[tap_y * rows : (tap_y + 1) * rows, :] = jnp.concatenate([high, low], axis=1)


def stencils_body(one_ref, two_ref, *refs):
    indices, outs = refs[:4], refs[4:]
    for place, (index_ref, out_ref) in enumerate(zip(indices, outs)):
        stencil_matrix(index_ref[...], one_ref if place % 2 == 0 else two_ref, out_ref)


def spread_body(data_ref, out_ref):
    parts, chunks, cols, lanes = out_ref.shape
    count = chunks - 1
    low = lax.broadcasted_iota(jnp.int32, (cols, lanes), 1) < lanes // 2
    nothing = jnp.zeros((cols, lanes), F32)
    for part in range(parts):
        first, end = part * count, (part + 1) * count
        before = data_ref[first - 1].astype(F32) if part > 0 else nothing
        after = data_ref[end].astype(F32) if part < parts - 1 else nothing
        out_ref[part, 0] = jnp.where(low, after, before).astype(BF16)
        out_ref[part, 1:chunks] = data_ref[first:end]


def edges_body(data_ref, take_ref, first_ref, last_ref):
    sections, chunks, cols, lanes = data_ref.shape
    side = first_ref.shape[0]
    for chunk in range(chunks):
        rim = dot(take_ref[...], data_ref[:, chunk].reshape(sections * cols, lanes)).astype(BF16)
        where = slice(chunk * lanes, (chunk + 1) * lanes)
        first_ref[:, where] = rim[:side]
        last_ref[:, where] = rim[side:]


def shifted_sum(matrix_ref, volume, rows):
    size = volume.shape[1]
    every = dot(matrix_ref[...], volume)
    before, here, after = every[0:rows], every[rows : 2 * rows], every[2 * rows : 3 * rows]
    return pltpu.roll(before, 1, 1) + here + pltpu.roll(after, size - 1, 1)


def inside(keep_ref, which, values):
    keep = jnp.broadcast_to(keep_ref[which : which + 1], values.shape)
    return jnp.where(keep > 0.0, values, 0.0)


def interior_body(keep_ref, first_ref, second_ref, order_ref, data_ref, out_ref, passed_ref, aligned_ref, volume_ref, pass_ref):
    sections, chunks, cols, lanes = data_ref.shape
    main = sections * cols
    length = chunks * lanes
    for chunk in range(chunks):
        block = data_ref[:, chunk].reshape(main, lanes)
        volume_ref[0:main, chunk * lanes : (chunk + 1) * lanes] = block
        volume_ref[main : 2 * main, chunk * lanes : (chunk + 1) * lanes] = block
    volume = volume_ref[...]
    ordered = dot(order_ref[...], volume[0:main])
    rim = aligned_ref.shape[0]
    aligned_ref[...] = ordered[0:rim].astype(BF16)
    rows = first_ref.shape[0] // 3
    passed = jnp.maximum(shifted_sum(first_ref, volume, rows), 0.0)
    passed = inside(keep_ref, 0, passed).astype(BF16)
    passed_ref[...] = passed[0 : passed_ref.shape[0]]
    pass_ref[0:rows] = passed
    pass_ref[rows : 2 * rows] = passed
    total = shifted_sum(second_ref, pass_ref[...], main - rim) + ordered[rim:]
    out_ref[...] = total[:, lanes:].astype(BF16)


def rim_body(keep_ref, first_ref, second_ref, put_ref, left_ref, right_ref, passed_ref, aligned_ref, inner_ref, out_ref, volume_ref, pass_ref, done_ref, sems):
    lanes = LANES
    sections = out_ref.shape[0]
    rim, length = aligned_ref.shape
    side = left_ref.shape[0]
    for start in (0, rim + 2 * side):
        volume_ref[start : start + rim] = aligned_ref[...]
        volume_ref[start + rim : start + rim + side] = left_ref[...]
        volume_ref[start + rim + side : start + rim + 2 * side] = right_ref[...]
    rows = first_ref.shape[0] // 3
    passed = jnp.maximum(shifted_sum(first_ref, volume_ref[...], rows), 0.0)
    passed = [
        inside(keep_ref, 1, passed[0:sections]),
        inside(keep_ref, 0, passed[sections : rows - sections]),
        inside(keep_ref, 2, passed[rows - sections :]),
    ]
    passed = jnp.concatenate(passed, axis=0).astype(BF16)
    inner = passed_ref.shape[0]
    for start in (0, inner + rows):
        pass_ref[start : start + inner] = passed_ref[...]
        pass_ref[start + inner : start + inner + rows] = passed
    second = shifted_sum(second_ref, pass_ref[...], rim)
    total = (second + aligned_ref[...].astype(F32))[:, lanes:].astype(BF16)
    pieces = sems.shape[0]
    width = total.shape[1] // pieces
    copies = []
    for piece in range(pieces):
        where = slice(piece * width, (piece + 1) * width)
        rows_out = jnp.concatenate([total[:, where], inner_ref[:, where]], axis=0)
        done_ref[:, :, where] = dot(put_ref[...], rows_out).astype(BF16).reshape(sections, -1, width)
        copies.append(pltpu.make_async_copy(done_ref.at[:, :, where], out_ref.at[:, :, where], sems.at[piece]))
        copies[-1].start()
    for copy in copies:
        copy.wait()


def one_hot(out_pixels, in_pixels):
    match = [[pixel == other for other in in_pixels] for pixel in out_pixels]
    return jnp.asarray(np.array(match, np.float32), BF16)


def body(source, coarse, fraction, kernel_one, kernel_two):
    _, edge, width = source.shape
    columns = width // edge
    n_xy, n_sec = lax.axis_size("xy"), lax.axis_size("sec")
    cols = width // n_xy
    chunks = edge // LANES

    of_below, of_above = from_behind(coarse, "xy", -1), from_behind(coarse, "xy", 1)
    staged = call(stage_body, shaped(*source.shape), [ANY], "stage", 8, [pltpu.SemaphoreType.DMA])(source)
    of_below, of_above, staged = lax.optimization_barrier((of_below, of_above, staged))
    for_below, for_above = call(
        choose_body, (shaped(1, edge, edge),) * 2, [VMEM] * 3, "choose", 8
    )(of_below, of_above, staged)
    for_below, for_above, fraction, kernel_one, kernel_two = lax.optimization_barrier(
        (for_below, for_above, fraction, kernel_one, kernel_two)
    )
    above, below = from_behind(for_below, "xy", 1), from_behind(for_above, "xy", -1)

    matrix = call(matrices_body, shaped(2, columns, edge, edge), [SMEM], "matrices", 16)(fraction)

    def pixels(*columns_taken):
        return [(section, column) for section in range(n_sec) for column in columns_taken]

    def by_column(*columns_taken):
        return [(section, column) for column in columns_taken for section in range(n_sec)]

    last = cols - 1
    natural = pixels(*range(cols))
    near = pixels(1, 2, last - 2, last - 1)
    rim = pixels(0, 1, last - 1, last)
    inner_pass = near + pixels(*range(3, last - 2))
    rim_in = rim + pixels(-2, -1) + pixels(last + 1, last + 2)
    rim_pass = by_column(-1, 0, last, last + 1)
    inner_out = pixels(*range(HALO, cols - HALO))
    indices = [
        tap_index(inner_pass, natural),
        tap_index(inner_out, inner_pass),
        tap_index(rim_pass, rim_in),
        tap_index(rim, near + rim_pass),
    ]
    stencils = call(
        stencils_body,
        tuple(shaped(3 * index.shape[0], 2 * index.shape[1]) for index in indices),
        [SMEM, SMEM] + [VMEM] * 4,
        "stencils",
        8,
    )(kernel_one, kernel_two, *map(jnp.asarray, indices))

    at_xy, at_sec = lax.axis_index("xy"), lax.axis_index("sec")
    per_sec = n_xy * chunks // n_sec
    length = (per_sec + 1) * LANES
    lane = jnp.arange(length, dtype=jnp.int32)
    after, before = lane < LANES // 2, (lane >= LANES // 2) & (lane < LANES)
    real = ~(after & (at_sec == n_sec - 1)) & ~(before & (at_sec == 0))
    keep = jnp.stack([real, real & (at_xy > 0), real & (at_xy < n_xy - 1)]).astype(F32)
    strip_of = shaped(n_xy, chunks, cols, LANES)
    strip = call(warp_body, strip_of, [VMEM] * 3, "warp", 16)(coarse, staged, matrix)
    strip, stencils, keep, above = lax.optimization_barrier((strip, stencils, keep, above))
    for moved, sign, name in ((above, -1, "warp_above"), (below, 1, "warp_below")):
        strip = call(lambda *refs, sign=sign: moved_body(sign, *refs), strip_of, [VMEM] * 4, name, 16)(
            coarse, moved, matrix, strip
        )
    mine = lax.all_to_all(strip, "xy", split_axis=0, concat_axis=0, tiled=True)
    spread = call(spread_body, shaped(n_sec, per_sec + 1, cols, LANES), [VMEM], "spread", 8)(
        mine.reshape(n_xy * chunks, cols, LANES)
    )
    data = lax.all_to_all(spread, "sec", split_axis=0, concat_axis=0, tiled=True)

    out = shaped(n_sec, cols, per_sec * LANES)
    firsts, lasts = call(
        edges_body, (shaped(n_sec * HALO, length),) * 2, [VMEM, VMEM], "edges", 8
    )(data, one_hot(pixels(0, 1) + pixels(last - 1, last), natural))
    left, right = from_behind(lasts, "xy", 1), from_behind(firsts, "xy", -1)
    inner, passed, aligned = call(
        interior_body,
        (shaped(len(inner_out), per_sec * LANES), shaped(len(near), length), shaped(len(rim), length)),
        [VMEM] * 5,
        "interior",
        32,
        [pltpu.VMEM((2 * len(natural), length), BF16), pltpu.VMEM((2 * len(inner_pass), length), BF16)],
    )(keep, stencils[0], stencils[1], one_hot(rim + inner_out, natural), data)
    return call(
        rim_body,
        out,
        [VMEM] * 9,
        "rim",
        32,
        [
            pltpu.VMEM((2 * len(rim_in), length), BF16),
            pltpu.VMEM((2 * (len(near) + len(rim_pass)), length), BF16),
            pltpu.VMEM(out.shape, BF16),
            pltpu.SemaphoreType.DMA((4,)),
        ],
        ANY,
    )(keep, stencils[2], stencils[3], one_hot(natural, rim + inner_out), left, right, passed, aligned, inner)


def solution(mesh):
    placed = (P("sec", "xy", None), P("sec", None, "xy"), P("sec", None, "xy"), P(), P())
    return jax.shard_map(
        body, mesh=mesh, in_specs=placed, out_specs=P(None, "xy", "sec"), check_vma=False
    )
```

```python
import numpy as np
import jax
import jax.numpy as jnp
from jax import lax
from jax.experimental import pallas as pl
from jax.experimental.pallas import tpu as pltpu
from jax.sharding import PartitionSpec as P

LANES = 128
HALO = 2
BF16 = jnp.bfloat16
F32 = jnp.float32
VMEM = pl.BlockSpec(memory_space=pltpu.VMEM)
SMEM = pl.BlockSpec(memory_space=pltpu.SMEM)
ANY = pl.BlockSpec(memory_space=pl.ANY)


def call(body, outs, ins, name, mib, scratch=(), space=VMEM):
    return pl.pallas_call(
        body,
        out_shape=outs,
        in_specs=ins,
        out_specs=jax.tree.map(lambda _: space, outs),
        scratch_shapes=scratch,
        compiler_params=pltpu.CompilerParams(vmem_limit_bytes=mib << 20),
        name=name,
    )


def shaped(*shape):
    return jax.ShapeDtypeStruct(shape, BF16)


def dot(left, right):
    return jnp.dot(left, right, preferred_element_type=F32)


def shift_pairs(count, steps):
    first, last = (max(0, -steps), min(count, count - steps))
    return [(source, source + steps) for source in range(first, last)]


def from_behind(value, axis, steps):
    return lax.ppermute(value, axis, shift_pairs(lax.axis_size(axis), steps))


def interpolation(amount, edge):
    row_index = lax.broadcasted_iota(jnp.int32, (edge, edge), 0)
    col_index = lax.broadcasted_iota(jnp.int32, (edge, edge), 1)
    offset = col_index - row_index
    w_before = ((-0.5 * amount + 1.0) * amount - 0.5) * amount
    w_center = (1.5 * amount - 2.5) * amount * amount + 1.0
    w_after = ((-1.5 * amount + 2.0) * amount + 0.5) * amount
    w_beyond = (0.5 * amount - 0.5) * amount * amount
    matrix = jnp.where(offset == -1, w_before, 0.0)
    matrix = jnp.where(offset == 0, w_center, matrix)
    matrix = jnp.where(offset == 1, w_after, matrix)
    return jnp.where(offset == 2, w_beyond, matrix)


def matrices_body(fraction_ref, out_ref):
    _, kinds, columns = fraction_ref.shape
    edge = out_ref.shape[-1]
    for kind in range(kinds):
        for block in range(columns):
            out_ref[kind, block] = interpolation(fraction_ref[0, kind, block], edge).astype(BF16)


def stage_body(source_ref, out_ref, sem):
    copy = pltpu.make_async_copy(source_ref, out_ref, sem)
    copy.start()
    copy.wait()


def offsets(coarse_ref):
    tile = coarse_ref[0].astype(F32)
    return tile[0:1], tile[1:2] + lax.broadcasted_iota(jnp.int32, (1, tile.shape[1]), 1).astype(F32)


def choose_body(below_ref, above_ref, source_ref, for_below_ref, for_above_ref):
    edge = for_below_ref.shape[-1]
    columns = source_ref.shape[-1] // edge
    for coarse_ref, sign, out_ref in ((below_ref, -1, for_below_ref), (above_ref, 1, for_above_ref)):
        down, anchor = offsets(coarse_ref)
        wanted = jnp.sum(jnp.where(down == sign, anchor, 0.0)).astype(jnp.int32)
        for column in range(columns):

            @pl.when(wanted == column)
            def _():
                out_ref[0] = source_ref[0, :, column * edge : (column + 1) * edge]


def warp_block(matrix_ref, block, picked, out_ref):
    edge = picked.shape[0]
    total, chunks, cols, _ = out_ref.shape
    groups = edge // cols
    rows_warped = dot(matrix_ref[0, block], picked).astype(BF16)
    warped = lax.dot_general(
        matrix_ref[1, block], rows_warped, (((1,), (1,)), ((), ())), preferred_element_type=F32
    ).astype(BF16)
    warped = warped.reshape(groups, cols, edge)
    for chunk in range(chunks):
        out_ref[block * groups : (block + 1) * groups, chunk] = warped[:, :, chunk * LANES : (chunk + 1) * LANES]


def block_offsets(coarse_ref, columns):
    downs, anchors = offsets(coarse_ref)
    lane = lax.broadcasted_iota(jnp.int32, downs.shape, 1)

    def at(values, block):
        return jnp.sum(jnp.where(lane == block, values, 0.0)).astype(jnp.int32)

    return [(at(downs, block), at(anchors, block)) for block in range(columns)]


def warp_body(coarse_ref, source_ref, matrix_ref, out_ref):
    _, edge, width = source_ref.shape
    columns = width // edge
    for block, (_, anchor) in enumerate(block_offsets(coarse_ref, columns)):
        picked = source_ref[0, :, 0:edge]
        for column in range(1, columns):
            picked = jnp.where(anchor == column, source_ref[0, :, column * edge : (column + 1) * edge], picked)
        warp_block(matrix_ref, block, picked, out_ref)


def moved_body(sign, coarse_ref, moved_ref, matrix_ref, strip_ref, out_ref):
    out_ref[...] = strip_ref[...]
    for block, (down, _) in enumerate(block_offsets(coarse_ref, matrix_ref.shape[1])):

        @pl.when(down == sign)
        def _():
            warp_block(matrix_ref, block, moved_ref[0], out_ref)


def tap_index(out_pixels, in_pixels):
    out_sec, out_col = np.array(out_pixels).T[:, :, None]
    in_sec, in_col = np.array(in_pixels).T[:, None, :]
    tap_z, tap_x = in_sec - out_sec + 1, in_col - out_col + 1
    linked = (tap_z >= 0) & (tap_z < 3) & (tap_x >= 0) & (tap_x < 3)
    return np.where(linked, tap_z * 3 + tap_x, -1).astype(np.int32)


def stencil_matrix(index, kernel_ref, out_ref):
    rows, width = index.shape
    for tap_y in range(3):
        value = jnp.zeros((rows, width), F32)
        for tap in range(9):
            value = jnp.where(index == tap, kernel_ref[tap // 3, tap % 3, tap_y], value)
        high = value.astype(BF16)
        low = (value - high.astype(F32)).astype(BF16)
        out_ref[tap_y * rows : (tap_y + 1) * rows, :] = jnp.concatenate([high, low], axis=1)


def stencils_body(one_ref, two_ref, *refs):
    half = len(refs) // 2
    indices, outs = refs[:half], refs[half:]
    for place, (index_ref, out_ref) in enumerate(zip(indices, outs)):
        stencil_matrix(index_ref[...], one_ref if place % 2 == 0 else two_ref, out_ref)


def spread_body(data_ref, out_ref):
    parts, chunks, cols, lanes = out_ref.shape
    count = chunks - 1
    low = lax.broadcasted_iota(jnp.int32, (cols, lanes), 1) < lanes // 2
    nothing = jnp.zeros((cols, lanes), F32)
    for part in range(parts):
        first, end = part * count, (part + 1) * count
        before = data_ref[first - 1].astype(F32) if part > 0 else nothing
        after = data_ref[end].astype(F32) if part < parts - 1 else nothing
        out_ref[part, 0] = jnp.where(low, after, before).astype(BF16)
        out_ref[part, 1:chunks] = data_ref[first:end]


def edges_body(data_ref, take_ref, first_ref, last_ref):
    sections, chunks, cols, lanes = data_ref.shape
    side = first_ref.shape[0]
    for chunk in range(chunks):
        rim = dot(take_ref[...], data_ref[:, chunk].reshape(sections * cols, lanes)).astype(BF16)
        where = slice(chunk * lanes, (chunk + 1) * lanes)
        first_ref[:, where] = rim[:side]
        last_ref[:, where] = rim[side:]


def shifted_sum(matrix_ref, volume, rows):
    size = volume.shape[1]
    every = dot(matrix_ref[...], volume)
    before, here, after = every[0:rows], every[rows : 2 * rows], every[2 * rows : 3 * rows]
    return pltpu.roll(before, 1, 1) + here + pltpu.roll(after, size - 1, 1)


def inside(keep_ref, which, values):
    keep = jnp.broadcast_to(keep_ref[which : which + 1], values.shape)
    return jnp.where(keep > 0.0, values, 0.0)


def interior_body(keep_ref, first_ref, second_ref, order_ref, data_ref, out_ref, passed_ref, aligned_ref, volume_ref, pass_ref):
    sections, chunks, cols, lanes = data_ref.shape
    main = sections * cols
    length = chunks * lanes
    for chunk in range(chunks):
        block = data_ref[:, chunk].reshape(main, lanes)
        volume_ref[0:main, chunk * lanes : (chunk + 1) * lanes] = block
        volume_ref[main : 2 * main, chunk * lanes : (chunk + 1) * lanes] = block
    volume = volume_ref[...]
    ordered = dot(order_ref[...], volume[0:main])
    rim = aligned_ref.shape[0]
    aligned_ref[...] = ordered[0:rim].astype(BF16)
    rows = first_ref.shape[0] // 3
    passed = jnp.maximum(shifted_sum(first_ref, volume, rows), 0.0)
    passed = inside(keep_ref, 0, passed).astype(BF16)
    passed_ref[...] = passed[0 : passed_ref.shape[0]]
    pass_ref[0:rows] = passed
    pass_ref[rows : 2 * rows] = passed
    total = shifted_sum(second_ref, pass_ref[...], main - rim) + ordered[rim:]
    out_ref[...] = total[:, lanes:].astype(BF16)


def rim_rows(which, keep_ref, first_ref, second_ref, halo_ref, passed_ref, aligned_ref, volume_ref, pass_ref):
    sections = halo_ref.shape[0] // HALO
    side = halo_ref.shape[0]
    own = slice(which * side, (which + 1) * side)
    aligned = aligned_ref[own]
    for start in (0, 2 * side):
        volume_ref[start : start + side] = aligned
        volume_ref[start + side : start + 2 * side] = halo_ref[...]
    rows = first_ref.shape[0] // 3
    passed = jnp.maximum(shifted_sum(first_ref, volume_ref[...], rows), 0.0)
    low = inside(keep_ref, 0 if which else 1, passed[0:sections])
    high = inside(keep_ref, 2 if which else 0, passed[sections:])
    passed = jnp.concatenate([low, high], axis=0).astype(BF16)
    for start in (0, side + rows):
        pass_ref[start : start + side] = passed_ref[own]
        pass_ref[start + side : start + side + rows] = passed
    second = shifted_sum(second_ref, pass_ref[...], side)
    return (second + aligned.astype(F32))[:, LANES:].astype(BF16)


def left_body(keep_ref, first_ref, second_ref, put_ref, halo_ref, passed_ref, aligned_ref, inner_ref, out_ref, volume_ref, pass_ref):
    total = rim_rows(0, keep_ref, first_ref, second_ref, halo_ref, passed_ref, aligned_ref, volume_ref, pass_ref)
    rows_out = jnp.concatenate([total, inner_ref[...]], axis=0)
    out_ref[...] = dot(put_ref[...], rows_out).astype(BF16).reshape(out_ref.shape)


def right_body(keep_ref, first_ref, second_ref, put_ref, halo_ref, passed_ref, aligned_ref, inner_ref, out_ref, volume_ref, pass_ref, done_ref, sems):
    sections, cols, length = out_ref.shape
    half = cols // 2
    pieces = sems.shape[0] - 1
    copies = [pltpu.make_async_copy(inner_ref.at[:, 0:half], out_ref.at[:, 0:half], sems.at[pieces])]
    copies[0].start()
    total = rim_rows(1, keep_ref, first_ref, second_ref, halo_ref, passed_ref, aligned_ref, volume_ref, pass_ref)
    width = length // pieces
    for piece in range(pieces):
        where = slice(piece * width, (piece + 1) * width)
        placed = dot(put_ref[...], total[:, where]).astype(BF16).reshape(sections, half, width)
        done_ref[:, :, where] = placed + inner_ref[:, half:, where]
        copies.append(
            pltpu.make_async_copy(done_ref.at[:, :, where], out_ref.at[:, half:, where], sems.at[piece])
        )
        copies[-1].start()
    for copy in copies:
        copy.wait()


def one_hot(out_pixels, in_pixels):
    match = [[pixel == other for other in in_pixels] for pixel in out_pixels]
    return jnp.asarray(np.array(match, np.float32), BF16)


def body(source, coarse, fraction, kernel_one, kernel_two):
    _, edge, width = source.shape
    columns = width // edge
    n_xy, n_sec = lax.axis_size("xy"), lax.axis_size("sec")
    cols = width // n_xy
    chunks = edge // LANES

    of_below, of_above = from_behind(coarse, "xy", -1), from_behind(coarse, "xy", 1)
    staged = call(stage_body, shaped(*source.shape), [ANY], "stage", 8, [pltpu.SemaphoreType.DMA])(source)
    of_below, of_above, staged = lax.optimization_barrier((of_below, of_above, staged))
    for_below, for_above = call(
        choose_body, (shaped(1, edge, edge),) * 2, [VMEM] * 3, "choose", 8
    )(of_below, of_above, staged)
    for_below, for_above, fraction, kernel_one, kernel_two = lax.optimization_barrier(
        (for_below, for_above, fraction, kernel_one, kernel_two)
    )
    above, below = from_behind(for_below, "xy", 1), from_behind(for_above, "xy", -1)

    matrix = call(matrices_body, shaped(2, columns, edge, edge), [SMEM], "matrices", 16)(fraction)

    def pixels(*columns_taken):
        return [(section, column) for section in range(n_sec) for column in columns_taken]

    def by_column(*columns_taken):
        return [(section, column) for column in columns_taken for section in range(n_sec)]

    last = cols - 1
    natural = pixels(*range(cols))
    near = pixels(1, 2), pixels(last - 2, last - 1)
    rim = pixels(0, 1), pixels(last - 1, last)
    beyond = pixels(-2, -1), pixels(last + 1, last + 2)
    rim_pass = by_column(-1, 0), by_column(last, last + 1)
    inner_pass = near[0] + near[1] + pixels(*range(3, last - 2))
    inner_out = pixels(*range(HALO, cols - HALO))
    indices = [tap_index(inner_pass, natural), tap_index(inner_out, inner_pass)]
    for which in range(2):
        indices.append(tap_index(rim_pass[which], rim[which] + beyond[which]))
        indices.append(tap_index(rim[which], near[which] + rim_pass[which]))
    stencils = call(
        stencils_body,
        tuple(shaped(3 * index.shape[0], 2 * index.shape[1]) for index in indices),
        [SMEM, SMEM] + [VMEM] * len(indices),
        "stencils",
        8,
    )(kernel_one, kernel_two, *map(jnp.asarray, indices))

    at_xy, at_sec = lax.axis_index("xy"), lax.axis_index("sec")
    per_sec = n_xy * chunks // n_sec
    length = (per_sec + 1) * LANES
    lane = jnp.arange(length, dtype=jnp.int32)
    after, before = lane < LANES // 2, (lane >= LANES // 2) & (lane < LANES)
    real = ~(after & (at_sec == n_sec - 1)) & ~(before & (at_sec == 0))
    keep = jnp.stack([real, real & (at_xy > 0), real & (at_xy < n_xy - 1)]).astype(F32)
    strip_of = shaped(n_xy, chunks, cols, LANES)
    strip = call(warp_body, strip_of, [VMEM] * 3, "warp", 16)(coarse, staged, matrix)
    strip, stencils, keep, above = lax.optimization_barrier((strip, stencils, keep, above))
    for moved, sign, name in ((above, -1, "warp_above"), (below, 1, "warp_below")):
        strip = call(lambda *refs, sign=sign: moved_body(sign, *refs), strip_of, [VMEM] * 4, name, 16)(
            coarse, moved, matrix, strip
        )
    mine = lax.all_to_all(strip, "xy", split_axis=0, concat_axis=0, tiled=True)
    spread = call(spread_body, shaped(n_sec, per_sec + 1, cols, LANES), [VMEM], "spread", 8)(
        mine.reshape(n_xy * chunks, cols, LANES)
    )
    data = lax.all_to_all(spread, "sec", split_axis=0, concat_axis=0, tiled=True)

    out = shaped(n_sec, cols, per_sec * LANES)
    firsts, lasts = call(
        edges_body, (shaped(n_sec * HALO, length),) * 2, [VMEM, VMEM], "edges", 8
    )(data, one_hot(pixels(0, 1) + pixels(last - 1, last), natural))
    left, right = from_behind(lasts, "xy", 1), from_behind(firsts, "xy", -1)
    side = n_sec * HALO
    inner, passed, aligned = call(
        interior_body,
        (shaped(len(inner_out), per_sec * LANES), shaped(2 * side, length), shaped(2 * side, length)),
        [VMEM] * 5,
        "interior",
        32,
        [pltpu.VMEM((2 * len(natural), length), BF16), pltpu.VMEM((2 * len(inner_pass), length), BF16)],
    )(keep, stencils[0], stencils[1], one_hot(rim[0] + rim[1] + inner_out, natural), data)
    scratch = [pltpu.VMEM((4 * side, length), BF16)] * 2
    placed = call(left_body, out, [VMEM] * 8, "left", 24, scratch)(
        keep, stencils[2], stencils[3], one_hot(natural, rim[0] + inner_out), left, passed, aligned, inner
    )
    scratch = scratch + [pltpu.VMEM((n_sec, cols // 2, per_sec * LANES), BF16), pltpu.SemaphoreType.DMA((5,))]
    return call(right_body, out, [VMEM] * 8, "right", 24, scratch, ANY)(
        keep, stencils[4], stencils[5], one_hot(pixels(*range(cols // 2, cols)), rim[1]), right, passed, aligned, placed
    )


def solution(mesh):
    placed = (P("sec", "xy", None), P("sec", None, "xy"), P("sec", None, "xy"), P(), P())
    return jax.shard_map(
        body, mesh=mesh, in_specs=placed, out_specs=P(None, "xy", "sec"), check_vma=False
    )
```

```python
import numpy as np
import jax
import jax.numpy as jnp
from jax import lax
from jax.experimental import pallas as pl
from jax.experimental.pallas import tpu as pltpu
from jax.sharding import PartitionSpec as P

LANES = 128
HALO = 2
BF16 = jnp.bfloat16
F32 = jnp.float32
VMEM = pl.BlockSpec(memory_space=pltpu.VMEM)
SMEM = pl.BlockSpec(memory_space=pltpu.SMEM)
ANY = pl.BlockSpec(memory_space=pl.ANY)


def call(body, outs, ins, name, mib, scratch=(), space=VMEM):
    return pl.pallas_call(
        body,
        out_shape=outs,
        in_specs=ins,
        out_specs=jax.tree.map(lambda _: space, outs),
        scratch_shapes=scratch,
        compiler_params=pltpu.CompilerParams(vmem_limit_bytes=mib << 20),
        name=name,
    )


def shaped(*shape):
    return jax.ShapeDtypeStruct(shape, BF16)


def dot(left, right):
    return jnp.dot(left, right, preferred_element_type=F32)


def shift_pairs(count, steps):
    first, last = (max(0, -steps), min(count, count - steps))
    return [(source, source + steps) for source in range(first, last)]


def from_behind(value, axis, steps):
    return lax.ppermute(value, axis, shift_pairs(lax.axis_size(axis), steps))


def interpolation(amount, edge):
    row_index = lax.broadcasted_iota(jnp.int32, (edge, edge), 0)
    col_index = lax.broadcasted_iota(jnp.int32, (edge, edge), 1)
    offset = col_index - row_index
    w_before = ((-0.5 * amount + 1.0) * amount - 0.5) * amount
    w_center = (1.5 * amount - 2.5) * amount * amount + 1.0
    w_after = ((-1.5 * amount + 2.0) * amount + 0.5) * amount
    w_beyond = (0.5 * amount - 0.5) * amount * amount
    matrix = jnp.where(offset == -1, w_before, 0.0)
    matrix = jnp.where(offset == 0, w_center, matrix)
    matrix = jnp.where(offset == 1, w_after, matrix)
    return jnp.where(offset == 2, w_beyond, matrix)


def matrices_body(fraction_ref, out_ref):
    _, kinds, columns = fraction_ref.shape
    edge = out_ref.shape[-1]
    for kind in range(kinds):
        for block in range(columns):
            out_ref[kind, block] = interpolation(fraction_ref[0, kind, block], edge).astype(BF16)


def stage_body(source_ref, out_ref, sem):
    copy = pltpu.make_async_copy(source_ref, out_ref, sem)
    copy.start()
    copy.wait()


def offsets(coarse_ref):
    tile = coarse_ref[0].astype(F32)
    return tile[0:1], tile[1:2] + lax.broadcasted_iota(jnp.int32, (1, tile.shape[1]), 1).astype(F32)


def choose_body(below_ref, above_ref, source_ref, for_below_ref, for_above_ref):
    edge = for_below_ref.shape[-1]
    columns = source_ref.shape[-1] // edge
    for coarse_ref, sign, out_ref in ((below_ref, -1, for_below_ref), (above_ref, 1, for_above_ref)):
        down, anchor = offsets(coarse_ref)
        wanted = jnp.sum(jnp.where(down == sign, anchor, 0.0)).astype(jnp.int32)
        for column in range(columns):

            @pl.when(wanted == column)
            def _():
                out_ref[0] = source_ref[0, :, column * edge : (column + 1) * edge]


def warp_block(matrix_ref, block, picked, out_ref):
    edge = picked.shape[0]
    total, chunks, cols, _ = out_ref.shape
    groups = edge // cols
    rows_warped = dot(matrix_ref[0, block], picked).astype(BF16)
    warped = lax.dot_general(
        matrix_ref[1, block], rows_warped, (((1,), (1,)), ((), ())), preferred_element_type=F32
    ).astype(BF16)
    warped = warped.reshape(groups, cols, edge)
    for chunk in range(chunks):
        out_ref[block * groups : (block + 1) * groups, chunk] = warped[:, :, chunk * LANES : (chunk + 1) * LANES]


def block_offsets(coarse_ref, columns):
    downs, anchors = offsets(coarse_ref)
    lane = lax.broadcasted_iota(jnp.int32, downs.shape, 1)

    def at(values, block):
        return jnp.sum(jnp.where(lane == block, values, 0.0)).astype(jnp.int32)

    return [(at(downs, block), at(anchors, block)) for block in range(columns)]


def warp_body(coarse_ref, source_ref, matrix_ref, out_ref):
    _, edge, width = source_ref.shape
    columns = width // edge
    for block, (_, anchor) in enumerate(block_offsets(coarse_ref, columns)):
        picked = source_ref[0, :, 0:edge]
        for column in range(1, columns):
            picked = jnp.where(anchor == column, source_ref[0, :, column * edge : (column + 1) * edge], picked)
        warp_block(matrix_ref, block, picked, out_ref)


def moved_body(sign, coarse_ref, moved_ref, matrix_ref, strip_ref, out_ref):
    out_ref[...] = strip_ref[...]
    for block, (down, _) in enumerate(block_offsets(coarse_ref, matrix_ref.shape[1])):

        @pl.when(down == sign)
        def _():
            warp_block(matrix_ref, block, moved_ref[0], out_ref)


def tap_index(out_pixels, in_pixels):
    out_sec, out_col = np.array(out_pixels).T[:, :, None]
    in_sec, in_col = np.array(in_pixels).T[:, None, :]
    tap_z, tap_x = in_sec - out_sec + 1, in_col - out_col + 1
    linked = (tap_z >= 0) & (tap_z < 3) & (tap_x >= 0) & (tap_x < 3)
    return np.where(linked, tap_z * 3 + tap_x, -1).astype(np.int32)


def stencil_matrix(index, kernel_ref, out_ref):
    rows, width = index.shape
    for tap_y in range(3):
        value = jnp.zeros((rows, width), F32)
        for tap in range(9):
            value = jnp.where(index == tap, kernel_ref[tap // 3, tap % 3, tap_y], value)
        high = value.astype(BF16)
        low = (value - high.astype(F32)).astype(BF16)
        out_ref[tap_y * rows : (tap_y + 1) * rows, :] = jnp.concatenate([high, low], axis=1)


def stencils_body(one_ref, two_ref, *refs):
    half = len(refs) // 2
    indices, outs = refs[:half], refs[half:]
    for place, (index_ref, out_ref) in enumerate(zip(indices, outs)):
        stencil_matrix(index_ref[...], one_ref if place % 2 == 0 else two_ref, out_ref)


def spread_body(data_ref, out_ref):
    parts, chunks, cols, lanes = out_ref.shape
    count = chunks - 1
    low = lax.broadcasted_iota(jnp.int32, (cols, lanes), 1) < lanes // 2
    nothing = jnp.zeros((cols, lanes), F32)
    for part in range(parts):
        first, end = part * count, (part + 1) * count
        before = data_ref[first - 1].astype(F32) if part > 0 else nothing
        after = data_ref[end].astype(F32) if part < parts - 1 else nothing
        out_ref[part, 0] = jnp.where(low, after, before).astype(BF16)
        out_ref[part, 1:chunks] = data_ref[first:end]


def edges_body(data_ref, take_ref, first_ref, last_ref):
    sections, chunks, cols, lanes = data_ref.shape
    side = first_ref.shape[0]
    for chunk in range(chunks):
        rim = dot(take_ref[...], data_ref[:, chunk].reshape(sections * cols, lanes)).astype(BF16)
        where = slice(chunk * lanes, (chunk + 1) * lanes)
        first_ref[:, where] = rim[:side]
        last_ref[:, where] = rim[side:]


def shifted_sum(matrix_ref, volume, rows):
    size = volume.shape[1]
    every = dot(matrix_ref[...], volume)
    before, here, after = every[0:rows], every[rows : 2 * rows], every[2 * rows : 3 * rows]
    return pltpu.roll(before, 1, 1) + here + pltpu.roll(after, size - 1, 1)


def inside(keep_ref, which, values):
    keep = jnp.broadcast_to(keep_ref[which : which + 1], values.shape)
    return jnp.where(keep > 0.0, values, 0.0)


def interior_body(keep_ref, first_ref, second_ref, order_ref, data_ref, out_ref, passed_ref, aligned_ref, volume_ref, pass_ref):
    sections, chunks, cols, lanes = data_ref.shape
    main = sections * cols
    length = chunks * lanes
    for chunk in range(chunks):
        block = data_ref[:, chunk].reshape(main, lanes)
        volume_ref[0:main, chunk * lanes : (chunk + 1) * lanes] = block
        volume_ref[main : 2 * main, chunk * lanes : (chunk + 1) * lanes] = block
    volume = volume_ref[...]
    ordered = dot(order_ref[...], volume[0:main])
    rim = aligned_ref.shape[0]
    aligned_ref[...] = ordered[0:rim].astype(BF16)
    rows = first_ref.shape[0] // 3
    passed = jnp.maximum(shifted_sum(first_ref, volume, rows), 0.0)
    passed = inside(keep_ref, 0, passed).astype(BF16)
    passed_ref[...] = passed[0 : passed_ref.shape[0]]
    pass_ref[0:rows] = passed
    pass_ref[rows : 2 * rows] = passed
    total = shifted_sum(second_ref, pass_ref[...], main - rim) + ordered[rim:]
    out_ref[...] = total[:, lanes:].astype(BF16)


def rim_rows(which, keep_ref, first_ref, second_ref, halo_ref, passed_ref, aligned_ref, volume_ref, pass_ref):
    sections = halo_ref.shape[0] // HALO
    side = halo_ref.shape[0]
    own = slice(which * side, (which + 1) * side)
    aligned = aligned_ref[own]
    for start in (0, 2 * side):
        volume_ref[start : start + side] = aligned
        volume_ref[start + side : start + 2 * side] = halo_ref[...]
    rows = first_ref.shape[0] // 3
    passed = jnp.maximum(shifted_sum(first_ref, volume_ref[...], rows), 0.0)
    low = inside(keep_ref, 0 if which else 1, passed[0:sections])
    high = inside(keep_ref, 2 if which else 0, passed[sections:])
    passed = jnp.concatenate([low, high], axis=0).astype(BF16)
    for start in (0, side + rows):
        pass_ref[start : start + side] = passed_ref[own]
        pass_ref[start + side : start + side + rows] = passed
    second = shifted_sum(second_ref, pass_ref[...], side)
    return (second + aligned.astype(F32))[:, LANES:].astype(BF16)


def left_body(keep_ref, first_ref, second_ref, put_ref, halo_ref, passed_ref, aligned_ref, inner_ref, out_ref, volume_ref, pass_ref):
    total = rim_rows(0, keep_ref, first_ref, second_ref, halo_ref, passed_ref, aligned_ref, volume_ref, pass_ref)
    rows_out = jnp.concatenate([total, inner_ref[0 : inner_ref.shape[0] // 2]], axis=0)
    out_ref[...] = dot(put_ref[...], rows_out).astype(BF16).reshape(out_ref.shape)


def right_body(keep_ref, first_ref, second_ref, put_ref, halo_ref, passed_ref, aligned_ref, inner_ref, lower_ref, out_ref, volume_ref, pass_ref, done_ref, sems):
    sections, cols, length = out_ref.shape
    half = cols // 2
    pieces = sems.shape[0] - 1
    copies = [pltpu.make_async_copy(lower_ref, out_ref.at[:, 0:half], sems.at[pieces])]
    copies[0].start()
    total = rim_rows(1, keep_ref, first_ref, second_ref, halo_ref, passed_ref, aligned_ref, volume_ref, pass_ref)
    width = length // pieces
    for piece in range(pieces):
        where = slice(piece * width, (piece + 1) * width)
        rows_out = jnp.concatenate([total[:, where], inner_ref[inner_ref.shape[0] // 2 :, where]], axis=0)
        done_ref[:, :, where] = dot(put_ref[...], rows_out).astype(BF16).reshape(sections, half, width)
        copies.append(
            pltpu.make_async_copy(done_ref.at[:, :, where], out_ref.at[:, half:, where], sems.at[piece])
        )
        copies[-1].start()
    for copy in copies:
        copy.wait()


def one_hot(out_pixels, in_pixels):
    match = [[pixel == other for other in in_pixels] for pixel in out_pixels]
    return jnp.asarray(np.array(match, np.float32), BF16)


def body(source, coarse, fraction, kernel_one, kernel_two):
    _, edge, width = source.shape
    columns = width // edge
    n_xy, n_sec = lax.axis_size("xy"), lax.axis_size("sec")
    cols = width // n_xy
    chunks = edge // LANES

    of_below, of_above = from_behind(coarse, "xy", -1), from_behind(coarse, "xy", 1)
    staged = call(stage_body, shaped(*source.shape), [ANY], "stage", 8, [pltpu.SemaphoreType.DMA])(source)
    of_below, of_above, staged = lax.optimization_barrier((of_below, of_above, staged))
    for_below, for_above = call(
        choose_body, (shaped(1, edge, edge),) * 2, [VMEM] * 3, "choose", 8
    )(of_below, of_above, staged)
    for_below, for_above, fraction, kernel_one, kernel_two = lax.optimization_barrier(
        (for_below, for_above, fraction, kernel_one, kernel_two)
    )
    above, below = from_behind(for_below, "xy", 1), from_behind(for_above, "xy", -1)

    matrix = call(matrices_body, shaped(2, columns, edge, edge), [SMEM], "matrices", 16)(fraction)

    def pixels(*columns_taken):
        return [(section, column) for section in range(n_sec) for column in columns_taken]

    def by_column(*columns_taken):
        return [(section, column) for column in columns_taken for section in range(n_sec)]

    last = cols - 1
    natural = pixels(*range(cols))
    near = pixels(1, 2), pixels(last - 2, last - 1)
    rim = pixels(0, 1), pixels(last - 1, last)
    beyond = pixels(-2, -1), pixels(last + 1, last + 2)
    rim_pass = by_column(-1, 0), by_column(last, last + 1)
    inner_pass = near[0] + near[1] + pixels(*range(3, last - 2))
    inner_out = pixels(*range(HALO, cols // 2)) + pixels(*range(cols // 2, cols - HALO))
    indices = [tap_index(inner_pass, natural), tap_index(inner_out, inner_pass)]
    for which in range(2):
        indices.append(tap_index(rim_pass[which], rim[which] + beyond[which]))
        indices.append(tap_index(rim[which], near[which] + rim_pass[which]))
    stencils = call(
        stencils_body,
        tuple(shaped(3 * index.shape[0], 2 * index.shape[1]) for index in indices),
        [SMEM, SMEM] + [VMEM] * len(indices),
        "stencils",
        8,
    )(kernel_one, kernel_two, *map(jnp.asarray, indices))

    at_xy, at_sec = lax.axis_index("xy"), lax.axis_index("sec")
    per_sec = n_xy * chunks // n_sec
    length = (per_sec + 1) * LANES
    lane = jnp.arange(length, dtype=jnp.int32)
    after, before = lane < LANES // 2, (lane >= LANES // 2) & (lane < LANES)
    real = ~(after & (at_sec == n_sec - 1)) & ~(before & (at_sec == 0))
    keep = jnp.stack([real, real & (at_xy > 0), real & (at_xy < n_xy - 1)]).astype(F32)
    strip_of = shaped(n_xy, chunks, cols, LANES)
    strip = call(warp_body, strip_of, [VMEM] * 3, "warp", 16)(coarse, staged, matrix)
    strip, stencils, keep, above = lax.optimization_barrier((strip, stencils, keep, above))
    for moved, sign, name in ((above, -1, "warp_above"), (below, 1, "warp_below")):
        strip = call(lambda *refs, sign=sign: moved_body(sign, *refs), strip_of, [VMEM] * 4, name, 16)(
            coarse, moved, matrix, strip
        )
    mine = lax.all_to_all(strip, "xy", split_axis=0, concat_axis=0, tiled=True)
    spread = call(spread_body, shaped(n_sec, per_sec + 1, cols, LANES), [VMEM], "spread", 8)(
        mine.reshape(n_xy * chunks, cols, LANES)
    )
    data = lax.all_to_all(spread, "sec", split_axis=0, concat_axis=0, tiled=True)

    out = shaped(n_sec, cols, per_sec * LANES)
    firsts, lasts = call(
        edges_body, (shaped(n_sec * HALO, length),) * 2, [VMEM, VMEM], "edges", 8
    )(data, one_hot(pixels(0, 1) + pixels(last - 1, last), natural))
    left, right = from_behind(lasts, "xy", 1), from_behind(firsts, "xy", -1)
    side = n_sec * HALO
    inner, passed, aligned = call(
        interior_body,
        (shaped(len(inner_out), per_sec * LANES), shaped(2 * side, length), shaped(2 * side, length)),
        [VMEM] * 5,
        "interior",
        32,
        [pltpu.VMEM((2 * len(natural), length), BF16), pltpu.VMEM((2 * len(inner_pass), length), BF16)],
    )(keep, stencils[0], stencils[1], one_hot(rim[0] + rim[1] + inner_out, natural), data)
    scratch = [pltpu.VMEM((4 * side, length), BF16)] * 2
    lower, upper = pixels(*range(cols // 2)), pixels(*range(cols // 2, cols))
    middle = len(inner_out) // 2
    part = shaped(n_sec, cols // 2, per_sec * LANES)
    done = call(left_body, part, [VMEM] * 8, "left", 24, scratch)(
        keep, stencils[2], stencils[3], one_hot(lower, rim[0] + inner_out[:middle]), left, passed, aligned, inner
    )
    scratch = scratch + [pltpu.VMEM(part.shape, BF16), pltpu.SemaphoreType.DMA((5,))]
    return call(right_body, out, [VMEM] * 9, "right", 24, scratch, ANY)(
        keep, stencils[4], stencils[5], one_hot(upper, rim[1] + inner_out[middle:]), right, passed, aligned, inner, done
    )


def solution(mesh):
    placed = (P("sec", "xy", None), P("sec", None, "xy"), P("sec", None, "xy"), P(), P())
    return jax.shard_map(
        body, mesh=mesh, in_specs=placed, out_specs=P(None, "xy", "sec"), check_vma=False
    )
```

```python
import numpy as np
import jax
import jax.numpy as jnp
from jax import lax
from jax.experimental import pallas as pl
from jax.experimental.pallas import tpu as pltpu
from jax.sharding import PartitionSpec as P

LANES = 128
HALO = 2
BF16 = jnp.bfloat16
F32 = jnp.float32
VMEM = pl.BlockSpec(memory_space=pltpu.VMEM)
SMEM = pl.BlockSpec(memory_space=pltpu.SMEM)
ANY = pl.BlockSpec(memory_space=pl.ANY)


def call(body, outs, ins, name, mib, scratch=(), space=VMEM):
    return pl.pallas_call(
        body,
        out_shape=outs,
        in_specs=ins,
        out_specs=jax.tree.map(lambda _: space, outs),
        scratch_shapes=scratch,
        compiler_params=pltpu.CompilerParams(vmem_limit_bytes=mib << 20),
        name=name,
    )


def shaped(*shape):
    return jax.ShapeDtypeStruct(shape, BF16)


def dot(left, right):
    return jnp.dot(left, right, preferred_element_type=F32)


def shift_pairs(count, steps):
    first, last = (max(0, -steps), min(count, count - steps))
    return [(source, source + steps) for source in range(first, last)]


def from_behind(value, axis, steps):
    return lax.ppermute(value, axis, shift_pairs(lax.axis_size(axis), steps))


def interpolation(amount, edge):
    row_index = lax.broadcasted_iota(jnp.int32, (edge, edge), 0)
    col_index = lax.broadcasted_iota(jnp.int32, (edge, edge), 1)
    offset = col_index - row_index
    w_before = ((-0.5 * amount + 1.0) * amount - 0.5) * amount
    w_center = (1.5 * amount - 2.5) * amount * amount + 1.0
    w_after = ((-1.5 * amount + 2.0) * amount + 0.5) * amount
    w_beyond = (0.5 * amount - 0.5) * amount * amount
    matrix = jnp.where(offset == -1, w_before, 0.0)
    matrix = jnp.where(offset == 0, w_center, matrix)
    matrix = jnp.where(offset == 1, w_after, matrix)
    return jnp.where(offset == 2, w_beyond, matrix)


def matrices_body(fraction_ref, out_ref):
    _, kinds, columns = fraction_ref.shape
    edge = out_ref.shape[-1]
    for kind in range(kinds):
        for block in range(columns):
            out_ref[kind, block] = interpolation(fraction_ref[0, kind, block], edge).astype(BF16)


def stage_body(source_ref, out_ref, sem):
    copy = pltpu.make_async_copy(source_ref, out_ref, sem)
    copy.start()
    copy.wait()


def offsets(coarse_ref):
    tile = coarse_ref[0].astype(F32)
    return tile[0:1], tile[1:2] + lax.broadcasted_iota(jnp.int32, (1, tile.shape[1]), 1).astype(F32)


def choose_body(below_ref, above_ref, source_ref, for_below_ref, for_above_ref):
    edge = for_below_ref.shape[-1]
    columns = source_ref.shape[-1] // edge
    for coarse_ref, sign, out_ref in ((below_ref, -1, for_below_ref), (above_ref, 1, for_above_ref)):
        down, anchor = offsets(coarse_ref)
        wanted = jnp.sum(jnp.where(down == sign, anchor, 0.0)).astype(jnp.int32)
        for column in range(columns):

            @pl.when(wanted == column)
            def _():
                out_ref[0] = source_ref[0, :, column * edge : (column + 1) * edge]


def warp_block(matrix_ref, block, picked, out_ref):
    edge = picked.shape[0]
    total, chunks, cols, _ = out_ref.shape
    groups = edge // cols
    rows_warped = dot(matrix_ref[0, block], picked).astype(BF16)
    warped = lax.dot_general(
        matrix_ref[1, block], rows_warped, (((1,), (1,)), ((), ())), preferred_element_type=F32
    ).astype(BF16)
    warped = warped.reshape(groups, cols, edge)
    for chunk in range(chunks):
        out_ref[block * groups : (block + 1) * groups, chunk] = warped[:, :, chunk * LANES : (chunk + 1) * LANES]


def block_offsets(coarse_ref, columns):
    downs, anchors = offsets(coarse_ref)
    lane = lax.broadcasted_iota(jnp.int32, downs.shape, 1)

    def at(values, block):
        return jnp.sum(jnp.where(lane == block, values, 0.0)).astype(jnp.int32)

    return [(at(downs, block), at(anchors, block)) for block in range(columns)]


def warp_body(coarse_ref, source_ref, matrix_ref, out_ref):
    _, edge, width = source_ref.shape
    columns = width // edge
    for block, (_, anchor) in enumerate(block_offsets(coarse_ref, columns)):
        picked = source_ref[0, :, 0:edge]
        for column in range(1, columns):
            picked = jnp.where(anchor == column, source_ref[0, :, column * edge : (column + 1) * edge], picked)
        warp_block(matrix_ref, block, picked, out_ref)


def moved_body(sign, coarse_ref, moved_ref, matrix_ref, strip_ref, out_ref):
    out_ref[...] = strip_ref[...]
    for block, (down, _) in enumerate(block_offsets(coarse_ref, matrix_ref.shape[1])):

        @pl.when(down == sign)
        def _():
            warp_block(matrix_ref, block, moved_ref[0], out_ref)


def tap_index(out_pixels, in_pixels):
    out_sec, out_col = np.array(out_pixels).T[:, :, None]
    in_sec, in_col = np.array(in_pixels).T[:, None, :]
    tap_z, tap_x = in_sec - out_sec + 1, in_col - out_col + 1
    linked = (tap_z >= 0) & (tap_z < 3) & (tap_x >= 0) & (tap_x < 3)
    return np.where(linked, tap_z * 3 + tap_x, -1).astype(np.int32)


def stencil_matrix(index, kernel_ref, out_ref):
    rows, width = index.shape
    for tap_y in range(3):
        value = jnp.zeros((rows, width), F32)
        for tap in range(9):
            value = jnp.where(index == tap, kernel_ref[tap // 3, tap % 3, tap_y], value)
        high = value.astype(BF16)
        low = (value - high.astype(F32)).astype(BF16)
        out_ref[tap_y * rows : (tap_y + 1) * rows, :] = jnp.concatenate([high, low], axis=1)


def stencils_body(one_ref, two_ref, *refs):
    half = len(refs) // 2
    indices, outs = refs[:half], refs[half:]
    for place, (index_ref, out_ref) in enumerate(zip(indices, outs)):
        stencil_matrix(index_ref[...], one_ref if place % 2 == 0 else two_ref, out_ref)


def spread_body(data_ref, out_ref):
    parts, chunks, cols, lanes = out_ref.shape
    count = chunks - 1
    low = lax.broadcasted_iota(jnp.int32, (cols, lanes), 1) < lanes // 2
    nothing = jnp.zeros((cols, lanes), F32)
    for part in range(parts):
        first, end = part * count, (part + 1) * count
        before = data_ref[first - 1].astype(F32) if part > 0 else nothing
        after = data_ref[end].astype(F32) if part < parts - 1 else nothing
        out_ref[part, 0] = jnp.where(low, after, before).astype(BF16)
        out_ref[part, 1:chunks] = data_ref[first:end]


def edges_body(data_ref, take_ref, first_ref, last_ref):
    sections, chunks, cols, lanes = data_ref.shape
    side = first_ref.shape[0]
    for chunk in range(chunks):
        rim = dot(take_ref[...], data_ref[:, chunk].reshape(sections * cols, lanes)).astype(BF16)
        where = slice(chunk * lanes, (chunk + 1) * lanes)
        first_ref[:, where] = rim[:side]
        last_ref[:, where] = rim[side:]


def shifted_sum(matrix_ref, volume, rows):
    size = volume.shape[1]
    every = dot(matrix_ref[...], volume)
    before, here, after = every[0:rows], every[rows : 2 * rows], every[2 * rows : 3 * rows]
    return pltpu.roll(before, 1, 1) + here + pltpu.roll(after, size - 1, 1)


def inside(keep_ref, which, values):
    keep = jnp.broadcast_to(keep_ref[which : which + 1], values.shape)
    return jnp.where(keep > 0.0, values, 0.0)


def interior_body(keep_ref, first_ref, second_ref, order_ref, data_ref, out_ref, passed_ref, aligned_ref, volume_ref, pass_ref):
    sections, chunks, cols, lanes = data_ref.shape
    main = sections * cols
    length = chunks * lanes
    for chunk in range(chunks):
        block = data_ref[:, chunk].reshape(main, lanes)
        volume_ref[0:main, chunk * lanes : (chunk + 1) * lanes] = block
        volume_ref[main : 2 * main, chunk * lanes : (chunk + 1) * lanes] = block
    volume = volume_ref[...]
    ordered = dot(order_ref[...], volume[0:main])
    rim = aligned_ref.shape[0]
    aligned_ref[...] = ordered[0:rim].astype(BF16)
    rows = first_ref.shape[0] // 3
    passed = jnp.maximum(shifted_sum(first_ref, volume, rows), 0.0)
    passed = inside(keep_ref, 0, passed).astype(BF16)
    passed_ref[...] = passed[0 : passed_ref.shape[0]]
    pass_ref[0:rows] = passed
    pass_ref[rows : 2 * rows] = passed
    total = shifted_sum(second_ref, pass_ref[...], main - rim) + ordered[rim:]
    out_ref[...] = total[:, lanes:].astype(BF16)


def rim_rows(which, keep_ref, first_ref, second_ref, halo_ref, passed_ref, aligned_ref, volume_ref, pass_ref):
    sections = halo_ref.shape[0] // HALO
    side = halo_ref.shape[0]
    own = slice(which * side, (which + 1) * side)
    aligned = aligned_ref[own]
    for start in (0, 2 * side):
        volume_ref[start : start + side] = aligned
        volume_ref[start + side : start + 2 * side] = halo_ref[...]
    rows = first_ref.shape[0] // 3
    passed = jnp.maximum(shifted_sum(first_ref, volume_ref[...], rows), 0.0)
    low = inside(keep_ref, 0 if which else 1, passed[0:sections])
    high = inside(keep_ref, 2 if which else 0, passed[sections:])
    passed = jnp.concatenate([low, high], axis=0).astype(BF16)
    for start in (0, side + rows):
        pass_ref[start : start + side] = passed_ref[own]
        pass_ref[start + side : start + side + rows] = passed
    second = shifted_sum(second_ref, pass_ref[...], side)
    return (second + aligned.astype(F32))[:, LANES:].astype(BF16)


def left_body(keep_ref, first_ref, second_ref, put_ref, halo_ref, passed_ref, aligned_ref, inner_ref, out_ref, volume_ref, pass_ref):
    total = rim_rows(0, keep_ref, first_ref, second_ref, halo_ref, passed_ref, aligned_ref, volume_ref, pass_ref)
    rows_out = jnp.concatenate([total, inner_ref[0 : inner_ref.shape[0] // 2]], axis=0)
    out_ref[...] = dot(put_ref[...], rows_out).astype(BF16).reshape(out_ref.shape)


def right_body(keep_ref, first_ref, second_ref, put_ref, halo_ref, passed_ref, aligned_ref, inner_ref, lower_ref, out_ref, volume_ref, pass_ref, done_ref, sems):
    sections, cols, length = out_ref.shape
    half = cols // 2
    pieces = sems.shape[0] - 1
    copies = [pltpu.make_async_copy(lower_ref, out_ref.at[:, 0:half], sems.at[pieces])]
    copies[0].start()
    total = rim_rows(1, keep_ref, first_ref, second_ref, halo_ref, passed_ref, aligned_ref, volume_ref, pass_ref)
    width = length // pieces
    for piece in range(pieces):
        where = slice(piece * width, (piece + 1) * width)
        rows_out = jnp.concatenate([total[:, where], inner_ref[inner_ref.shape[0] // 2 :, where]], axis=0)
        done_ref[:, :, where] = dot(put_ref[...], rows_out).astype(BF16).reshape(sections, half, width)
        copies.append(
            pltpu.make_async_copy(done_ref.at[:, :, where], out_ref.at[:, half:, where], sems.at[piece])
        )
        copies[-1].start()
    for copy in copies:
        copy.wait()


def one_hot(out_pixels, in_pixels):
    match = [[pixel == other for other in in_pixels] for pixel in out_pixels]
    return jnp.asarray(np.array(match, np.float32), BF16)


def body(source, coarse, fraction, kernel_one, kernel_two):
    _, edge, width = source.shape
    columns = width // edge
    n_xy, n_sec = lax.axis_size("xy"), lax.axis_size("sec")
    cols = width // n_xy
    chunks = edge // LANES

    of_below, of_above = from_behind(coarse, "xy", -1), from_behind(coarse, "xy", 1)
    staged = call(stage_body, shaped(*source.shape), [ANY], "stage", 8, [pltpu.SemaphoreType.DMA])(source)
    of_below, of_above, staged = lax.optimization_barrier((of_below, of_above, staged))
    for_below, for_above = call(
        choose_body, (shaped(1, edge, edge),) * 2, [VMEM] * 3, "choose", 8
    )(of_below, of_above, staged)
    for_below, for_above, fraction, kernel_one, kernel_two = lax.optimization_barrier(
        (for_below, for_above, fraction, kernel_one, kernel_two)
    )
    above, below = from_behind(for_below, "xy", 1), from_behind(for_above, "xy", -1)

    matrix = call(matrices_body, shaped(2, columns, edge, edge), [SMEM], "matrices", 16)(fraction)

    def pixels(*columns_taken):
        return [(section, column) for section in range(n_sec) for column in columns_taken]

    def by_column(*columns_taken):
        return [(section, column) for column in columns_taken for section in range(n_sec)]

    last = cols - 1
    natural = pixels(*range(cols))
    near = pixels(1, 2), pixels(last - 2, last - 1)
    rim = pixels(0, 1), pixels(last - 1, last)
    beyond = pixels(-2, -1), pixels(last + 1, last + 2)
    rim_pass = by_column(-1, 0), by_column(last, last + 1)
    inner_pass = near[0] + near[1] + pixels(*range(3, last - 2))
    inner_out = pixels(*range(HALO, cols // 2)) + pixels(*range(cols // 2, cols - HALO))
    indices = [tap_index(inner_pass, natural), tap_index(inner_out, inner_pass)]
    for which in range(2):
        indices.append(tap_index(rim_pass[which], rim[which] + beyond[which]))
        indices.append(tap_index(rim[which], near[which] + rim_pass[which]))
    stencils = call(
        stencils_body,
        tuple(shaped(3 * index.shape[0], 2 * index.shape[1]) for index in indices),
        [SMEM, SMEM] + [VMEM] * len(indices),
        "stencils",
        8,
    )(kernel_one, kernel_two, *map(jnp.asarray, indices))

    at_xy, at_sec = lax.axis_index("xy"), lax.axis_index("sec")
    per_sec = n_xy * chunks // n_sec
    length = (per_sec + 1) * LANES
    lane = jnp.arange(length, dtype=jnp.int32)
    after, before = lane < LANES // 2, (lane >= LANES // 2) & (lane < LANES)
    real = ~(after & (at_sec == n_sec - 1)) & ~(before & (at_sec == 0))
    keep = jnp.stack([real, real & (at_xy > 0), real & (at_xy < n_xy - 1)]).astype(F32)
    strip_of = shaped(n_xy, chunks, cols, LANES)
    strip = call(warp_body, strip_of, [VMEM] * 3, "warp", 16)(coarse, staged, matrix)
    strip, stencils, keep, above = lax.optimization_barrier((strip, stencils, keep, above))
    for moved, sign, name in ((above, -1, "warp_above"), (below, 1, "warp_below")):
        strip = call(lambda *refs, sign=sign: moved_body(sign, *refs), strip_of, [VMEM] * 4, name, 16)(
            coarse, moved, matrix, strip
        )
    mine = lax.all_to_all(strip, "xy", split_axis=0, concat_axis=0, tiled=True)
    spread = call(spread_body, shaped(n_sec, per_sec + 1, cols, LANES), [VMEM], "spread", 8)(
        mine.reshape(n_xy * chunks, cols, LANES)
    )
    data = lax.all_to_all(spread, "sec", split_axis=0, concat_axis=0, tiled=True)

    out = shaped(n_sec, cols, per_sec * LANES)
    firsts, lasts = call(
        edges_body, (shaped(n_sec * HALO, length),) * 2, [VMEM, VMEM], "edges", 8
    )(data, one_hot(pixels(0, 1) + pixels(last - 1, last), natural))
    left = from_behind(lasts, "xy", 1)
    side = n_sec * HALO
    inner, passed, aligned = call(
        interior_body,
        (shaped(len(inner_out), per_sec * LANES), shaped(2 * side, length), shaped(2 * side, length)),
        [VMEM] * 5,
        "interior",
        32,
        [pltpu.VMEM((2 * len(natural), length), BF16), pltpu.VMEM((2 * len(inner_pass), length), BF16)],
    )(keep, stencils[0], stencils[1], one_hot(rim[0] + rim[1] + inner_out, natural), data)
    firsts, inner = lax.optimization_barrier((firsts, inner))
    right = from_behind(firsts, "xy", -1)
    scratch = [pltpu.VMEM((4 * side, length), BF16)] * 2
    lower, upper = pixels(*range(cols // 2)), pixels(*range(cols // 2, cols))
    middle = len(inner_out) // 2
    part = shaped(n_sec, cols // 2, per_sec * LANES)
    done = call(left_body, part, [VMEM] * 8, "left", 24, scratch)(
        keep, stencils[2], stencils[3], one_hot(lower, rim[0] + inner_out[:middle]), left, passed, aligned, inner
    )
    scratch = scratch + [pltpu.VMEM(part.shape, BF16), pltpu.SemaphoreType.DMA((5,))]
    return call(right_body, out, [VMEM] * 9, "right", 24, scratch, ANY)(
        keep, stencils[4], stencils[5], one_hot(upper, rim[1] + inner_out[middle:]), right, passed, aligned, inner, done
    )


def solution(mesh):
    placed = (P("sec", "xy", None), P("sec", None, "xy"), P("sec", None, "xy"), P(), P())
    return jax.shard_map(
        body, mesh=mesh, in_specs=placed, out_specs=P(None, "xy", "sec"), check_vma=False
    )
```

```python
import numpy as np
import jax
import jax.numpy as jnp
from jax import lax
from jax.experimental import pallas as pl
from jax.experimental.pallas import tpu as pltpu
from jax.sharding import PartitionSpec as P

LANES = 128
HALO = 2
BF16 = jnp.bfloat16
F32 = jnp.float32
VMEM = pl.BlockSpec(memory_space=pltpu.VMEM)
SMEM = pl.BlockSpec(memory_space=pltpu.SMEM)
ANY = pl.BlockSpec(memory_space=pl.ANY)


def call(body, outs, ins, name, mib, scratch=(), space=VMEM):
    return pl.pallas_call(
        body,
        out_shape=outs,
        in_specs=ins,
        out_specs=jax.tree.map(lambda _: space, outs),
        scratch_shapes=scratch,
        compiler_params=pltpu.CompilerParams(vmem_limit_bytes=mib << 20),
        name=name,
    )


def shaped(*shape):
    return jax.ShapeDtypeStruct(shape, BF16)


def dot(left, right):
    return jnp.dot(left, right, preferred_element_type=F32)


def shift_pairs(count, steps):
    first, last = (max(0, -steps), min(count, count - steps))
    return [(source, source + steps) for source in range(first, last)]


def from_behind(value, axis, steps):
    return lax.ppermute(value, axis, shift_pairs(lax.axis_size(axis), steps))


def interpolation(amount, edge):
    row_index = lax.broadcasted_iota(jnp.int32, (edge, edge), 0)
    col_index = lax.broadcasted_iota(jnp.int32, (edge, edge), 1)
    offset = col_index - row_index
    w_before = ((-0.5 * amount + 1.0) * amount - 0.5) * amount
    w_center = (1.5 * amount - 2.5) * amount * amount + 1.0
    w_after = ((-1.5 * amount + 2.0) * amount + 0.5) * amount
    w_beyond = (0.5 * amount - 0.5) * amount * amount
    matrix = jnp.where(offset == -1, w_before, 0.0)
    matrix = jnp.where(offset == 0, w_center, matrix)
    matrix = jnp.where(offset == 1, w_after, matrix)
    return jnp.where(offset == 2, w_beyond, matrix)


def matrices_body(fraction_ref, out_ref):
    _, kinds, columns = fraction_ref.shape
    edge = out_ref.shape[-1]
    for kind in range(kinds):
        for block in range(columns):
            out_ref[kind, block] = interpolation(fraction_ref[0, kind, block], edge).astype(BF16)


def stage_body(source_ref, out_ref, sem):
    copy = pltpu.make_async_copy(source_ref, out_ref, sem)
    copy.start()
    copy.wait()


def offsets(coarse_ref):
    tile = coarse_ref[0].astype(F32)
    return tile[0:1], tile[1:2] + lax.broadcasted_iota(jnp.int32, (1, tile.shape[1]), 1).astype(F32)


def choose_body(below_ref, above_ref, source_ref, for_below_ref, for_above_ref):
    edge = for_below_ref.shape[-1]
    columns = source_ref.shape[-1] // edge
    for coarse_ref, sign, out_ref in ((below_ref, -1, for_below_ref), (above_ref, 1, for_above_ref)):
        down, anchor = offsets(coarse_ref)
        wanted = jnp.sum(jnp.where(down == sign, anchor, 0.0)).astype(jnp.int32)
        for column in range(columns):

            @pl.when(wanted == column)
            def _():
                out_ref[0] = source_ref[0, :, column * edge : (column + 1) * edge]


def warp_block(matrix_ref, block, picked, out_ref):
    edge = picked.shape[0]
    total, chunks, cols, _ = out_ref.shape
    groups = edge // cols
    rows_warped = dot(matrix_ref[0, block], picked).astype(BF16)
    warped = lax.dot_general(
        matrix_ref[1, block], rows_warped, (((1,), (1,)), ((), ())), preferred_element_type=F32
    ).astype(BF16)
    warped = warped.reshape(groups, cols, edge)
    for chunk in range(chunks):
        out_ref[block * groups : (block + 1) * groups, chunk] = warped[:, :, chunk * LANES : (chunk + 1) * LANES]


def block_offsets(coarse_ref, columns):
    downs, anchors = offsets(coarse_ref)
    lane = lax.broadcasted_iota(jnp.int32, downs.shape, 1)

    def at(values, block):
        return jnp.sum(jnp.where(lane == block, values, 0.0)).astype(jnp.int32)

    return [(at(downs, block), at(anchors, block)) for block in range(columns)]


def warp_body(coarse_ref, source_ref, matrix_ref, out_ref):
    _, edge, width = source_ref.shape
    columns = width // edge
    for block, (_, anchor) in enumerate(block_offsets(coarse_ref, columns)):
        picked = source_ref[0, :, 0:edge]
        for column in range(1, columns):
            picked = jnp.where(anchor == column, source_ref[0, :, column * edge : (column + 1) * edge], picked)
        warp_block(matrix_ref, block, picked, out_ref)


def moved_body(sign, coarse_ref, moved_ref, matrix_ref, strip_ref, out_ref):
    out_ref[...] = strip_ref[...]
    for block, (down, _) in enumerate(block_offsets(coarse_ref, matrix_ref.shape[1])):

        @pl.when(down == sign)
        def _():
            warp_block(matrix_ref, block, moved_ref[0], out_ref)


def tap_index(out_pixels, in_pixels):
    out_sec, out_col = np.array(out_pixels).T[:, :, None]
    in_sec, in_col = np.array(in_pixels).T[:, None, :]
    tap_z, tap_x = in_sec - out_sec + 1, in_col - out_col + 1
    linked = (tap_z >= 0) & (tap_z < 3) & (tap_x >= 0) & (tap_x < 3)
    return np.where(linked, tap_z * 3 + tap_x, -1).astype(np.int32)


def stencil_matrix(index, kernel_ref, out_ref):
    rows, width = index.shape
    for tap_y in range(3):
        value = jnp.zeros((rows, width), F32)
        for tap in range(9):
            value = jnp.where(index == tap, kernel_ref[tap // 3, tap % 3, tap_y], value)
        high = value.astype(BF16)
        low = (value - high.astype(F32)).astype(BF16)
        out_ref[tap_y * rows : (tap_y + 1) * rows, :] = jnp.concatenate([high, low], axis=1)


def stencils_body(one_ref, two_ref, *refs):
    half = len(refs) // 2
    indices, outs = refs[:half], refs[half:]
    for place, (index_ref, out_ref) in enumerate(zip(indices, outs)):
        stencil_matrix(index_ref[...], one_ref if place % 2 == 0 else two_ref, out_ref)


def spread_body(data_ref, out_ref):
    parts, chunks, cols, lanes = out_ref.shape
    count = chunks - 1
    low = lax.broadcasted_iota(jnp.int32, (cols, lanes), 1) < lanes // 2
    nothing = jnp.zeros((cols, lanes), F32)
    for part in range(parts):
        first, end = part * count, (part + 1) * count
        before = data_ref[first - 1].astype(F32) if part > 0 else nothing
        after = data_ref[end].astype(F32) if part < parts - 1 else nothing
        out_ref[part, 0] = jnp.where(low, after, before).astype(BF16)
        out_ref[part, 1:chunks] = data_ref[first:end]


def edges_body(data_ref, take_ref, first_ref, last_ref):
    sections, chunks, cols, lanes = data_ref.shape
    side = first_ref.shape[0]
    for start in range(0, chunks, 2):
        taken = range(start, min(start + 2, chunks))
        blocks = [data_ref[:, chunk].reshape(sections * cols, lanes) for chunk in taken]
        rim = dot(take_ref[...], jnp.concatenate(blocks, axis=1)).astype(BF16)
        where = slice(start * lanes, (start + len(blocks)) * lanes)
        first_ref[:, where] = rim[:side]
        last_ref[:, where] = rim[side:]


def shifted_sum(matrix_ref, volume, rows):
    size = volume.shape[1]
    every = dot(matrix_ref[...], volume)
    before, here, after = every[0:rows], every[rows : 2 * rows], every[2 * rows : 3 * rows]
    return pltpu.roll(before, 1, 1) + here + pltpu.roll(after, size - 1, 1)


def inside(keep_ref, which, values):
    keep = jnp.broadcast_to(keep_ref[which : which + 1], values.shape)
    return jnp.where(keep > 0.0, values, 0.0)


def interior_body(keep_ref, first_ref, second_ref, order_ref, data_ref, out_ref, passed_ref, aligned_ref, volume_ref, pass_ref):
    sections, chunks, cols, lanes = data_ref.shape
    main = sections * cols
    length = chunks * lanes
    for chunk in range(chunks):
        block = data_ref[:, chunk].reshape(main, lanes)
        volume_ref[0:main, chunk * lanes : (chunk + 1) * lanes] = block
        volume_ref[main : 2 * main, chunk * lanes : (chunk + 1) * lanes] = block
    volume = volume_ref[...]
    ordered = dot(order_ref[...], volume[0:main])
    rim = aligned_ref.shape[0]
    aligned_ref[...] = ordered[0:rim].astype(BF16)
    rows = first_ref.shape[0] // 3
    passed = jnp.maximum(shifted_sum(first_ref, volume, rows), 0.0)
    passed = inside(keep_ref, 0, passed).astype(BF16)
    passed_ref[...] = passed[0 : passed_ref.shape[0]]
    pass_ref[0:rows] = passed
    pass_ref[rows : 2 * rows] = passed
    total = shifted_sum(second_ref, pass_ref[...], main - rim) + ordered[rim:]
    out_ref[...] = total[:, lanes:].astype(BF16)


def rim_rows(which, keep_ref, first_ref, second_ref, halo_ref, passed_ref, aligned_ref, volume_ref, pass_ref):
    sections = halo_ref.shape[0] // HALO
    side = halo_ref.shape[0]
    own = slice(which * side, (which + 1) * side)
    aligned = aligned_ref[own]
    for start in (0, 2 * side):
        volume_ref[start : start + side] = aligned
        volume_ref[start + side : start + 2 * side] = halo_ref[...]
    rows = first_ref.shape[0] // 3
    passed = jnp.maximum(shifted_sum(first_ref, volume_ref[...], rows), 0.0)
    low = inside(keep_ref, 0 if which else 1, passed[0:sections])
    high = inside(keep_ref, 2 if which else 0, passed[sections:])
    passed = jnp.concatenate([low, high], axis=0).astype(BF16)
    for start in (0, side + rows):
        pass_ref[start : start + side] = passed_ref[own]
        pass_ref[start + side : start + side + rows] = passed
    second = shifted_sum(second_ref, pass_ref[...], side)
    return (second + aligned.astype(F32))[:, LANES:].astype(BF16)


def left_body(keep_ref, first_ref, second_ref, put_ref, halo_ref, passed_ref, aligned_ref, inner_ref, out_ref, volume_ref, pass_ref):
    total = rim_rows(0, keep_ref, first_ref, second_ref, halo_ref, passed_ref, aligned_ref, volume_ref, pass_ref)
    rows_out = jnp.concatenate([total, inner_ref[0 : inner_ref.shape[0] // 2]], axis=0)
    out_ref[...] = dot(put_ref[...], rows_out).astype(BF16).reshape(out_ref.shape)


def right_body(keep_ref, first_ref, second_ref, put_ref, halo_ref, passed_ref, aligned_ref, inner_ref, lower_ref, out_ref, volume_ref, pass_ref, done_ref, sems):
    sections, cols, length = out_ref.shape
    half = cols // 2
    pieces = sems.shape[0] - 1
    copies = [pltpu.make_async_copy(lower_ref, out_ref.at[:, 0:half], sems.at[pieces])]
    copies[0].start()
    total = rim_rows(1, keep_ref, first_ref, second_ref, halo_ref, passed_ref, aligned_ref, volume_ref, pass_ref)
    width = length // pieces
    for piece in range(pieces):
        where = slice(piece * width, (piece + 1) * width)
        rows_out = jnp.concatenate([total[:, where], inner_ref[inner_ref.shape[0] // 2 :, where]], axis=0)
        done_ref[:, :, where] = dot(put_ref[...], rows_out).astype(BF16).reshape(sections, half, width)
        copies.append(
            pltpu.make_async_copy(done_ref.at[:, :, where], out_ref.at[:, half:, where], sems.at[piece])
        )
        copies[-1].start()
    for copy in copies:
        copy.wait()


def one_hot(out_pixels, in_pixels):
    match = [[pixel == other for other in in_pixels] for pixel in out_pixels]
    return jnp.asarray(np.array(match, np.float32), BF16)


def body(source, coarse, fraction, kernel_one, kernel_two):
    _, edge, width = source.shape
    columns = width // edge
    n_xy, n_sec = lax.axis_size("xy"), lax.axis_size("sec")
    cols = width // n_xy
    chunks = edge // LANES

    of_below, of_above = from_behind(coarse, "xy", -1), from_behind(coarse, "xy", 1)
    staged = call(stage_body, shaped(*source.shape), [ANY], "stage", 8, [pltpu.SemaphoreType.DMA])(source)
    of_below, of_above, staged = lax.optimization_barrier((of_below, of_above, staged))
    for_below, for_above = call(
        choose_body, (shaped(1, edge, edge),) * 2, [VMEM] * 3, "choose", 8
    )(of_below, of_above, staged)
    for_below, for_above, fraction, kernel_one, kernel_two = lax.optimization_barrier(
        (for_below, for_above, fraction, kernel_one, kernel_two)
    )
    above, below = from_behind(for_below, "xy", 1), from_behind(for_above, "xy", -1)

    matrix = call(matrices_body, shaped(2, columns, edge, edge), [SMEM], "matrices", 16)(fraction)

    def pixels(*columns_taken):
        return [(section, column) for section in range(n_sec) for column in columns_taken]

    def by_column(*columns_taken):
        return [(section, column) for column in columns_taken for section in range(n_sec)]

    last = cols - 1
    natural = pixels(*range(cols))
    near = pixels(1, 2), pixels(last - 2, last - 1)
    rim = pixels(0, 1), pixels(last - 1, last)
    beyond = pixels(-2, -1), pixels(last + 1, last + 2)
    rim_pass = by_column(-1, 0), by_column(last, last + 1)
    inner_pass = near[0] + near[1] + pixels(*range(3, last - 2))
    inner_out = pixels(*range(HALO, cols // 2)) + pixels(*range(cols // 2, cols - HALO))
    indices = [tap_index(inner_pass, natural), tap_index(inner_out, inner_pass)]
    for which in range(2):
        indices.append(tap_index(rim_pass[which], rim[which] + beyond[which]))
        indices.append(tap_index(rim[which], near[which] + rim_pass[which]))
    stencils = call(
        stencils_body,
        tuple(shaped(3 * index.shape[0], 2 * index.shape[1]) for index in indices),
        [SMEM, SMEM] + [VMEM] * len(indices),
        "stencils",
        8,
    )(kernel_one, kernel_two, *map(jnp.asarray, indices))

    at_xy, at_sec = lax.axis_index("xy"), lax.axis_index("sec")
    per_sec = n_xy * chunks // n_sec
    length = (per_sec + 1) * LANES
    lane = jnp.arange(length, dtype=jnp.int32)
    after, before = lane < LANES // 2, (lane >= LANES // 2) & (lane < LANES)
    real = ~(after & (at_sec == n_sec - 1)) & ~(before & (at_sec == 0))
    keep = jnp.stack([real, real & (at_xy > 0), real & (at_xy < n_xy - 1)]).astype(F32)
    strip_of = shaped(n_xy, chunks, cols, LANES)
    strip = call(warp_body, strip_of, [VMEM] * 3, "warp", 16)(coarse, staged, matrix)
    strip, stencils, keep, above = lax.optimization_barrier((strip, stencils, keep, above))
    for moved, sign, name in ((above, -1, "warp_above"), (below, 1, "warp_below")):
        strip = call(lambda *refs, sign=sign: moved_body(sign, *refs), strip_of, [VMEM] * 4, name, 16)(
            coarse, moved, matrix, strip
        )
    mine = lax.all_to_all(strip, "xy", split_axis=0, concat_axis=0, tiled=True)
    spread = call(spread_body, shaped(n_sec, per_sec + 1, cols, LANES), [VMEM], "spread", 8)(
        mine.reshape(n_xy * chunks, cols, LANES)
    )
    data = lax.all_to_all(spread, "sec", split_axis=0, concat_axis=0, tiled=True)

    out = shaped(n_sec, cols, per_sec * LANES)
    firsts, lasts = call(
        edges_body, (shaped(n_sec * HALO, length),) * 2, [VMEM, VMEM], "edges", 8
    )(data, one_hot(pixels(0, 1) + pixels(last - 1, last), natural))
    left, right = from_behind(lasts, "xy", 1), from_behind(firsts, "xy", -1)
    side = n_sec * HALO
    inner, passed, aligned = call(
        interior_body,
        (shaped(len(inner_out), per_sec * LANES), shaped(2 * side, length), shaped(2 * side, length)),
        [VMEM] * 5,
        "interior",
        32,
        [pltpu.VMEM((2 * len(natural), length), BF16), pltpu.VMEM((2 * len(inner_pass), length), BF16)],
    )(keep, stencils[0], stencils[1], one_hot(rim[0] + rim[1] + inner_out, natural), data)
    scratch = [pltpu.VMEM((4 * side, length), BF16)] * 2
    lower, upper = pixels(*range(cols // 2)), pixels(*range(cols // 2, cols))
    middle = len(inner_out) // 2
    part = shaped(n_sec, cols // 2, per_sec * LANES)
    done = call(left_body, part, [VMEM] * 8, "left", 24, scratch)(
        keep, stencils[2], stencils[3], one_hot(lower, rim[0] + inner_out[:middle]), left, passed, aligned, inner
    )
    scratch = scratch + [pltpu.VMEM(part.shape, BF16), pltpu.SemaphoreType.DMA((5,))]
    return call(right_body, out, [VMEM] * 9, "right", 24, scratch, ANY)(
        keep, stencils[4], stencils[5], one_hot(upper, rim[1] + inner_out[middle:]), right, passed, aligned, inner, done
    )


def solution(mesh):
    placed = (P("sec", "xy", None), P("sec", None, "xy"), P("sec", None, "xy"), P(), P())
    return jax.shard_map(
        body, mesh=mesh, in_specs=placed, out_specs=P(None, "xy", "sec"), check_vma=False
    )
```
